256 devices in a mesh: grp: 4 (over x), pen: 64 (over y, z, core).
Axes of the slice: x: 4, y: 4, z: 8, core: 2. Of those that a mesh axis runs over, the one named last changes fastest.
Arguments:
- occupancy: int32 [256, 512, 256], P('grp', 'pen'), may hold values from 0 to 11, as said below
- embedding: float32 [12, 16], replicated, may hold values from -6 to 6
- spectral_weight: float32 [256, 16, 2, 16, 16], P(('grp', 'pen')), may hold values from -1.5 to 1.5
- point_weight: float32 [16, 16], replicated, may hold values from -1.5 to 1.5
- point_bias: float32 [16], replicated, may hold values from -3 to 3
- expand_weight: bfloat16 [16, 64], replicated, may hold values from -1.5 to 1.5
- expand_bias: float32 [64], replicated, may hold values from -3 to 3
- reduce_weight: bfloat16 [64, 16], replicated, may hold values from -0.75 to 0.75
- reduce_bias: float32 [16], replicated, may hold values from -3 to 3
Outputs:
- encoded: bfloat16 [16, 256, 512, 256], P(None, 'grp', 'pen')
The draws below stay inside these ranges and needn't reach their ends.
Inputs may be any that keep to these rules, and one draw needn't show every extreme that they name: `occupancy`: each cell holds one of 12 class labels.
All inputs are finite; a program needn't handle non-finite values.
Results may differ from the reference program's by a relative error of at most 0.001.
The reference program's roundings to bfloat16 on the way count: a program that leaves them out, or rounds other values in their place, can miss the bound.
Values may be sent and summed in bfloat16 or wider, within the bound.
No kernel may reach another device: no remote copies, remote signals or barrier semaphores. Data moves between devices by JAX's collectives and lax.ppermute only.
A program may use at most 128 MiB of HBM per device.

```python
import math
import jax
import jax.numpy as jnp
from jax import lax

NZ = 256
NX = 512
NY = 256
CH = 16
MODES = 16
NCLASS = 12
HIDDEN_SIZE = 64
PAIRS = 256


def draw_occupancy(key, part):
    room_key = jax.random.fold_in(key, 11)
    noise_key = jax.random.fold_in(key, 12)
    pick_key = jax.random.fold_in(key, 13)
    room_labels = jax.random.randint(room_key, (8, 8, 8), 0, NCLASS)
    z_room = jnp.arange(NZ, dtype=jnp.int32) * 8 // NZ
    x_room = jnp.arange(NX, dtype=jnp.int32) * 8 // NX
    y_room = jnp.arange(NY, dtype=jnp.int32) * 8 // NY
    coarse = room_labels[z_room[:, None, None], x_room[None, :, None], y_room[None, None, :]]
    noise_labels = jax.random.randint(noise_key, (NZ, NX, NY), 0, NCLASS)
    pick_value = jax.random.randint(pick_key, (NZ, NX, NY), 0, 4)
    return jnp.where(pick_value == 0, noise_labels, coarse).astype(jnp.int32)


def block_levels(stream_key, extent, split, least, top_value):
    def one(axis_at, blocks):
        heights = jax.random.uniform(jax.random.fold_in(jax.random.fold_in(stream_key, 6), axis_at), (blocks,), jnp.float32, least / len(split), top_value / len(split))
        return jnp.repeat(jnp.exp(heights), extent[axis_at] // blocks).reshape((-1,) + (1,) * (len(extent) - axis_at - 1))

    loudness = one(*split[0])
    for cut in split[1:]:
        loudness = loudness * one(*cut)
    return loudness


def bell_draw(rng, dims, spread, most, split=(), kind=jnp.bfloat16):
    array = jax.random.normal(rng, dims, jnp.float32) * spread
    if len(split) > 0:
        array = block_levels(rng, dims, split, -0.22, 0.18) * array
    return jnp.clip(array, min=-most, max=most).astype(kind)


def setup_inputs(seed: int = 0) -> dict:
    streams_of = jax.random.split(jax.random.key(seed), 10)
    return {
        "occupancy": draw_occupancy(jax.random.fold_in(streams_of[9], 71), 0),
        "embedding": bell_draw(streams_of[1], (NCLASS, CH), 1.0, 6.0, (), jnp.float32),
        "spectral_weight": bell_draw(streams_of[2], (PAIRS, MODES, 2, CH, CH), CH ** -0.5, 1.5, ((0, 256),), jnp.float32),
        "point_weight": bell_draw(streams_of[3], (CH, CH), CH ** -0.5, 1.5, (), jnp.float32),
        "point_bias": bell_draw(streams_of[4], (CH,), 0.5, 3.0, (), jnp.float32),
        "expand_weight": bell_draw(streams_of[5], (CH, HIDDEN_SIZE), CH ** -0.5, 1.5),
        "expand_bias": bell_draw(streams_of[6], (HIDDEN_SIZE,), 0.5, 3.0, (), jnp.float32),
        "reduce_weight": bell_draw(streams_of[7], (HIDDEN_SIZE, CH), HIDDEN_SIZE ** -0.5, 0.75),
        "reduce_bias": bell_draw(streams_of[8], (CH,), 0.5, 3.0, (), jnp.float32),
    }


highest = lax.Precision.HIGHEST


def kept_index(mode_count, length):
    indices = jnp.arange(mode_count, dtype=jnp.int32)
    return jnp.where(indices < mode_count // 2, indices, length - mode_count + indices).astype(jnp.int32)


def kept_freq(mode_count):
    indices = jnp.arange(mode_count, dtype=jnp.int32)
    return jnp.where(indices < mode_count // 2, indices, indices - mode_count).astype(jnp.int32)


def phase_tables(frequencies, positions, length):
    product = jnp.remainder(frequencies[:, None] * positions[None, :], length)
    angles = product.astype(jnp.float32) * (2.0 * math.pi / length)
    return jnp.cos(angles), jnp.sin(angles)


def rounded(values):
    narrow = lax.optimization_barrier(values.astype(jnp.bfloat16))
    return narrow.astype(jnp.float32)


def reference(occupancy, embedding, spectral_weight, point_weight, point_bias, expand_weight, expand_bias, reduce_weight, reduce_bias):
    z_index = kept_index(MODES, NZ)
    x_index = kept_index(MODES, NX)
    frequencies = kept_freq(MODES)
    y_cos, y_sin = phase_tables(frequencies, jnp.arange(NY, dtype=jnp.int32), NY)
    y_cos = rounded(y_cos)
    y_sin = rounded(y_sin)

    def class_spectrum(label):
        indicator = (occupancy == label).astype(jnp.float32)
        rows_real = jnp.einsum('zxy,ky->zxk', indicator, y_cos, precision=highest)
        rows_imag = -jnp.einsum('zxy,ky->zxk', indicator, y_sin, precision=highest)
        spectrum = rows_real + 1j * rows_imag
        spectrum = jnp.fft.fft(spectrum, axis=1)
        spectrum = jnp.take(spectrum, x_index, axis=1)
        spectrum = jnp.fft.fft(spectrum, axis=0)
        spectrum = jnp.take(spectrum, z_index, axis=0)
        return jnp.stack([jnp.real(spectrum), jnp.imag(spectrum)])

    per_class = lax.map(class_spectrum, jnp.arange(NCLASS, dtype=jnp.int32))
    spectrum = jnp.einsum('lc,lrzxy->crzxy', embedding, per_class, precision=highest)
    weight = spectral_weight.reshape(MODES, MODES, MODES, 2, CH, CH)
    w_real = weight[:, :, :, 0]
    w_imag = weight[:, :, :, 1]
    s_real = spectrum[:, 0]
    s_imag = spectrum[:, 1]
    total = NZ * NX * NY
    m_real = (jnp.einsum('yxzab,azxy->bzxy', w_real, s_real, precision=highest)
              - jnp.einsum('yxzab,azxy->bzxy', w_imag, s_imag, precision=highest)) / total
    m_imag = (jnp.einsum('yxzab,azxy->bzxy', w_real, s_imag, precision=highest)
              + jnp.einsum('yxzab,azxy->bzxy', w_imag, s_real, precision=highest)) / total
    x_cos, x_sin = phase_tables(frequencies, jnp.arange(NX, dtype=jnp.int32), NX)
    table = jnp.dot(embedding, point_weight, precision=highest) + point_bias
    slab_size = 8

    def one_slab(slab_index, result):
        start = (slab_index * slab_size).astype(jnp.int32)
        positions = start + jnp.arange(slab_size, dtype=jnp.int32)
        z_cos, z_sin = phase_tables(frequencies, positions, NZ)
        g_real = (jnp.einsum('czxy,zw->cwxy', m_real, z_cos, precision=highest)
                  - jnp.einsum('czxy,zw->cwxy', m_imag, z_sin, precision=highest))
        g_imag = (jnp.einsum('czxy,zw->cwxy', m_real, z_sin, precision=highest)
                  + jnp.einsum('czxy,zw->cwxy', m_imag, z_cos, precision=highest))
        h_real = (jnp.einsum('cwxy,xn->cwny', g_real, x_cos, precision=highest)
                  - jnp.einsum('cwxy,xn->cwny', g_imag, x_sin, precision=highest))
        h_imag = (jnp.einsum('cwxy,xn->cwny', g_real, x_sin, precision=highest)
                  + jnp.einsum('cwxy,xn->cwny', g_imag, x_cos, precision=highest))
        h_real = rounded(h_real)
        h_imag = rounded(h_imag)
        spatial = (jnp.einsum('cwny,ym->cwnm', h_real, y_cos, precision=highest)
                   - jnp.einsum('cwny,ym->cwnm', h_imag, y_sin, precision=highest))
        labels = lax.dynamic_slice_in_dim(occupancy, start, slab_size, 0)
        pointwise = jnp.moveaxis(jnp.take(table, labels, axis=0), -1, 0)
        activated = jax.nn.gelu(spatial + pointwise, approximate=False).astype(jnp.bfloat16)
        hidden = jnp.einsum('ch,cwnm->hwnm', expand_weight.astype(jnp.float32), activated.astype(jnp.float32), precision=highest)
        hidden = jax.nn.gelu(hidden + expand_bias[:, None, None, None], approximate=False).astype(jnp.bfloat16)
        encoded = jnp.einsum('hc,hwnm->cwnm', reduce_weight.astype(jnp.float32), hidden.astype(jnp.float32), precision=highest)
        encoded = encoded + reduce_bias[:, None, None, None]
        return lax.dynamic_update_slice_in_dim(result, encoded.astype(jnp.bfloat16), start, 1)

    return lax.fori_loop(0, NZ // slab_size, one_slab, jnp.zeros((CH, NZ, NX, NY), jnp.bfloat16))
```

```python
import functools
import math

import jax
import jax.numpy as jnp
import ml_dtypes
import numpy as np
from jax import lax
from jax.experimental import pallas as pl
from jax.experimental.pallas import tpu as pltpu
from jax.sharding import PartitionSpec as P

NZ = 256
NX = 512
NY = 256
CH = 16
MODES = 16
NCLASS = 12
HIDDEN = 64
LZ = 64
LX = 8
ROWS = LZ * LX

highest = lax.Precision.HIGHEST
f32 = jnp.float32
bf16 = jnp.bfloat16
FREQ = np.where(np.arange(MODES) < 8, np.arange(MODES), np.arange(MODES) - MODES)


def split(values):
    hi = values.astype(ml_dtypes.bfloat16)
    lo = (values - hi.astype(np.float64)).astype(ml_dtypes.bfloat16)
    return hi, lo


def y_tables():
    product = np.remainder(FREQ[:, None] * np.arange(NY)[None, :], NY)
    angles = product.astype(np.float32) * np.float32(2.0 * math.pi / NY)
    cos = np.cos(angles).astype(ml_dtypes.bfloat16)
    sin = np.sin(angles).astype(ml_dtypes.bfloat16)
    return np.stack([cos, -sin], axis=1).reshape(2 * MODES, NY)


def plane_tables():
    z = np.arange(LZ)
    x = np.arange(LX)
    turn = (
        2 * FREQ[None, :, None, None] * z[None, None, :, None]
        + FREQ[:, None, None, None] * x[None, None, None, :]
    )
    angles = 2.0 * np.pi * np.remainder(turn, NX) / NX
    table = np.stack([np.cos(angles), np.sin(angles)])
    return table.reshape(2 * MODES * MODES, ROWS)


def pen_phases():
    turn = np.remainder(np.arange(64)[:, None] * FREQ[None, :], 64)
    angles = 2.0 * np.pi * turn / 64
    return np.concatenate([np.cos(angles), np.sin(angles)], axis=1).astype(np.float32)


def iota(shape, axis):
    return lax.broadcasted_iota(jnp.int32, shape, axis)


def times_j(tile):
    imag_lane = (iota(tile.shape, 1) // 16) % 2 == 1
    return jnp.where(imag_lane, pltpu.roll(tile, 16, 1), -pltpu.roll(tile, 112, 1))


def swap_blocks(tile):
    row = iota(tile.shape, 0) % 4
    block = iota(tile.shape, 1) // 32
    out = tile
    for step in (-3, -2, -1, 1, 2, 3):
        moved = pltpu.roll(pltpu.roll(tile, (-step) % 16, 0), (32 * step) % 128, 1)
        out = jnp.where(block - row == step, moved, out)
    return out


def to_parts(values):
    hi = values.astype(bf16)
    lo = (values - hi.astype(f32)).astype(bf16)
    return hi, lo


def dot(left, right, dims=((1,), (0,)), precision=None):
    return lax.dot_general(
        left, right, (dims, ((), ())), precision=precision, preferred_element_type=f32
    )


def forward_kernel(occ_ref, ytab_ref, hi_ref, lo_ref, out_ref, rows_ref):
    rows_ref[...] = jnp.zeros_like(rows_ref)
    labels = occ_ref[...]
    for label in range(NCLASS):
        hot = jnp.where(labels == label, 1.0, 0.0).astype(bf16)
        part = dot(ytab_ref[...], hot, ((1,), (1,)))
        for quarter in range(4):
            rows_ref[quarter, pl.ds(label, 32, stride=16), :] = part[
                :, quarter * 128 : (quarter + 1) * 128
            ]
    for group in range(4):
        block = [rows_ref[quarter, pl.ds(group * 128, 128), :] for quarter in range(4)]
        block_hi, block_lo = to_parts(jnp.concatenate(block, axis=1))
        nt = ((1,), (1,))
        full = (
            dot(hi_ref[...], block_hi, nt)
            + dot(hi_ref[...], block_lo, nt)
            + dot(lo_ref[...], block_hi, nt)
        )
        out_ref[group] = full[:256] - times_j(full[256:])


def gather_groups_kernel(phase_ref, in_ref, out_ref, mid_ref):
    quarter = iota((16, 128), 0) % 4
    zero = jnp.zeros((16, 128), f32)
    for kx in range(MODES):
        tiles = [in_ref[g, pl.ds(kx * 16, 16), :] for g in range(4)]
        real = zero
        imag = zero
        for g in range(4):
            turn = (quarter * g) % 4
            real = real + jnp.where(turn == 0, tiles[g], jnp.where(turn == 2, -tiles[g], zero))
            imag = imag + jnp.where(turn == 3, tiles[g], jnp.where(turn == 1, -tiles[g], zero))
        cos = phase_ref[kx]
        sin = phase_ref[16 + kx]
        tile = (real * cos + imag * sin) + times_j(imag * cos - real * sin)
        mid_ref[pl.ds(kx * 16, 16), :] = swap_blocks(tile)
    for q in range(4):
        out_ref[pl.ds(q * 64, 64), :] = mid_ref[pl.ds(q, 64, stride=4), :]


def mix_kernel(in_ref, weight_ref, emb_ref, rep_ref, out_ref):
    total = in_ref[0:8, :]
    for step in range(1, 32):
        total = total + in_ref[pl.ds(step * 8, 8), :]
    total = total + pltpu.roll(total, 4, 0)
    left = jnp.where(iota((128, NCLASS), 0) % 16 == iota((128, NCLASS), 1), 1.0, 0.0).astype(f32)
    right = jnp.where(iota((16, 128), 1) % 16 == iota((16, 128), 0), 1.0, 0.0).astype(f32)
    wide = dot(dot(left, emb_ref[...], precision=highest), right, precision=highest)
    wide = jnp.where(iota((128, 128), 0) // 16 == iota((128, 128), 1) // 16, wide, 0.0)
    lifted = dot(total, wide, precision=highest)
    first = lifted.astype(bf16)
    rest = lifted - first.astype(f32)
    second = rest.astype(bf16)
    third = (rest - second.astype(f32)).astype(bf16)
    rep = rep_ref[...]
    spread = dot(first, rep) + dot(second, rep) + dot(third, rep)
    weight = jnp.concatenate([weight_ref[...], weight_ref[...]], axis=0)
    pieces = []
    for k in range(4):
        s_real = spread[:, k * 512 : k * 512 + 256]
        s_imag = spread[:, k * 512 + 256 : k * 512 + 512]
        w_real = weight[:, k * 512 : k * 512 + 256]
        w_imag = weight[:, k * 512 + 256 : k * 512 + 512]
        pieces.append(w_real * s_real - w_imag * s_imag)
        pieces.append(w_real * s_imag + w_imag * s_real)
    acc = jnp.zeros((8, 128), f32)
    spot = iota((256, 128), 1)
    source = iota((256, 128), 0) % 16
    for n in range(8):
        pick = jnp.where(spot == source + 16 * n, 1.0, 0.0).astype(f32)
        acc = acc + dot(pieces[n], pick, precision=highest)
    acc = acc * (1.0 / (NZ * NX * NY))
    for step in range(32):
        out_ref[pl.ds(step * 8, 8), :] = acc


def scatter_groups_kernel(phase_ref, in_ref, out_ref, mid_ref):
    quarter = iota((16, 128), 0) % 4
    zero = jnp.zeros((16, 128), f32)
    for q in range(4):
        mid_ref[pl.ds(q, 64, stride=4), :] = in_ref[pl.ds(q * 64, 64), :]
    for kx in range(MODES):
        tile = swap_blocks(mid_ref[pl.ds(kx * 16, 16), :])
        turned = times_j(tile)
        cos = phase_ref[kx]
        sin = phase_ref[16 + kx]
        real = tile * cos + turned * sin
        imag = turned * cos - tile * sin
        for g in range(4):
            turn = (quarter * g) % 4
            out_ref[g, pl.ds(kx * 16, 16), :] = jnp.where(
                turn == 0, real, jnp.where(turn == 1, imag, jnp.where(turn == 2, -real, -imag))
            )


def gelu(values):
    half = values * 0.5
    return half + half * lax.erf(values * np.float32(math.sqrt(0.5)))


ZB = 4


def point_kernel(
    modes_ref, hi_ref, lo_ref, ytab_ref, occ_ref, emb_ref, pw_ref, pb_ref, w1_ref, b1_ref, w2_ref,
    b2_ref, out_ref, planes_ref, table_ref, wide1_ref, wide2_ref, bias1_ref, bias2_ref,
):
    @pl.when(pl.program_id(0) == 0)
    def _():
        hi = hi_ref[...]
        lo = lo_ref[...]
        for g in range(4):
            tile = modes_ref[g]
            both = jnp.concatenate([tile, times_j(tile)], axis=0)
            part_hi, part_lo = to_parts(both)
            full = dot(hi, part_hi) + dot(hi, part_lo) + dot(lo, part_hi)
            planes_ref[:, pl.ds(g * 128, 128)] = full.astype(bf16).astype(f32)
        table = dot(pw_ref[...], emb_ref[...], ((0,), (1,)), highest)
        spread = jnp.where(
            iota((NCLASS, 128), 0) == iota((NCLASS, 128), 1), 1.0, 0.0
        ).astype(f32)
        eye = iota((16, 16), 0) == iota((16, 16), 1)
        bias = jnp.sum(jnp.where(eye, pb_ref[...], 0.0), axis=1, keepdims=True)
        table_ref[...] = dot(table, spread, precision=highest) + bias
        r1 = jnp.where(iota((512, 64), 0) % 64 == iota((512, 64), 1), 1.0, 0.0)
        r2 = jnp.where(iota((16, 128), 1) % 16 == iota((16, 128), 0), 1.0, 0.0).astype(bf16)
        a1 = dot(r1.astype(bf16), w1_ref[...], ((1,), (1,))).astype(bf16)
        full1 = dot(a1, r2)
        same1 = iota((512, 128), 0) // 64 == iota((512, 128), 1) // 16
        wide1_ref[...] = jnp.where(same1, full1, 0.0).astype(bf16)
        col1 = jnp.sum(r1 * b1_ref[...], axis=1, keepdims=True)
        bias1_ref[...] = jnp.broadcast_to(col1, (512, 128))
        r3 = jnp.where(iota((128, 16), 0) // 8 == iota((128, 16), 1), 1.0, 0.0)
        r4 = jnp.where(iota((64, 512), 1) % 64 == iota((64, 512), 0), 1.0, 0.0).astype(bf16)
        a2 = dot(r3.astype(bf16), w2_ref[...], ((1,), (1,))).astype(bf16)
        full2 = dot(a2, r4)
        same2 = iota((128, 512), 0) % 8 == iota((128, 512), 1) // 64
        wide2_ref[...] = jnp.where(same2, full2, 0.0).astype(bf16)
        col2 = jnp.sum(r3 * b2_ref[...], axis=1, keepdims=True)
        bias2_ref[...] = jnp.broadcast_to(col2, (128, 128))

    own = iota((16, 512), 0) == iota((16, 512), 1) % 16
    table = table_ref[...]
    bias1 = jnp.concatenate([bias1_ref[...]] * 2, axis=1)
    bias2 = jnp.concatenate([bias2_ref[...]] * 2, axis=1)
    for zi in range(ZB):
        base = pl.multiple_of((pl.program_id(0) * ZB + zi) * 8, 8)
        left = []
        point = []
        rows = planes_ref[pl.ds(base, 8), :]
        labels = occ_ref[pl.ds(base, 8), :]
        for x in range(LX):
            row = jnp.broadcast_to(rows[x : x + 1], (16, 512))
            left.append(jnp.where(own, row, 0.0).astype(bf16))
            for half in range(2):
                label = jnp.broadcast_to(
                    labels[x : x + 1, half * 128 : (half + 1) * 128], (16, 128)
                )
                point.append(jnp.take_along_axis(table, label, axis=1))
        left = jnp.concatenate(left, axis=0)
        pointwise = jnp.concatenate(
            [jnp.concatenate(point[0::2], axis=0), jnp.concatenate(point[1::2], axis=0)], axis=1
        )
        spatial = dot(left, ytab_ref[...])
        activated = gelu(spatial + pointwise).astype(bf16)
        hidden = gelu(dot(wide1_ref[...], activated) + bias1).astype(bf16)
        encoded = dot(wide2_ref[...], hidden) + bias2
        out_ref[:, zi] = encoded.reshape(16, 8, 256).astype(bf16)


def vmem():
    return pl.BlockSpec(memory_space=pltpu.VMEM)


def smem():
    return pl.BlockSpec(memory_space=pltpu.SMEM)


def shards(
    occupancy,
    embedding,
    spectral_weight,
    point_weight,
    point_bias,
    expand_weight,
    expand_bias,
    reduce_weight,
    reduce_bias,
):
    ytab = y_tables()
    hi, lo = split(plane_tables())
    labels = occupancy.reshape(ROWS, NY)
    phases = lax.dynamic_slice_in_dim(jnp.asarray(pen_phases()), lax.axis_index("pen"), 1, 0)[0]
    partial = pl.pallas_call(
        forward_kernel,
        out_shape=jax.ShapeDtypeStruct((4, 256, 128), f32),
        in_specs=[vmem()] * 4,
        out_specs=vmem(),
        scratch_shapes=[pltpu.VMEM((4, 512, 128), f32)],
        name="forward",
    )(labels, jnp.asarray(ytab), jnp.asarray(hi), jnp.asarray(lo))
    partial = lax.all_to_all(partial, "grp", 0, 0, tiled=True)
    chunks = pl.pallas_call(
        gather_groups_kernel,
        out_shape=jax.ShapeDtypeStruct((256, 128), f32),
        in_specs=[smem(), vmem()],
        out_specs=vmem(),
        scratch_shapes=[pltpu.VMEM((256, 128), f32)],
        name="gather_groups",
    )(phases, partial)
    chunks = lax.all_to_all(chunks.reshape(64, 4, 128), "pen", 0, 0, tiled=True)
    rep = (np.arange(2048)[None, :] // 16 == np.arange(128)[:, None]).astype(ml_dtypes.bfloat16)
    mixed = pl.pallas_call(
        mix_kernel,
        out_shape=jax.ShapeDtypeStruct((256, 128), f32),
        in_specs=[vmem()] * 4,
        out_specs=vmem(),
        name="mix",
    )(chunks.reshape(256, 128), spectral_weight.reshape(4, 2048), embedding, jnp.asarray(rep))
    mixed = lax.all_to_all(mixed.reshape(64, 4, 128), "pen", 0, 0, tiled=True)
    modes = pl.pallas_call(
        scatter_groups_kernel,
        out_shape=jax.ShapeDtypeStruct((4, 256, 128), f32),
        in_specs=[smem(), vmem()],
        out_specs=vmem(),
        scratch_shapes=[pltpu.VMEM((256, 128), f32)],
        name="scatter_groups",
    )(phases, mixed.reshape(256, 128))
    modes = lax.all_to_all(modes, "grp", 0, 0, tiled=True)
    whole = lambda *shape: pl.BlockSpec(shape, lambda i: (0,) * len(shape))
    return pl.pallas_call(
        point_kernel,
        out_shape=jax.ShapeDtypeStruct((CH, LZ, LX, NY), bf16),
        grid=(LZ // ZB,),
        in_specs=[
            whole(4, 256, 128),
            whole(512, 512),
            whole(512, 512),
            whole(512, 256),
            whole(512, 256),
            whole(NCLASS, CH),
            whole(CH, CH),
            whole(1, CH),
            whole(CH, HIDDEN),
            whole(1, HIDDEN),
            whole(HIDDEN, CH),
            whole(1, CH),
        ],
        out_specs=pl.BlockSpec((CH, ZB, LX, NY), lambda i: (0, i, 0, 0)),
        scratch_shapes=[
            pltpu.VMEM((512, 512), f32),
            pltpu.VMEM((16, 128), f32),
            pltpu.VMEM((512, 128), bf16),
            pltpu.VMEM((128, 512), bf16),
            pltpu.VMEM((512, 128), f32),
            pltpu.VMEM((128, 128), f32),
        ],
        name="point",
    )(
        modes,
        jnp.asarray(hi.T.copy()),
        jnp.asarray(lo.T.copy()),
        jnp.asarray(np.repeat(ytab, 16, axis=0)),
        labels,
        embedding,
        point_weight,
        point_bias.reshape(1, CH),
        expand_weight,
        expand_bias.reshape(1, HIDDEN),
        reduce_weight,
        reduce_bias.reshape(1, CH),
    )


def solution(mesh):
    return jax.shard_map(
        shards,
        mesh=mesh,
        in_specs=(
            P("grp", "pen", None),
            P(),
            P(("grp", "pen"), None, None, None, None),
            P(),
            P(),
            P(),
            P(),
            P(),
            P(),
        ),
        out_specs=P(None, "grp", "pen", None),
        check_vma=False,
    )
```

```python
import functools
import math

import jax
import jax.numpy as jnp
import ml_dtypes
import numpy as np
from jax import lax
from jax.experimental import pallas as pl
from jax.experimental.pallas import tpu as pltpu
from jax.sharding import PartitionSpec as P

NZ = 256
NX = 512
NY = 256
CH = 16
MODES = 16
NCLASS = 12
HIDDEN = 64
LZ = 64
LX = 8
ROWS = LZ * LX

highest = lax.Precision.HIGHEST
f32 = jnp.float32
bf16 = jnp.bfloat16
FREQ = np.where(np.arange(MODES) < 8, np.arange(MODES), np.arange(MODES) - MODES)


def split(values):
    hi = values.astype(ml_dtypes.bfloat16)
    lo = (values - hi.astype(np.float64)).astype(ml_dtypes.bfloat16)
    return hi, lo


def y_tables():
    product = np.remainder(FREQ[:, None] * np.arange(NY)[None, :], NY)
    angles = product.astype(np.float32) * np.float32(2.0 * math.pi / NY)
    cos = np.cos(angles).astype(ml_dtypes.bfloat16)
    sin = np.sin(angles).astype(ml_dtypes.bfloat16)
    return np.stack([cos, -sin], axis=1).reshape(2 * MODES, NY)


def z_tables():
    angles = 2.0 * np.pi * np.remainder(FREQ[None, :] * np.arange(LZ)[:, None], NZ) / NZ
    table = np.zeros((LZ, LX, 2, LX, MODES))
    for x in range(LX):
        table[:, x, 0, x] = np.cos(angles)
        table[:, x, 1, x] = np.sin(angles)
    return table.reshape(ROWS, 2 * LX * MODES)


def x_tables():
    angles = 2.0 * np.pi * np.remainder(FREQ[None, :] * np.arange(LX)[:, None], NX) / NX
    table = np.zeros((2, LX, MODES, MODES, MODES))
    for kz in range(MODES):
        table[0, :, kz, :, kz] = np.cos(angles)
        table[1, :, kz, :, kz] = np.sin(angles)
    return table.reshape(2, LX * MODES, MODES * MODES)


def y_lanes(ytab):
    table = ytab.reshape(2, 2, 4, 2, NY)
    table = np.moveaxis(table, (0, 1, 2, 3), (0, 3, 1, 2))
    return np.repeat(table.reshape(2 * MODES, NY), 8, axis=0)


def pen_phases():
    turn = np.remainder(np.arange(64)[:, None] * FREQ[None, :], 64)
    angles = 2.0 * np.pi * turn / 64
    return np.concatenate([np.cos(angles), np.sin(angles)], axis=1).astype(np.float32)


def iota(shape, axis):
    return lax.broadcasted_iota(jnp.int32, shape, axis)


def times_j(tile):
    imag_lane = (iota(tile.shape, 1) // 16) % 2 == 1
    return jnp.where(imag_lane, pltpu.roll(tile, 16, 1), -pltpu.roll(tile, 112, 1))


def swap_blocks(tile):
    row = iota(tile.shape, 0) % 4
    block = iota(tile.shape, 1) // 32
    out = tile
    for step in (-3, -2, -1, 1, 2, 3):
        moved = pltpu.roll(pltpu.roll(tile, (-step) % 16, 0), (32 * step) % 128, 1)
        out = jnp.where(block - row == step, moved, out)
    return out


def to_parts(values):
    hi = values.astype(bf16)
    lo = (values - hi.astype(f32)).astype(bf16)
    return hi, lo


def dot(left, right, dims=((1,), (0,)), precision=None):
    return lax.dot_general(
        left, right, (dims, ((), ())), precision=precision, preferred_element_type=f32
    )


def three(hi, lo, right):
    right_hi, right_lo = to_parts(right)
    return dot(hi, right_hi) + dot(hi, right_lo) + dot(lo, right_hi)


def forward_kernel(occ_ref, ytab_ref, hi_ref, lo_ref, out_ref, rows_ref):
    rows_ref[...] = jnp.zeros_like(rows_ref)
    labels = occ_ref[...]
    for label in range(NCLASS):
        hot = jnp.where(labels == label, 1.0, 0.0).astype(bf16)
        part = dot(ytab_ref[...], hot, ((1,), (1,)))
        for quarter in range(4):
            rows_ref[quarter, pl.ds(label, 32, stride=16), :] = part[
                :, quarter * 128 : (quarter + 1) * 128
            ]
    for group in range(4):
        block = [rows_ref[quarter, pl.ds(group * 128, 128), :] for quarter in range(4)]
        block_hi, block_lo = to_parts(jnp.concatenate(block, axis=1))
        nt = ((1,), (1,))
        full = (
            dot(hi_ref[...], block_hi, nt)
            + dot(hi_ref[...], block_lo, nt)
            + dot(lo_ref[...], block_hi, nt)
        )
        out_ref[group] = full[:128] - times_j(full[128:])


def gather_groups_kernel(phase_ref, hi_ref, lo_ref, in_ref, out_ref, mid_ref):
    spot = lax.axis_index("pen") * 32
    quarter = iota((128, 128), 0) % 4
    tiles = [in_ref[g] for g in range(4)]
    real = tiles[0]
    imag = jnp.zeros((128, 128), f32)
    for g in range(1, 4):
        turn = (quarter * g) % 4
        real = real + jnp.where(turn == 0, tiles[g], jnp.where(turn == 2, -tiles[g], 0.0))
        imag = imag + jnp.where(turn == 3, tiles[g], jnp.where(turn == 1, -tiles[g], 0.0))
    real = real + times_j(imag)
    both = three(hi_ref[...], lo_ref[...], jnp.concatenate([real, -times_j(real)], axis=0))
    turned = times_j(both)
    for kx in range(MODES):
        cos = phase_ref[spot + kx]
        sin = phase_ref[spot + 16 + kx]
        tile = both[kx * 16 : kx * 16 + 16] * cos - turned[kx * 16 : kx * 16 + 16] * sin
        mid_ref[pl.ds(kx * 16, 16), :] = swap_blocks(tile)
    for q in range(4):
        out_ref[pl.ds(q * 64, 64), :] = mid_ref[pl.ds(q, 64, stride=4), :]


def mix_kernel(in_ref, weight_ref, emb_ref, rep_ref, out_ref):
    total = in_ref[0:8, :]
    for step in range(1, 32):
        total = total + in_ref[pl.ds(step * 8, 8), :]
    total = total + pltpu.roll(total, 4, 0)
    left = jnp.where(iota((128, NCLASS), 0) % 16 == iota((128, NCLASS), 1), 1.0, 0.0).astype(f32)
    right = jnp.where(iota((16, 128), 1) % 16 == iota((16, 128), 0), 1.0, 0.0).astype(f32)
    wide = dot(dot(left, emb_ref[...], precision=highest), right, precision=highest)
    wide = jnp.where(iota((128, 128), 0) // 16 == iota((128, 128), 1) // 16, wide, 0.0)
    lifted = dot(total, wide, precision=highest)
    first = lifted.astype(bf16)
    rest = lifted - first.astype(f32)
    second = rest.astype(bf16)
    third = (rest - second.astype(f32)).astype(bf16)
    rep = rep_ref[...]
    spread = dot(first, rep) + dot(second, rep) + dot(third, rep)
    weight = jnp.concatenate([weight_ref[...], weight_ref[...]], axis=0)
    pieces = []
    for k in range(4):
        s_real = spread[:, k * 512 : k * 512 + 256]
        s_imag = spread[:, k * 512 + 256 : k * 512 + 512]
        w_real = weight[:, k * 512 : k * 512 + 256]
        w_imag = weight[:, k * 512 + 256 : k * 512 + 512]
        pieces.append(w_real * s_real - w_imag * s_imag)
        pieces.append(w_real * s_imag + w_imag * s_real)
    acc = jnp.zeros((8, 128), f32)
    spot = iota((256, 128), 1)
    source = iota((256, 128), 0) % 16
    for n in range(8):
        pick = jnp.where(spot == source + 16 * n, 1.0, 0.0).astype(f32)
        acc = acc + dot(pieces[n], pick, precision=highest)
    acc = acc * (1.0 / (NZ * NX * NY))
    for step in range(32):
        out_ref[pl.ds(step * 8, 8), :] = acc


def scatter_groups_kernel(phase_ref, hi_ref, lo_ref, in_ref, out_ref, mid_ref):
    spot = lax.axis_index("pen") * 32
    for q in range(4):
        mid_ref[pl.ds(q, 64, stride=4), :] = in_ref[pl.ds(q * 64, 64), :]
    real = []
    imag = []
    for kx in range(MODES):
        tile = swap_blocks(mid_ref[pl.ds(kx * 16, 16), :])
        turned = times_j(tile)
        cos = phase_ref[spot + kx]
        sin = phase_ref[spot + 16 + kx]
        real.append(tile * cos + turned * sin)
        imag.append(turned * cos - tile * sin)
    real = three(hi_ref[...], lo_ref[...], jnp.concatenate(real + imag, axis=0))
    imag = times_j(real)
    quarter = iota((128, 128), 0) % 4
    for g in range(4):
        turn = (quarter * g) % 4
        out_ref[g] = jnp.where(
            turn == 0, real, jnp.where(turn == 1, imag, jnp.where(turn == 2, -real, -imag))
        )


def twice_gelu(values):
    return values + values * lax.erf(values * np.float32(math.sqrt(0.5)))


ZB = 4


def point_kernel(
    modes_ref, hi_ref, lo_ref, ytab_ref, occ_ref, emb_ref, pw_ref, pb_ref, w1_ref, b1_ref, w2_ref,
    b2_ref, out_ref, planes_ref, table_ref, wide1_ref, wide2_ref, bias2_ref, label_ref,
):
    @pl.when(pl.program_id(0) == 0)
    def _():
        for half in range(2):
            label_ref[half] = occ_ref[:, half * 128 : (half + 1) * 128]
        hi = hi_ref[...]
        lo = lo_ref[...]
        high_lane = (iota((128, 128), 1) // 8) % 2 == 1
        for pair in range(2):
            even = modes_ref[2 * pair]
            odd = modes_ref[2 * pair + 1]
            for c_hi in range(2):
                if c_hi == 0:
                    tile = jnp.where(high_lane, pltpu.roll(odd, 8, 1), even)
                else:
                    tile = jnp.where(high_lane, odd, pltpu.roll(even, 120, 1))
                full = three(hi, lo, jnp.concatenate([tile, times_j(tile)], axis=0))
                planes_ref[c_hi * 2 + pair] = full.astype(bf16).astype(f32)
        table = dot(pw_ref[...], emb_ref[...], ((0,), (1,)), highest)
        spread = jnp.where(
            iota((NCLASS, 128), 0) == iota((NCLASS, 128), 1), 1.0, 0.0
        ).astype(f32)
        eye = iota((16, 16), 0) == iota((16, 16), 1)
        bias = jnp.sum(jnp.where(eye, pb_ref[...], 0.0), axis=1, keepdims=True)
        table_ref[...] = dot(table, spread, precision=highest) + bias
        r1 = jnp.where(iota((512, 64), 0) % 64 == iota((512, 64), 1), 1.0, 0.0)
        r2 = jnp.where(iota((16, 128), 1) % 16 == iota((16, 128), 0), 0.5, 0.0).astype(bf16)
        a1 = dot(r1.astype(bf16), w1_ref[...], ((1,), (1,))).astype(bf16)
        full1 = dot(a1, r2)
        same1 = iota((512, 128), 0) // 64 == iota((512, 128), 1) // 16
        wide1_ref[:, 0:128] = jnp.where(same1, full1, 0.0).astype(bf16)
        col1 = jnp.sum(r1 * b1_ref[...], axis=1, keepdims=True)
        first = col1.astype(bf16).astype(f32)
        second = (col1 - first).astype(bf16).astype(f32)
        third = col1 - first - second
        lane = iota((512, 128), 1)
        wide1_ref[:, 128:256] = jnp.where(
            lane == 0, first, jnp.where(lane == 1, second, jnp.where(lane == 2, third, 0.0))
        ).astype(bf16)
        r3 = jnp.where(iota((128, 16), 0) // 8 == iota((128, 16), 1), 1.0, 0.0)
        r4 = jnp.where(iota((64, 512), 1) % 64 == iota((64, 512), 0), 0.5, 0.0).astype(bf16)
        a2 = dot(r3.astype(bf16), w2_ref[...]).astype(bf16)
        full2 = dot(a2, r4)
        same2 = iota((128, 512), 0) % 8 == iota((128, 512), 1) // 64
        wide2_ref[...] = jnp.where(same2, full2, 0.0).astype(bf16)
        col2 = jnp.sum(r3 * b2_ref[...], axis=1, keepdims=True)
        bias2_ref[...] = jnp.broadcast_to(col2, (128, 128))

    own = jnp.where(iota((16, 256), 0) % 8 == iota((16, 256), 1) % 8, 1.0, 0.0).astype(bf16)
    low = table_ref[0:8, :]
    high = table_ref[8:16, :]
    ones = jnp.ones((16, 256), bf16)
    bias2 = jnp.concatenate([bias2_ref[...]] * 2, axis=1)
    left = []
    for zi in range(ZB):
        base = pl.multiple_of((pl.program_id(0) * ZB + zi) * 8, 8)
        for x in range(LX):
            rows = [planes_ref[t, pl.ds(base + x, 8, stride=0), :] for t in range(4)]
            block = jnp.concatenate(
                [jnp.concatenate(rows[0:2], axis=1), jnp.concatenate(rows[2:4], axis=1)], axis=0
            )
            left.append(block.astype(bf16) * own)
    spatial = dot(jnp.concatenate(left, axis=0), ytab_ref[...])
    for zi in range(ZB):
        base = pl.multiple_of((pl.program_id(0) * ZB + zi) * 8, 8)
        point = []
        for x in range(LX):
            halves = []
            for half in range(2):
                label = label_ref[half, pl.ds(base + x, 8, stride=0), :]
                halves.append(
                    jnp.concatenate(
                        [
                            jnp.take_along_axis(low, label, axis=1),
                            jnp.take_along_axis(high, label, axis=1),
                        ],
                        axis=0,
                    )
                )
            point.append(jnp.concatenate(halves, axis=1))
        pointwise = jnp.concatenate(point, axis=0)
        activated = twice_gelu(spatial[zi * 128 : zi * 128 + 128] + pointwise).astype(bf16)
        hidden = dot(wide1_ref[:, 0:144], jnp.concatenate([activated, ones], axis=0))
        hidden = twice_gelu(hidden).astype(bf16)
        encoded = dot(wide2_ref[...], hidden) + bias2
        out_ref[:, zi] = encoded.reshape(16, 8, 256).astype(bf16)


def room(mib):
    return pltpu.CompilerParams(vmem_limit_bytes=mib * 1024 * 1024)


def vmem():
    return pl.BlockSpec(memory_space=pltpu.VMEM)


def smem():
    return pl.BlockSpec(memory_space=pltpu.SMEM)


def shards(
    occupancy,
    embedding,
    spectral_weight,
    point_weight,
    point_bias,
    expand_weight,
    expand_bias,
    reduce_weight,
    reduce_bias,
):
    ytab = y_tables()
    z_hi, z_lo = split(z_tables())
    x_hi, x_lo = split(x_tables())
    x_in = [jnp.asarray(t.transpose(2, 0, 1).reshape(256, 256)) for t in (x_hi, x_lo)]
    x_out = [jnp.asarray(t.transpose(1, 0, 2).reshape(128, 512)) for t in (x_hi, x_lo)]
    labels = occupancy.reshape(ROWS, NY)
    phases = jnp.asarray(pen_phases().reshape(-1))
    partial = pl.pallas_call(
        forward_kernel,
        out_shape=jax.ShapeDtypeStruct((4, 128, 128), f32),
        in_specs=[vmem()] * 4,
        out_specs=vmem(),
        scratch_shapes=[pltpu.VMEM((4, 512, 128), f32)],
        compiler_params=room(16),
        name="forward",
    )(labels, jnp.asarray(ytab), jnp.asarray(z_hi.T.copy()), jnp.asarray(z_lo.T.copy()))
    weight = spectral_weight.reshape(4, 2048)
    partial, weight = lax.optimization_barrier((partial, weight))
    partial = lax.all_to_all(partial, "grp", 0, 0, tiled=True)
    chunks = pl.pallas_call(
        gather_groups_kernel,
        out_shape=jax.ShapeDtypeStruct((256, 128), f32),
        in_specs=[smem()] + [vmem()] * 3,
        out_specs=vmem(),
        scratch_shapes=[pltpu.VMEM((256, 128), f32)],
        compiler_params=room(8),
        name="gather_groups",
    )(phases, *x_in, partial)
    chunks = lax.all_to_all(chunks.reshape(64, 4, 128), "pen", 0, 0, tiled=True)
    rep = (np.arange(2048)[None, :] // 16 == np.arange(128)[:, None]).astype(ml_dtypes.bfloat16)
    mixed = pl.pallas_call(
        mix_kernel,
        out_shape=jax.ShapeDtypeStruct((256, 128), f32),
        in_specs=[vmem()] * 4,
        out_specs=vmem(),
        compiler_params=room(8),
        name="mix",
    )(chunks.reshape(256, 128), weight, embedding, jnp.asarray(rep))
    mixed = lax.all_to_all(mixed.reshape(64, 4, 128), "pen", 0, 0, tiled=True)
    modes = pl.pallas_call(
        scatter_groups_kernel,
        out_shape=jax.ShapeDtypeStruct((4, 128, 128), f32),
        in_specs=[smem()] + [vmem()] * 3,
        out_specs=vmem(),
        scratch_shapes=[pltpu.VMEM((256, 128), f32)],
        compiler_params=room(8),
        name="scatter_groups",
    )(phases, *x_out, mixed.reshape(256, 128))
    modes = lax.all_to_all(modes, "grp", 0, 0, tiled=True)
    whole = lambda *shape: pl.BlockSpec(shape, lambda i: (0,) * len(shape))
    return pl.pallas_call(
        point_kernel,
        out_shape=jax.ShapeDtypeStruct((CH, LZ, LX, NY), bf16),
        grid=(LZ // ZB,),
        in_specs=[
            whole(4, 128, 128),
            whole(512, 256),
            whole(512, 256),
            whole(256, 256),
            whole(512, 256),
            whole(NCLASS, CH),
            whole(CH, CH),
            whole(1, CH),
            whole(CH, HIDDEN),
            whole(1, HIDDEN),
            whole(CH, HIDDEN),
            whole(1, CH),
        ],
        out_specs=pl.BlockSpec((CH, ZB, LX, NY), lambda i: (0, i, 0, 0)),
        scratch_shapes=[
            pltpu.VMEM((4, 512, 128), f32),
            pltpu.VMEM((16, 128), f32),
            pltpu.VMEM((512, 256), bf16),
            pltpu.VMEM((128, 512), bf16),
            pltpu.VMEM((128, 128), f32),
            pltpu.VMEM((2, 512, 128), jnp.int32),
        ],
        compiler_params=room(28),
        name="point",
    )(
        modes,
        jnp.asarray(z_hi),
        jnp.asarray(z_lo),
        jnp.asarray(y_lanes(ytab)),
        labels,
        embedding,
        point_weight,
        point_bias.reshape(1, CH),
        expand_weight,
        expand_bias.reshape(1, HIDDEN),
        reduce_weight.T,
        reduce_bias.reshape(1, CH),
    )


def solution(mesh):
    return jax.shard_map(
        shards,
        mesh=mesh,
        in_specs=(
            P("grp", "pen", None),
            P(),
            P(("grp", "pen"), None, None, None, None),
            P(),
            P(),
            P(),
            P(),
            P(),
            P(),
        ),
        out_specs=P(None, "grp", "pen", None),
        check_vma=False,
    )
```

```python
import functools
import math

import jax
import jax.numpy as jnp
import ml_dtypes
import numpy as np
from jax import lax
from jax.experimental import pallas as pl
from jax.experimental.pallas import tpu as pltpu
from jax.sharding import PartitionSpec as P

NZ = 256
NX = 512
NY = 256
CH = 16
MODES = 16
NCLASS = 12
HIDDEN = 64
LZ = 64
LX = 8
ROWS = LZ * LX

highest = lax.Precision.HIGHEST
f32 = jnp.float32
bf16 = jnp.bfloat16
FREQ = np.where(np.arange(MODES) < 8, np.arange(MODES), np.arange(MODES) - MODES)


def split(values):
    hi = values.astype(ml_dtypes.bfloat16)
    lo = (values - hi.astype(np.float64)).astype(ml_dtypes.bfloat16)
    return hi, lo


def y_tables():
    product = np.remainder(FREQ[:, None] * np.arange(NY)[None, :], NY)
    angles = product.astype(np.float32) * np.float32(2.0 * math.pi / NY)
    cos = np.cos(angles).astype(ml_dtypes.bfloat16)
    sin = np.sin(angles).astype(ml_dtypes.bfloat16)
    return np.stack([cos, -sin], axis=1).reshape(2 * MODES, NY)


def z_tables():
    angles = 2.0 * np.pi * np.remainder(FREQ[None, :] * np.arange(LZ)[:, None], NZ) / NZ
    table = np.zeros((LZ, LX, 2, LX, MODES))
    for x in range(LX):
        table[:, x, 0, x] = np.cos(angles)
        table[:, x, 1, x] = np.sin(angles)
    return table.reshape(ROWS, 2 * LX * MODES)


def x_tables():
    angles = 2.0 * np.pi * np.remainder(FREQ[None, :] * np.arange(LX)[:, None], NX) / NX
    table = np.zeros((2, LX, MODES, MODES, MODES))
    for kz in range(MODES):
        table[0, :, kz, :, kz] = np.cos(angles)
        table[1, :, kz, :, kz] = np.sin(angles)
    table = table.reshape(2, LX * MODES, MODES, 4, 4)
    return table.transpose(0, 1, 4, 3, 2).reshape(2, LX * MODES, MODES * MODES)


def y_lanes(ytab):
    table = ytab.reshape(2, 2, 4, 2, NY)
    table = np.moveaxis(table, (0, 1, 2, 3), (0, 3, 1, 2))
    return np.repeat(table.reshape(2 * MODES, NY), 8, axis=0)


def pen_phases():
    turn = np.remainder(np.arange(64)[:, None] * FREQ[None, :], 64)
    angles = 2.0 * np.pi * turn / 64
    table = np.zeros((64, 128), np.float32)
    table[:, 0:16] = np.cos(angles)
    table[:, 16:32] = np.sin(angles)
    return table


def iota(shape, axis):
    return lax.broadcasted_iota(jnp.int32, shape, axis)


def times_j(tile):
    imag_lane = (iota(tile.shape, 1) // 16) % 2 == 1
    return jnp.where(imag_lane, pltpu.roll(tile, 16, 1), -pltpu.roll(tile, 112, 1))


def exchange(tiles):
    block = iota(tiles[0].shape, 1) // 32
    out = []
    for i in range(4):
        best = tiles[i]
        for j in range(4):
            if j != i:
                best = jnp.where(block == j, pltpu.roll(tiles[j], 32 * (j - i) % 128, 1), best)
        out.append(best)
    return out


def quarter_signs(shape):
    quarter = iota(shape, 0) % 4
    cos = jnp.where(quarter == 0, 1.0, jnp.where(quarter == 2, -1.0, 0.0))
    sin = jnp.where(quarter == 1, 1.0, jnp.where(quarter == 3, -1.0, 0.0))
    flip = jnp.where(quarter % 2 == 0, 1.0, -1.0)
    return cos, sin, flip


def to_parts(values):
    hi = values.astype(bf16)
    lo = (values - hi.astype(f32)).astype(bf16)
    return hi, lo


def dot(left, right, dims=((1,), (0,)), precision=None):
    return lax.dot_general(
        left, right, (dims, ((), ())), precision=precision, preferred_element_type=f32
    )


def three(hi, lo, right):
    right_hi, right_lo = to_parts(right)
    return dot(hi, right_hi) + dot(hi, right_lo) + dot(lo, right_hi)


def forward_kernel(
    occ, ytab, zt_hi, zt_lo, xi_hi, xi_lo, xo_hi, xo_lo, z_hi, z_lo, ylane, phase, emb, weight,
    pw, pb, w1, b1, w2, b2,
    out_ref, wide_ref, rep_ref, xi_hi_out, xi_lo_out, xo_hi_out, xo_lo_out, z_hi_out, z_lo_out,
    ylane_out, label_ref, phase_out, table_ref, wide1_ref, wide2_ref, bias2_ref,
    occ_v, ytab_v, zt_hi_v, zt_lo_v, phase_v, emb_v, weight_v, pw_v, pb_v, w1_v, b1_v, w2_v, b2_v,
    small_ref, rows_ref, sems,
):
    pairs = [
        (occ, occ_v), (ytab, ytab_v), (zt_hi, zt_hi_v), (zt_lo, zt_lo_v), (emb, emb_v),
        (weight, weight_v), (pw, pw_v), (pb, pb_v), (w1, w1_v), (b1, b1_v), (w2, w2_v), (b2, b2_v),
        (phase, phase_v), (xi_hi, xi_hi_out), (xi_lo, xi_lo_out), (xo_hi, xo_hi_out),
        (xo_lo, xo_lo_out), (z_hi, z_hi_out), (z_lo, z_lo_out), (ylane, ylane_out),
    ]
    copies = [pltpu.make_async_copy(a, b, sems.at[i]) for i, (a, b) in enumerate(pairs)]
    for copy in copies:
        copy.start()
    rows_ref[...] = jnp.zeros_like(rows_ref)
    copies[0].wait()
    copies[1].wait()
    for half in range(2):
        piece = occ_v[:, half * 128 : (half + 1) * 128]
        label_ref[half] = piece
        small_ref[:, half * 128 : (half + 1) * 128] = piece.astype(f32).astype(bf16)
    for label in range(NCLASS):
        same = small_ref[...] == jnp.array(label, bf16)
        hot = jnp.where(same, jnp.array(1.0, bf16), jnp.array(0.0, bf16))
        part = dot(ytab_v[...], hot, ((1,), (1,)))
        for quarter in range(4):
            rows_ref[quarter, pl.ds(label, 32, stride=16), :] = part[
                :, quarter * 128 : (quarter + 1) * 128
            ]
    for copy in copies[2:]:
        copy.wait()
    nt = ((1,), (1,))
    for pair in range(2):
        block = [rows_ref[quarter, pl.ds(pair * 256, 256), :] for quarter in range(4)]
        block_hi, block_lo = to_parts(jnp.concatenate(block, axis=1))
        full = (
            dot(zt_hi_v[...], block_hi, nt)
            + dot(zt_hi_v[...], block_lo, nt)
            + dot(zt_lo_v[...], block_hi, nt)
        )
        for half in range(2):
            tile = full[:, half * 128 : (half + 1) * 128]
            out_ref[pair * 2 + half] = tile[:128] - times_j(tile[128:])

    left = jnp.where(iota((128, NCLASS), 0) % 16 == iota((128, NCLASS), 1), 1.0, 0.0).astype(f32)
    right = jnp.where(iota((16, 128), 1) % 16 == iota((16, 128), 0), 1.0, 0.0).astype(f32)
    lifted = dot(left, emb_v[...], precision=highest)
    wide = dot(right, lifted, ((0,), (1,)), highest)
    wide_ref[...] = jnp.where(
        iota((128, 128), 0) // 16 == iota((128, 128), 1) // 16, wide, 0.0
    )
    rep_ref[...] = jnp.concatenate([weight_v[...]] * 8, axis=1)
    row = phase_v[pl.ds(lax.axis_index("pen"), 16, stride=0), :]
    for half in range(2):
        pick = iota((16, 128), 1) == iota((16, 128), 0) + 16 * half
        column = jnp.sum(jnp.where(pick, row, 0.0), axis=1, keepdims=True)
        phase_out[half] = jnp.broadcast_to(column, (16, 128))

    table = dot(pw_v[...], emb_v[...], ((0,), (1,)), highest)
    spread = jnp.where(
        iota((NCLASS, 128), 0) == iota((NCLASS, 128), 1), 1.0, 0.0
    ).astype(f32)
    eye = iota((16, 16), 0) == iota((16, 16), 1)
    bias = jnp.sum(jnp.where(eye, pb_v[...], 0.0), axis=1, keepdims=True)
    table_ref[...] = dot(table, spread, precision=highest) + bias
    r1 = jnp.where(iota((64, 64), 0) == iota((64, 64), 1), 1.0, 0.0)
    r2 = jnp.where(iota((16, 128), 1) % 16 == iota((16, 128), 0), 0.5, 0.0).astype(bf16)
    full1 = dot(dot(r1.astype(bf16), w1_v[...], ((1,), (1,))).astype(bf16), r2)
    col1 = jnp.broadcast_to(jnp.sum(r1 * b1_v[...], axis=1, keepdims=True), (64, 128))
    first = col1.astype(bf16).astype(f32)
    second = (col1 - first).astype(bf16).astype(f32)
    third = col1 - first - second
    lane = iota((64, 128), 1)
    extra = jnp.where(
        lane == 0, first, jnp.where(lane == 1, second, jnp.where(lane == 2, third, 0.0))
    ).astype(bf16)
    for x in range(LX):
        wide1_ref[x * 64 : x * 64 + 64, 0:128] = jnp.where(lane // 16 == x, full1, 0.0).astype(bf16)
        wide1_ref[x * 64 : x * 64 + 64, 128:256] = extra
    r3 = jnp.where(iota((128, 16), 0) // 8 == iota((128, 16), 1), 1.0, 0.0)
    r4 = jnp.where(iota((64, 128), 1) % 64 == iota((64, 128), 0), 0.5, 0.0).astype(bf16)
    full2 = dot(dot(r3.astype(bf16), w2_v[...]).astype(bf16), r4)
    x_row = iota((128, 128), 0) % 8
    x_lane = iota((128, 128), 1) // 64
    for tile in range(4):
        wide2_ref[:, tile * 128 : tile * 128 + 128] = jnp.where(
            x_row == x_lane + 2 * tile, full2, 0.0
        ).astype(bf16)
    col2 = jnp.sum(r3 * b2_v[...], axis=1, keepdims=True)
    bias2_ref[...] = jnp.broadcast_to(col2, (128, 128))


def gather_groups_kernel(phase_ref, hi_ref, lo_ref, in_ref, out_ref):
    cos, sin, flip = quarter_signs((128, 128))
    real = in_ref[0] + flip * in_ref[2] + cos * (in_ref[1] + in_ref[3])
    imag = sin * (in_ref[3] - in_ref[1])
    real = real + times_j(imag)
    both = three(hi_ref[...], lo_ref[...], jnp.concatenate([real, -times_j(real)], axis=0))
    turned = times_j(both)
    for kz_hi in range(4):
        tiles = []
        for kz_lo in range(4):
            rows = slice((kz_lo * 4 + kz_hi) * 16, (kz_lo * 4 + kz_hi) * 16 + 16)
            tiles.append(both[rows] * phase_ref[0] - turned[rows] * phase_ref[1])
        for q, tile in enumerate(exchange(tiles)):
            out_ref[pl.ds(q * 64 + kz_hi, 16, stride=4), :] = tile


def mix_kernel(in_ref, weight_ref, wide_ref, out_ref):
    parts = [in_ref[pl.ds(step * 8, 8), :] for step in range(32)]
    while len(parts) > 1:
        parts = [a + b for a, b in zip(parts[0::2], parts[1::2])]
    total = parts[0] + pltpu.roll(parts[0], 4, 0)
    columns = dot(wide_ref[...], total, ((1,), (1,)), highest)
    row = iota((128, 128), 0)
    lane = iota((128, 128), 1)
    near = row // 32 == lane // 32
    row_imag = (row // 16) % 2 == 1
    lane_imag = (lane // 16) % 2 == 1
    flipped = jnp.concatenate(
        [columns[(n ^ 1) * 16 : (n ^ 1) * 16 + 16] for n in range(8)], axis=0
    )
    signed = jnp.where(row_imag[:, 0:8], -columns, columns)
    out = []
    for kz_hi in range(4):
        same = jnp.broadcast_to(signed[:, kz_hi : kz_hi + 1], (128, 128))
        other = jnp.broadcast_to(flipped[:, kz_hi : kz_hi + 1], (128, 128))
        factor = jnp.where(near, jnp.where(lane_imag, other, same), 0.0)
        product = factor * weight_ref[pl.ds(kz_hi * 128, 128), :]
        out.append(jnp.sum(product, axis=0, keepdims=True))
    tile = jnp.concatenate(out + out, axis=0) * (1.0 / (NZ * NX * NY))
    for step in range(32):
        out_ref[pl.ds(step * 8, 8), :] = tile


def scatter_groups_kernel(phase_ref, hi_ref, lo_ref, in_ref, out_ref):
    real = [None] * 16
    imag = [None] * 16
    for kz_hi in range(4):
        tiles = [in_ref[pl.ds(q * 64 + kz_hi, 16, stride=4), :] for q in range(4)]
        for kz_lo, tile in enumerate(exchange(tiles)):
            turned = times_j(tile)
            real[kz_lo * 4 + kz_hi] = tile * phase_ref[0] + turned * phase_ref[1]
            imag[kz_lo * 4 + kz_hi] = turned * phase_ref[0] - tile * phase_ref[1]
    real = three(hi_ref[...], lo_ref[...], jnp.concatenate(real + imag, axis=0))
    imag = times_j(real)
    cos, sin, flip = quarter_signs((128, 128))
    out_ref[0] = real
    out_ref[1] = cos * real + sin * imag
    out_ref[2] = flip * real
    out_ref[3] = cos * real - sin * imag


def twice_gelu(values):
    return values + values * lax.erf(values * np.float32(math.sqrt(0.5)))


ZB = 4
STEPS = LZ // ZB


def point_kernel(
    modes_ref, hi_ref, lo_ref, ytab_ref, label_ref, table_ref, wide1_ref, wide2_ref, bias2_ref,
    out_ref, planes_ref, pre_ref,
):
    step = pl.program_id(0)

    @pl.when(step == 0)
    def _():
        high_lane = (iota((128, 128), 1) // 8) % 2 == 1
        pair_tiles = []
        for c_hi in range(2):
            tiles = []
            for pair in range(2):
                even = modes_ref[2 * pair]
                odd = modes_ref[2 * pair + 1]
                if c_hi == 0:
                    tile = jnp.where(high_lane, pltpu.roll(odd, 8, 1), even)
                else:
                    tile = jnp.where(high_lane, odd, pltpu.roll(even, 120, 1))
                tiles.append(jnp.concatenate([tile, times_j(tile)], axis=0))
            full = three(hi_ref[...], lo_ref[...], jnp.concatenate(tiles, axis=1))
            full = full.astype(bf16).astype(f32)
            planes_ref[c_hi * 2] = full[:, 0:128]
            planes_ref[c_hi * 2 + 1] = full[:, 128:256]

    def finish(zi):
        hidden = twice_gelu(pre_ref[zi]).astype(bf16)
        bias2 = jnp.concatenate([bias2_ref[...]] * 2, axis=1)
        encoded = dot(wide2_ref[...], hidden) + bias2
        out_ref[:, zi] = encoded.reshape(16, 8, 256).astype(bf16)

    def begin():
        own = jnp.where(iota((16, 256), 0) % 8 == iota((16, 256), 1) % 8, 1.0, 0.0).astype(bf16)
        left = []
        for zi in range(ZB):
            base = pl.multiple_of((step * ZB + zi) * 8, 8)
            for x in range(LX):
                rows = [planes_ref[t, pl.ds(base + x, 8, stride=0), :] for t in range(4)]
                block = jnp.concatenate(
                    [jnp.concatenate(rows[0:2], axis=1), jnp.concatenate(rows[2:4], axis=1)],
                    axis=0,
                )
                left.append(block.astype(bf16) * own)
        return dot(jnp.concatenate(left, axis=0), ytab_ref[...])

    def expand(spatial, zi):
        low = table_ref[0:8, :]
        high = table_ref[8:16, :]
        ones = jnp.ones((16, 256), bf16)
        base = pl.multiple_of((step * ZB + zi) * 8, 8)
        point = []
        for x in range(LX):
            halves = []
            for half in range(2):
                label = label_ref[half, pl.ds(base + x, 8, stride=0), :]
                halves.append(
                    jnp.concatenate(
                        [
                            jnp.take_along_axis(low, label, axis=1),
                            jnp.take_along_axis(high, label, axis=1),
                        ],
                        axis=0,
                    )
                )
            point.append(jnp.concatenate(halves, axis=1))
        pointwise = jnp.concatenate(point, axis=0)
        activated = twice_gelu(spatial[zi * 128 : zi * 128 + 128] + pointwise).astype(bf16)
        pre_ref[zi] = dot(wide1_ref[:, 0:144], jnp.concatenate([activated, ones], axis=0))

    @pl.when(step == 0)
    def _():
        spatial = begin()
        for zi in range(ZB):
            expand(spatial, zi)

    @pl.when(jnp.logical_and(step > 0, step < STEPS))
    def _():
        spatial = begin()
        for zi in range(ZB):
            finish(zi)
            expand(spatial, zi)

    @pl.when(step == STEPS)
    def _():
        for zi in range(ZB):
            finish(zi)


def room(mib):
    return pltpu.CompilerParams(vmem_limit_bytes=mib * 1024 * 1024)


def vmem():
    return pl.BlockSpec(memory_space=pltpu.VMEM)


def shards(
    occupancy,
    embedding,
    spectral_weight,
    point_weight,
    point_bias,
    expand_weight,
    expand_bias,
    reduce_weight,
    reduce_bias,
):
    ytab = y_tables()
    z_hi, z_lo = split(z_tables())
    x_hi, x_lo = split(x_tables())
    constants = [
        ytab,
        z_hi.T.copy(),
        z_lo.T.copy(),
        x_hi.transpose(2, 0, 1).reshape(256, 256),
        x_lo.transpose(2, 0, 1).reshape(256, 256),
        x_hi.transpose(1, 0, 2).reshape(128, 512),
        x_lo.transpose(1, 0, 2).reshape(128, 512),
        z_hi,
        z_lo,
        y_lanes(ytab),
        pen_phases(),
    ]
    shape = jax.ShapeDtypeStruct
    made = pl.pallas_call(
        forward_kernel,
        out_shape=[
            shape((4, 128, 128), f32),
            shape((128, 128), f32),
            shape((512, 128), f32),
            shape((256, 256), bf16),
            shape((256, 256), bf16),
            shape((128, 512), bf16),
            shape((128, 512), bf16),
            shape((512, 256), bf16),
            shape((512, 256), bf16),
            shape((256, 256), bf16),
            shape((2, 512, 128), jnp.int32),
            shape((2, 16, 128), f32),
            shape((16, 128), f32),
            shape((512, 256), bf16),
            shape((128, 512), bf16),
            shape((128, 128), f32),
        ],
        in_specs=[pl.BlockSpec(memory_space=pltpu.HBM)] * 20,
        out_specs=[vmem()] * 16,
        scratch_shapes=[
            pltpu.VMEM((ROWS, NY), jnp.int32),
            pltpu.VMEM((32, 256), bf16),
            pltpu.VMEM((256, 512), bf16),
            pltpu.VMEM((256, 512), bf16),
            pltpu.VMEM((64, 128), f32),
            pltpu.VMEM((NCLASS, CH), f32),
            pltpu.VMEM((512, 16), f32),
            pltpu.VMEM((CH, CH), f32),
            pltpu.VMEM((1, CH), f32),
            pltpu.VMEM((CH, HIDDEN), bf16),
            pltpu.VMEM((1, HIDDEN), f32),
            pltpu.VMEM((CH, HIDDEN), bf16),
            pltpu.VMEM((1, CH), f32),
            pltpu.VMEM((ROWS, NY), bf16),
            pltpu.VMEM((4, 512, 128), f32),
            pltpu.SemaphoreType.DMA((20,)),
        ],
        compiler_params=room(16),
        name="forward",
    )(
        occupancy.reshape(ROWS, NY),
        *[jnp.asarray(c) for c in constants],
        embedding,
        spectral_weight.reshape(512, 16),
        point_weight,
        point_bias.reshape(1, CH),
        expand_weight,
        expand_bias.reshape(1, HIDDEN),
        reduce_weight.T,
        reduce_bias.reshape(1, CH),
    )
    partial, wide, weight, xi_hi, xi_lo, xo_hi, xo_lo = made[:7]
    z_hi, z_lo, ylane, labels, phases, table, wide1, wide2, bias2 = made[7:]
    partial = lax.all_to_all(partial, "grp", 0, 0, tiled=True)
    chunks = pl.pallas_call(
        gather_groups_kernel,
        out_shape=shape((256, 128), f32),
        in_specs=[vmem()] * 4,
        out_specs=vmem(),
        compiler_params=room(8),
        name="gather_groups",
    )(phases, xi_hi, xi_lo, partial)
    chunks = lax.all_to_all(chunks.reshape(64, 4, 128), "pen", 0, 0, tiled=True)
    mixed = pl.pallas_call(
        mix_kernel,
        out_shape=shape((256, 128), f32),
        in_specs=[vmem()] * 3,
        out_specs=vmem(),
        compiler_params=room(8),
        name="mix",
    )(chunks.reshape(256, 128), weight, wide)
    mixed = lax.all_to_all(mixed.reshape(64, 4, 128), "pen", 0, 0, tiled=True)
    modes = pl.pallas_call(
        scatter_groups_kernel,
        out_shape=shape((4, 128, 128), f32),
        in_specs=[vmem()] * 4,
        out_specs=vmem(),
        compiler_params=room(8),
        name="scatter_groups",
    )(phases, xo_hi, xo_lo, mixed.reshape(256, 128))
    modes = lax.all_to_all(modes, "grp", 0, 0, tiled=True)
    return pl.pallas_call(
        point_kernel,
        out_shape=shape((CH, LZ, LX, NY), bf16),
        grid=(STEPS + 1,),
        in_specs=[vmem()] * 9,
        out_specs=pl.BlockSpec((CH, ZB, LX, NY), lambda i: (0, jnp.maximum(i - 1, 0), 0, 0)),
        scratch_shapes=[
            pltpu.VMEM((4, 512, 128), f32),
            pltpu.VMEM((ZB, 512, 256), f32),
        ],
        compiler_params=room(24),
        name="point",
    )(modes, z_hi, z_lo, ylane, labels, table, wide1, wide2, bias2)


def solution(mesh):
    return jax.shard_map(
        shards,
        mesh=mesh,
        in_specs=(
            P("grp", "pen", None),
            P(),
            P(("grp", "pen"), None, None, None, None),
            P(),
            P(),
            P(),
            P(),
            P(),
            P(),
        ),
        out_specs=P(None, "grp", "pen", None),
        check_vma=False,
    )
```

```python
import functools
import math

import jax
import jax.numpy as jnp
import ml_dtypes
import numpy as np
from jax import lax
from jax.experimental import pallas as pl
from jax.experimental.pallas import tpu as pltpu
from jax.sharding import PartitionSpec as P

NZ = 256
NX = 512
NY = 256
CH = 16
MODES = 16
NCLASS = 12
HIDDEN = 64
LZ = 64
LX = 8
ROWS = LZ * LX

highest = lax.Precision.HIGHEST
f32 = jnp.float32
bf16 = jnp.bfloat16
FREQ = np.where(np.arange(MODES) < 8, np.arange(MODES), np.arange(MODES) - MODES)


def split(values):
    hi = values.astype(ml_dtypes.bfloat16)
    lo = (values - hi.astype(np.float64)).astype(ml_dtypes.bfloat16)
    return hi, lo


def y_tables():
    product = np.remainder(FREQ[:, None] * np.arange(NY)[None, :], NY)
    angles = product.astype(np.float32) * np.float32(2.0 * math.pi / NY)
    cos = np.cos(angles).astype(ml_dtypes.bfloat16)
    sin = np.sin(angles).astype(ml_dtypes.bfloat16)
    return np.stack([cos, -sin], axis=1).reshape(2 * MODES, NY)


def z_tables():
    angles = 2.0 * np.pi * np.remainder(FREQ[None, :] * np.arange(LZ)[:, None], NZ) / NZ
    table = np.zeros((LZ, LX, 2, LX, MODES))
    for x in range(LX):
        table[:, x, 0, x] = np.cos(angles)
        table[:, x, 1, x] = np.sin(angles)
    return table.reshape(ROWS, 2 * LX * MODES)


def x_tables():
    angles = 2.0 * np.pi * np.remainder(FREQ[None, :] * np.arange(LX)[:, None], NX) / NX
    table = np.zeros((2, LX, MODES, MODES, MODES))
    for kz in range(MODES):
        table[0, :, kz, :, kz] = np.cos(angles)
        table[1, :, kz, :, kz] = np.sin(angles)
    table = table.reshape(2, LX * MODES, MODES, 4, 4)
    return table.transpose(0, 1, 4, 3, 2).reshape(2, LX * MODES, MODES * MODES)


def y_lanes(ytab):
    table = ytab.reshape(2, 2, 4, 2, NY)
    table = np.moveaxis(table, (0, 1, 2, 3), (0, 3, 1, 2))
    return np.repeat(table.reshape(2 * MODES, NY), 8, axis=0)


def pen_phases():
    turn = np.remainder(np.arange(64)[:, None] * FREQ[None, :], 64)
    angles = 2.0 * np.pi * turn / 64
    table = np.zeros((64, 128), np.float32)
    table[:, 0:16] = np.cos(angles)
    table[:, 16:32] = np.sin(angles)
    return table


def iota(shape, axis):
    return lax.broadcasted_iota(jnp.int32, shape, axis)


def times_j(tile):
    imag_lane = (iota(tile.shape, 1) // 16) % 2 == 1
    return jnp.where(imag_lane, pltpu.roll(tile, 16, 1), -pltpu.roll(tile, 112, 1))


def exchange(tiles):
    block = iota(tiles[0].shape, 1) // 32
    out = []
    for i in range(4):
        best = tiles[i]
        for j in range(4):
            if j != i:
                best = jnp.where(block == j, pltpu.roll(tiles[j], 32 * (j - i) % 128, 1), best)
        out.append(best)
    return out


def quarter_signs(shape):
    quarter = iota(shape, 0) % 4
    cos = jnp.where(quarter == 0, 1.0, jnp.where(quarter == 2, -1.0, 0.0))
    sin = jnp.where(quarter == 1, 1.0, jnp.where(quarter == 3, -1.0, 0.0))
    flip = jnp.where(quarter % 2 == 0, 1.0, -1.0)
    return cos, sin, flip


def to_parts(values):
    hi = values.astype(bf16)
    lo = (values - hi.astype(f32)).astype(bf16)
    return hi, lo


def dot(left, right, dims=((1,), (0,)), precision=None):
    return lax.dot_general(
        left, right, (dims, ((), ())), precision=precision, preferred_element_type=f32
    )


def three(hi, lo, right):
    right_hi, right_lo = to_parts(right)
    return dot(hi, right_hi) + dot(hi, right_lo) + dot(lo, right_hi)


def forward_kernel(
    occ, ytab, zt_hi, zt_lo, xi_hi, xi_lo, xo_hi, xo_lo, z_hi, z_lo, ylane, phase, emb, weight,
    pw, pb, w1, b1, w2, b2,
    out_ref, wide_ref, rep_ref, xi_hi_out, xi_lo_out, xo_hi_out, xo_lo_out, z_hi_out, z_lo_out,
    ylane_out, label_ref, phase_out, table_ref, wide1_ref, wide2_ref, bias2_ref,
    occ_v, ytab_v, zt_hi_v, zt_lo_v, phase_v, emb_v, weight_v, pw_v, pb_v, w1_v, b1_v, w2_v, b2_v,
    small_ref, rows_ref, sems,
):
    pairs = [
        (occ, occ_v), (ytab, ytab_v), (zt_hi, zt_hi_v), (zt_lo, zt_lo_v), (emb, emb_v),
        (weight, weight_v), (pw, pw_v), (pb, pb_v), (w1, w1_v), (b1, b1_v), (w2, w2_v), (b2, b2_v),
        (phase, phase_v), (xi_hi, xi_hi_out), (xi_lo, xi_lo_out), (xo_hi, xo_hi_out),
        (xo_lo, xo_lo_out), (z_hi, z_hi_out), (z_lo, z_lo_out), (ylane, ylane_out),
    ]
    copies = [pltpu.make_async_copy(a, b, sems.at[i]) for i, (a, b) in enumerate(pairs)]
    for copy in copies:
        copy.start()
    rows_ref[...] = jnp.zeros_like(rows_ref)
    copies[0].wait()
    copies[1].wait()
    for half in range(2):
        piece = occ_v[:, half * 128 : (half + 1) * 128]
        label_ref[half] = piece
        small_ref[:, half * 128 : (half + 1) * 128] = piece.astype(f32).astype(bf16)
    for label in range(NCLASS):
        same = small_ref[...] == jnp.array(label, bf16)
        hot = jnp.where(same, jnp.array(1.0, bf16), jnp.array(0.0, bf16))
        part = dot(ytab_v[...], hot, ((1,), (1,)))
        for quarter in range(4):
            rows_ref[quarter, pl.ds(label, 32, stride=16), :] = part[
                :, quarter * 128 : (quarter + 1) * 128
            ]
    for copy in copies[2:]:
        copy.wait()
    nt = ((1,), (1,))
    for pair in range(2):
        block = [rows_ref[quarter, pl.ds(pair * 256, 256), :] for quarter in range(4)]
        block_hi, block_lo = to_parts(jnp.concatenate(block, axis=1))
        full = (
            dot(zt_hi_v[...], block_hi, nt)
            + dot(zt_hi_v[...], block_lo, nt)
            + dot(zt_lo_v[...], block_hi, nt)
        )
        for half in range(2):
            tile = full[:, half * 128 : (half + 1) * 128]
            out_ref[pair * 2 + half] = tile[:128] - times_j(tile[128:])

    left = jnp.where(iota((128, NCLASS), 0) % 16 == iota((128, NCLASS), 1), 1.0, 0.0).astype(f32)
    right = jnp.where(iota((16, 128), 1) % 16 == iota((16, 128), 0), 1.0, 0.0).astype(f32)
    lifted = dot(left, emb_v[...], precision=highest)
    wide = dot(right, lifted, ((0,), (1,)), highest)
    wide_ref[...] = jnp.where(
        iota((128, 128), 0) // 16 == iota((128, 128), 1) // 16, wide, 0.0
    )
    rep_ref[...] = jnp.concatenate([weight_v[...]] * 8, axis=1)
    row = phase_v[pl.ds(lax.axis_index("pen"), 16, stride=0), :]
    for half in range(2):
        pick = iota((16, 128), 1) == iota((16, 128), 0) + 16 * half
        column = jnp.sum(jnp.where(pick, row, 0.0), axis=1, keepdims=True)
        phase_out[half] = jnp.broadcast_to(column, (16, 128))

    table = dot(pw_v[...], emb_v[...], ((0,), (1,)), highest)
    spread = jnp.where(
        iota((NCLASS, 128), 0) == iota((NCLASS, 128), 1), 1.0, 0.0
    ).astype(f32)
    eye = iota((16, 16), 0) == iota((16, 16), 1)
    bias = jnp.sum(jnp.where(eye, pb_v[...], 0.0), axis=1, keepdims=True)
    table_ref[...] = dot(table, spread, precision=highest) + bias
    r1 = jnp.where(iota((64, 64), 0) == iota((64, 64), 1), 1.0, 0.0)
    r2 = jnp.where(iota((16, 128), 1) % 16 == iota((16, 128), 0), 0.5, 0.0).astype(bf16)
    full1 = dot(dot(r1.astype(bf16), w1_v[...], ((1,), (1,))).astype(bf16), r2)
    col1 = jnp.broadcast_to(jnp.sum(r1 * b1_v[...], axis=1, keepdims=True), (64, 128))
    first = col1.astype(bf16).astype(f32)
    second = (col1 - first).astype(bf16).astype(f32)
    third = col1 - first - second
    lane = iota((64, 128), 1)
    extra = jnp.where(
        lane == 0, first, jnp.where(lane == 1, second, jnp.where(lane == 2, third, 0.0))
    ).astype(bf16)
    for x in range(LX):
        wide1_ref[x * 64 : x * 64 + 64, 0:128] = jnp.where(lane // 16 == x, full1, 0.0).astype(bf16)
        wide1_ref[x * 64 : x * 64 + 64, 128:256] = extra
    r3 = jnp.where(iota((128, 16), 0) // 8 == iota((128, 16), 1), 1.0, 0.0)
    r4 = jnp.where(iota((64, 128), 1) % 64 == iota((64, 128), 0), 0.5, 0.0).astype(bf16)
    full2 = dot(dot(r3.astype(bf16), w2_v[...]).astype(bf16), r4)
    x_row = iota((128, 128), 0) % 8
    x_lane = iota((128, 128), 1) // 64
    for tile in range(4):
        wide2_ref[:, tile * 128 : tile * 128 + 128] = jnp.where(
            x_row == x_lane + 2 * tile, full2, 0.0
        ).astype(bf16)
    col2 = jnp.sum(r3 * b2_v[...], axis=1, keepdims=True)
    bias2_ref[...] = jnp.broadcast_to(col2, (128, 128))


def gather_groups_kernel(phase_ref, hi_ref, lo_ref, in_ref, out_ref):
    cos, sin, flip = quarter_signs((128, 128))
    real = in_ref[0] + flip * in_ref[2] + cos * (in_ref[1] + in_ref[3])
    imag = sin * (in_ref[3] - in_ref[1])
    real = real + times_j(imag)
    both = three(hi_ref[...], lo_ref[...], jnp.concatenate([real, -times_j(real)], axis=0))
    turned = times_j(both)
    for kz_hi in range(4):
        tiles = []
        for kz_lo in range(4):
            rows = slice((kz_lo * 4 + kz_hi) * 16, (kz_lo * 4 + kz_hi) * 16 + 16)
            tiles.append(both[rows] * phase_ref[0] - turned[rows] * phase_ref[1])
        for q, tile in enumerate(exchange(tiles)):
            out_ref[pl.ds(q * 64 + kz_hi, 16, stride=4), :] = tile


def mix_kernel(in_ref, weight_ref, wide_ref, out_ref):
    parts = [in_ref[pl.ds(step * 8, 8), :] for step in range(32)]
    while len(parts) > 1:
        parts = [a + b for a, b in zip(parts[0::2], parts[1::2])]
    total = parts[0] + pltpu.roll(parts[0], 4, 0)
    columns = dot(wide_ref[...], total, ((1,), (1,)), highest)
    row = iota((128, 128), 0)
    lane = iota((128, 128), 1)
    near = row // 32 == lane // 32
    row_imag = (row // 16) % 2 == 1
    lane_imag = (lane // 16) % 2 == 1
    flipped = jnp.concatenate(
        [columns[(n ^ 1) * 16 : (n ^ 1) * 16 + 16] for n in range(8)], axis=0
    )
    signed = jnp.where(row_imag[:, 0:8], -columns, columns)
    out = []
    for kz_hi in range(4):
        same = jnp.broadcast_to(signed[:, kz_hi : kz_hi + 1], (128, 128))
        other = jnp.broadcast_to(flipped[:, kz_hi : kz_hi + 1], (128, 128))
        factor = jnp.where(near, jnp.where(lane_imag, other, same), 0.0)
        product = factor * weight_ref[pl.ds(kz_hi * 128, 128), :]
        out.append(jnp.sum(product, axis=0, keepdims=True))
    tile = jnp.concatenate(out + out, axis=0) * (1.0 / (NZ * NX * NY))
    for step in range(32):
        out_ref[pl.ds(step * 8, 8), :] = tile


def scatter_groups_kernel(phase_ref, hi_ref, lo_ref, in_ref, out_ref):
    real = [None] * 16
    imag = [None] * 16
    for kz_hi in range(4):
        tiles = [in_ref[pl.ds(q * 64 + kz_hi, 16, stride=4), :] for q in range(4)]
        for kz_lo, tile in enumerate(exchange(tiles)):
            turned = times_j(tile)
            real[kz_lo * 4 + kz_hi] = tile * phase_ref[0] + turned * phase_ref[1]
            imag[kz_lo * 4 + kz_hi] = turned * phase_ref[0] - tile * phase_ref[1]
    real = three(hi_ref[...], lo_ref[...], jnp.concatenate(real + imag, axis=0))
    imag = times_j(real)
    cos, sin, flip = quarter_signs((128, 128))
    out_ref[0] = real
    out_ref[1] = cos * real + sin * imag
    out_ref[2] = flip * real
    out_ref[3] = cos * real - sin * imag


def twice_gelu(values):
    return values + values * lax.erf(values * np.float32(math.sqrt(0.5)))


ZB = 4
STEPS = LZ // ZB


def point_kernel(
    modes_ref, hi_ref, lo_ref, ytab_ref, label_ref, table_ref, wide1_ref, wide2_ref, bias2_ref,
    out_ref, planes_ref, pre_ref,
):
    step = pl.program_id(0)

    @pl.when(step == 0)
    def _():
        high_lane = (iota((128, 128), 1) // 8) % 2 == 1
        pair_tiles = []
        for c_hi in range(2):
            tiles = []
            for pair in range(2):
                even = modes_ref[2 * pair]
                odd = modes_ref[2 * pair + 1]
                if c_hi == 0:
                    tile = jnp.where(high_lane, pltpu.roll(odd, 8, 1), even)
                else:
                    tile = jnp.where(high_lane, odd, pltpu.roll(even, 120, 1))
                tiles.append(jnp.concatenate([tile, times_j(tile)], axis=0))
            full = three(hi_ref[...], lo_ref[...], jnp.concatenate(tiles, axis=1))
            full = full.astype(bf16).astype(f32)
            planes_ref[c_hi * 2] = full[:, 0:128]
            planes_ref[c_hi * 2 + 1] = full[:, 128:256]

    def finish(zi):
        hidden = twice_gelu(pre_ref[zi]).astype(bf16)
        bias2 = jnp.concatenate([bias2_ref[...]] * 2, axis=1)
        encoded = dot(wide2_ref[...], hidden) + bias2
        out_ref[:, zi] = encoded.reshape(16, 8, 256).astype(bf16)

    def begin():
        own = jnp.where(iota((16, 256), 0) % 8 == iota((16, 256), 1) % 8, 1.0, 0.0).astype(bf16)
        left = []
        for zi in range(ZB):
            base = pl.multiple_of((step * ZB + zi) * 8, 8)
            for x in range(LX):
                rows = [planes_ref[t, pl.ds(base + x, 8, stride=0), :] for t in range(4)]
                block = jnp.concatenate(
                    [jnp.concatenate(rows[0:2], axis=1), jnp.concatenate(rows[2:4], axis=1)],
                    axis=0,
                )
                left.append(block.astype(bf16) * own)
        return dot(jnp.concatenate(left, axis=0), ytab_ref[...])

    def expand(spatial, zi):
        low = table_ref[0:8, :]
        high = table_ref[8:16, :]
        ones = jnp.ones((16, 256), bf16)
        base = pl.multiple_of((step * ZB + zi) * 8, 8)
        point = []
        for x in range(LX):
            halves = []
            for half in range(2):
                label = label_ref[half, pl.ds(base + x, 8, stride=0), :]
                halves.append(
                    jnp.concatenate(
                        [
                            jnp.take_along_axis(low, label, axis=1),
                            jnp.take_along_axis(high, label, axis=1),
                        ],
                        axis=0,
                    )
                )
            point.append(jnp.concatenate(halves, axis=1))
        pointwise = jnp.concatenate(point, axis=0)
        activated = twice_gelu(spatial[zi * 128 : zi * 128 + 128] + pointwise).astype(bf16)
        pre_ref[zi] = dot(wide1_ref[:, 0:144], jnp.concatenate([activated, ones], axis=0))

    @pl.when(step == 0)
    def _():
        spatial = begin()
        for zi in range(ZB):
            expand(spatial, zi)

    @pl.when(jnp.logical_and(step > 0, step < STEPS))
    def _():
        spatial = begin()
        for zi in range(ZB):
            finish(zi)
            expand(spatial, zi)

    @pl.when(step == STEPS)
    def _():
        for zi in range(ZB):
            finish(zi)


def room(mib):
    return pltpu.CompilerParams(vmem_limit_bytes=mib * 1024 * 1024)


def vmem():
    return pl.BlockSpec(memory_space=pltpu.VMEM)


def shards(
    occupancy,
    embedding,
    spectral_weight,
    point_weight,
    point_bias,
    expand_weight,
    expand_bias,
    reduce_weight,
    reduce_bias,
):
    ytab = y_tables()
    z_hi, z_lo = split(z_tables())
    x_hi, x_lo = split(x_tables())
    constants = [
        ytab,
        z_hi.T.copy(),
        z_lo.T.copy(),
        x_hi.transpose(2, 0, 1).reshape(256, 256),
        x_lo.transpose(2, 0, 1).reshape(256, 256),
        x_hi.transpose(1, 0, 2).reshape(128, 512),
        x_lo.transpose(1, 0, 2).reshape(128, 512),
        z_hi,
        z_lo,
        y_lanes(ytab),
        pen_phases(),
    ]
    sources = [
        occupancy.reshape(ROWS, NY),
        *[jnp.asarray(c) for c in constants],
        embedding,
        spectral_weight.reshape(512, 16),
        point_weight,
        point_bias.reshape(1, CH),
        expand_weight,
        expand_bias.reshape(1, HIDDEN),
        reduce_weight.T,
        reduce_bias.reshape(1, CH),
    ]
    shape = jax.ShapeDtypeStruct
    made = pl.pallas_call(
        forward_kernel,
        out_shape=[
            shape((4, 128, 128), f32),
            shape((128, 128), f32),
            shape((512, 128), f32),
            shape((256, 256), bf16),
            shape((256, 256), bf16),
            shape((128, 512), bf16),
            shape((128, 512), bf16),
            shape((512, 256), bf16),
            shape((512, 256), bf16),
            shape((256, 256), bf16),
            shape((2, 512, 128), jnp.int32),
            shape((2, 16, 128), f32),
            shape((16, 128), f32),
            shape((512, 256), bf16),
            shape((128, 512), bf16),
            shape((128, 128), f32),
        ],
        in_specs=[pl.BlockSpec(memory_space=pltpu.HBM)] * 20,
        out_specs=[vmem()] * 16,
        scratch_shapes=[
            pltpu.VMEM((ROWS, NY), jnp.int32),
            pltpu.VMEM((32, 256), bf16),
            pltpu.VMEM((256, 512), bf16),
            pltpu.VMEM((256, 512), bf16),
            pltpu.VMEM((64, 128), f32),
            pltpu.VMEM((NCLASS, CH), f32),
            pltpu.VMEM((512, 16), f32),
            pltpu.VMEM((CH, CH), f32),
            pltpu.VMEM((1, CH), f32),
            pltpu.VMEM((CH, HIDDEN), bf16),
            pltpu.VMEM((1, HIDDEN), f32),
            pltpu.VMEM((CH, HIDDEN), bf16),
            pltpu.VMEM((1, CH), f32),
            pltpu.VMEM((ROWS, NY), bf16),
            pltpu.VMEM((4, 512, 128), f32),
            pltpu.SemaphoreType.DMA((20,)),
        ],
        compiler_params=room(16),
        name="forward",
    )(*[pltpu.with_memory_space_constraint(value, pltpu.HBM) for value in sources])
    partial, wide, weight, xi_hi, xi_lo, xo_hi, xo_lo = made[:7]
    z_hi, z_lo, ylane, labels, phases, table, wide1, wide2, bias2 = made[7:]
    partial = lax.all_to_all(partial, "grp", 0, 0, tiled=True)
    chunks = pl.pallas_call(
        gather_groups_kernel,
        out_shape=shape((256, 128), f32),
        in_specs=[vmem()] * 4,
        out_specs=vmem(),
        compiler_params=room(8),
        name="gather_groups",
    )(phases, xi_hi, xi_lo, partial)
    chunks = lax.all_to_all(chunks.reshape(64, 4, 128), "pen", 0, 0, tiled=True)
    mixed = pl.pallas_call(
        mix_kernel,
        out_shape=shape((256, 128), f32),
        in_specs=[vmem()] * 3,
        out_specs=vmem(),
        compiler_params=room(8),
        name="mix",
    )(chunks.reshape(256, 128), weight, wide)
    mixed = lax.all_to_all(mixed.reshape(64, 4, 128), "pen", 0, 0, tiled=True)
    modes = pl.pallas_call(
        scatter_groups_kernel,
        out_shape=shape((4, 128, 128), f32),
        in_specs=[vmem()] * 4,
        out_specs=vmem(),
        compiler_params=room(8),
        name="scatter_groups",
    )(phases, xo_hi, xo_lo, mixed.reshape(256, 128))
    modes = lax.all_to_all(modes, "grp", 0, 0, tiled=True)
    return pl.pallas_call(
        point_kernel,
        out_shape=shape((CH, LZ, LX, NY), bf16),
        grid=(STEPS + 1,),
        in_specs=[vmem()] * 9,
        out_specs=pl.BlockSpec((CH, ZB, LX, NY), lambda i: (0, jnp.maximum(i - 1, 0), 0, 0)),
        scratch_shapes=[
            pltpu.VMEM((4, 512, 128), f32),
            pltpu.VMEM((ZB, 512, 256), f32),
        ],
        compiler_params=room(24),
        name="point",
    )(modes, z_hi, z_lo, ylane, labels, table, wide1, wide2, bias2)


def solution(mesh):
    return jax.shard_map(
        shards,
        mesh=mesh,
        in_specs=(
            P("grp", "pen", None),
            P(),
            P(("grp", "pen"), None, None, None, None),
            P(),
            P(),
            P(),
            P(),
            P(),
            P(),
        ),
        out_specs=P(None, "grp", "pen", None),
        check_vma=False,
    )
```

```python
import functools
import math

import jax
import jax.numpy as jnp
import ml_dtypes
import numpy as np
from jax import lax
from jax.experimental import pallas as pl
from jax.experimental.pallas import tpu as pltpu
from jax.sharding import PartitionSpec as P

NZ = 256
NX = 512
NY = 256
CH = 16
MODES = 16
NCLASS = 12
HIDDEN = 64
LZ = 64
LX = 8
ROWS = LZ * LX

highest = lax.Precision.HIGHEST
f32 = jnp.float32
bf16 = jnp.bfloat16
FREQ = np.where(np.arange(MODES) < 8, np.arange(MODES), np.arange(MODES) - MODES)


def split(values):
    hi = values.astype(ml_dtypes.bfloat16)
    lo = (values - hi.astype(np.float64)).astype(ml_dtypes.bfloat16)
    return hi, lo


def y_tables():
    product = np.remainder(FREQ[:, None] * np.arange(NY)[None, :], NY)
    angles = product.astype(np.float32) * np.float32(2.0 * math.pi / NY)
    cos = np.cos(angles).astype(ml_dtypes.bfloat16)
    sin = np.sin(angles).astype(ml_dtypes.bfloat16)
    return np.stack([cos, -sin], axis=1).reshape(2 * MODES, NY)


def z_tables():
    angles = 2.0 * np.pi * np.remainder(FREQ[None, :] * np.arange(LZ)[:, None], NZ) / NZ
    table = np.zeros((LZ, LX, 2, LX, MODES))
    for x in range(LX):
        table[:, x, 0, x] = np.cos(angles)
        table[:, x, 1, x] = np.sin(angles)
    return table.reshape(ROWS, 2 * LX * MODES)


def x_tables():
    angles = 2.0 * np.pi * np.remainder(FREQ[None, :] * np.arange(LX)[:, None], NX) / NX
    table = np.zeros((2, LX, MODES, MODES, MODES))
    for kz in range(MODES):
        table[0, :, kz, :, kz] = np.cos(angles)
        table[1, :, kz, :, kz] = np.sin(angles)
    table = table.reshape(2, LX * MODES, MODES, 4, 4)
    return table.transpose(0, 1, 4, 3, 2).reshape(2, LX * MODES, MODES * MODES)


def y_lanes(ytab):
    table = ytab.reshape(2, 2, 4, 2, NY)
    table = np.moveaxis(table, (0, 1, 2, 3), (0, 3, 1, 2))
    return np.repeat(table.reshape(2 * MODES, NY), 8, axis=0)


def pen_phases():
    turn = np.remainder(np.arange(64)[:, None] * FREQ[None, :], 64)
    angles = 2.0 * np.pi * turn / 64
    table = np.zeros((64, 128), np.float32)
    table[:, 0:16] = np.cos(angles)
    table[:, 16:32] = np.sin(angles)
    return table


def iota(shape, axis):
    return lax.broadcasted_iota(jnp.int32, shape, axis)


def times_j(tile):
    imag_lane = (iota(tile.shape, 1) // 16) % 2 == 1
    return jnp.where(imag_lane, pltpu.roll(tile, 16, 1), -pltpu.roll(tile, 112, 1))


def exchange(tiles):
    block = iota(tiles[0].shape, 1) // 32
    out = []
    for i in range(4):
        best = tiles[i]
        for j in range(4):
            if j != i:
                best = jnp.where(block == j, pltpu.roll(tiles[j], 32 * (j - i) % 128, 1), best)
        out.append(best)
    return out


def quarter_signs(shape):
    quarter = iota(shape, 0) % 4
    cos = jnp.where(quarter == 0, 1.0, jnp.where(quarter == 2, -1.0, 0.0))
    sin = jnp.where(quarter == 1, 1.0, jnp.where(quarter == 3, -1.0, 0.0))
    flip = jnp.where(quarter % 2 == 0, 1.0, -1.0)
    return cos, sin, flip


def to_parts(values):
    hi = values.astype(bf16)
    lo = (values - hi.astype(f32)).astype(bf16)
    return hi, lo


def dot(left, right, dims=((1,), (0,)), precision=None):
    return lax.dot_general(
        left, right, (dims, ((), ())), precision=precision, preferred_element_type=f32
    )


def three(hi, lo, right):
    right_hi, right_lo = to_parts(right)
    return dot(hi, right_hi) + dot(hi, right_lo) + dot(lo, right_hi)


def forward_kernel(
    occ, ytab, zt_hi, zt_lo, out_ref, occ_v, ytab_v, zt_hi_v, zt_lo_v, small_ref, rows_ref, sems
):
    pairs = [(occ, occ_v), (ytab, ytab_v), (zt_hi, zt_hi_v), (zt_lo, zt_lo_v)]
    copies = [pltpu.make_async_copy(a, b, sems.at[i]) for i, (a, b) in enumerate(pairs)]
    for copy in copies:
        copy.start()
    for label in range(NCLASS, 16):
        for quarter in range(4):
            rows_ref[quarter, pl.ds(label, 32, stride=16), :] = jnp.zeros((32, 128), f32)
    copies[0].wait()
    copies[1].wait()
    small_ref[...] = occ_v[...].astype(f32).astype(bf16)
    for label in range(NCLASS):
        same = small_ref[...] == jnp.array(label, bf16)
        hot = jnp.where(same, jnp.array(1.0, bf16), jnp.array(0.0, bf16))
        part = dot(ytab_v[...], hot, ((1,), (1,)))
        for quarter in range(4):
            rows_ref[quarter, pl.ds(label, 32, stride=16), :] = part[
                :, quarter * 128 : (quarter + 1) * 128
            ]
    copies[2].wait()
    copies[3].wait()
    nt = ((1,), (1,))
    for pair in range(2):
        block = [rows_ref[quarter, pl.ds(pair * 256, 256), :] for quarter in range(4)]
        block_hi, block_lo = to_parts(jnp.concatenate(block, axis=1))
        full = (
            dot(zt_hi_v[...], block_hi, nt)
            + dot(zt_hi_v[...], block_lo, nt)
            + dot(zt_lo_v[...], block_hi, nt)
        )
        for half in range(2):
            tile = full[:, half * 128 : (half + 1) * 128]
            out_ref[pair * 2 + half] = tile[:128] - times_j(tile[128:])


def prepare_kernel(
    occ, xi_hi, xi_lo, xo_hi, xo_lo, z_hi, z_lo, ylane, phase, emb, weight, pw, pb, w1, b1, w2, b2,
    wide_ref, rep_ref, xi_hi_out, xi_lo_out, xo_hi_out, xo_lo_out, z_hi_out, z_lo_out,
    ylane_out, label_ref, phase_out, table_ref, wide1_ref, wide2_ref, bias2_ref,
    occ_v, phase_v, emb_v, weight_v, pw_v, pb_v, w1_v, b1_v, w2_v, b2_v, sems,
):
    pairs = [
        (occ, occ_v), (emb, emb_v), (weight, weight_v), (pw, pw_v), (pb, pb_v), (w1, w1_v),
        (b1, b1_v), (w2, w2_v), (b2, b2_v), (phase, phase_v), (xi_hi, xi_hi_out),
        (xi_lo, xi_lo_out), (xo_hi, xo_hi_out), (xo_lo, xo_lo_out), (z_hi, z_hi_out),
        (z_lo, z_lo_out), (ylane, ylane_out),
    ]
    copies = [pltpu.make_async_copy(a, b, sems.at[i]) for i, (a, b) in enumerate(pairs)]
    for copy in copies:
        copy.start()
    for copy in copies:
        copy.wait()
    for half in range(2):
        label_ref[half] = occ_v[:, half * 128 : (half + 1) * 128]
    left = jnp.where(iota((128, NCLASS), 0) % 16 == iota((128, NCLASS), 1), 1.0, 0.0).astype(f32)
    right = jnp.where(iota((16, 128), 1) % 16 == iota((16, 128), 0), 1.0, 0.0).astype(f32)
    lifted = dot(left, emb_v[...], precision=highest)
    wide = dot(right, lifted, ((0,), (1,)), highest)
    wide_ref[...] = jnp.where(
        iota((128, 128), 0) // 16 == iota((128, 128), 1) // 16, wide, 0.0
    )
    rep_ref[...] = jnp.concatenate([weight_v[...]] * 8, axis=1)
    row = phase_v[pl.ds(lax.axis_index("pen"), 16, stride=0), :]
    for half in range(2):
        pick = iota((16, 128), 1) == iota((16, 128), 0) + 16 * half
        column = jnp.sum(jnp.where(pick, row, 0.0), axis=1, keepdims=True)
        phase_out[half] = jnp.broadcast_to(column, (16, 128))

    table = dot(pw_v[...], emb_v[...], ((0,), (1,)), highest)
    spread = jnp.where(
        iota((NCLASS, 128), 0) == iota((NCLASS, 128), 1), 1.0, 0.0
    ).astype(f32)
    eye = iota((16, 16), 0) == iota((16, 16), 1)
    bias = jnp.sum(jnp.where(eye, pb_v[...], 0.0), axis=1, keepdims=True)
    table_ref[...] = dot(table, spread, precision=highest) + bias
    r1 = jnp.where(iota((64, 64), 0) == iota((64, 64), 1), 1.0, 0.0)
    r2 = jnp.where(iota((16, 128), 1) % 16 == iota((16, 128), 0), 0.5, 0.0).astype(bf16)
    full1 = dot(dot(r1.astype(bf16), w1_v[...], ((1,), (1,))).astype(bf16), r2)
    col1 = jnp.broadcast_to(jnp.sum(r1 * b1_v[...], axis=1, keepdims=True), (64, 128))
    first = col1.astype(bf16).astype(f32)
    second = (col1 - first).astype(bf16).astype(f32)
    third = col1 - first - second
    lane = iota((64, 128), 1)
    extra = jnp.where(
        lane == 0, first, jnp.where(lane == 1, second, jnp.where(lane == 2, third, 0.0))
    ).astype(bf16)
    for x in range(LX):
        wide1_ref[x * 64 : x * 64 + 64, 0:128] = jnp.where(lane // 16 == x, full1, 0.0).astype(bf16)
        wide1_ref[x * 64 : x * 64 + 64, 128:256] = extra
    r3 = jnp.where(iota((128, 16), 0) // 8 == iota((128, 16), 1), 1.0, 0.0)
    r4 = jnp.where(iota((64, 128), 1) % 64 == iota((64, 128), 0), 0.5, 0.0).astype(bf16)
    full2 = dot(dot(r3.astype(bf16), w2_v[...]).astype(bf16), r4)
    x_row = iota((128, 128), 0) % 8
    x_lane = iota((128, 128), 1) // 64
    for tile in range(4):
        wide2_ref[:, tile * 128 : tile * 128 + 128] = jnp.where(
            x_row == x_lane + 2 * tile, full2, 0.0
        ).astype(bf16)
    col2 = jnp.sum(r3 * b2_v[...], axis=1, keepdims=True)
    bias2_ref[...] = jnp.broadcast_to(col2, (128, 128))


def gather_groups_kernel(phase_ref, hi_ref, lo_ref, in_ref, out_ref):
    cos, sin, flip = quarter_signs((128, 128))
    real = in_ref[0] + flip * in_ref[2] + cos * (in_ref[1] + in_ref[3])
    imag = sin * (in_ref[3] - in_ref[1])
    real = real + times_j(imag)
    both = three(hi_ref[...], lo_ref[...], jnp.concatenate([real, -times_j(real)], axis=0))
    turned = times_j(both)
    for kz_hi in range(4):
        tiles = []
        for kz_lo in range(4):
            rows = slice((kz_lo * 4 + kz_hi) * 16, (kz_lo * 4 + kz_hi) * 16 + 16)
            tiles.append(both[rows] * phase_ref[0] - turned[rows] * phase_ref[1])
        for q, tile in enumerate(exchange(tiles)):
            out_ref[pl.ds(q * 64 + kz_hi, 16, stride=4), :] = tile


def mix_kernel(in_ref, weight_ref, wide_ref, out_ref):
    parts = [in_ref[pl.ds(step * 8, 8), :] for step in range(32)]
    while len(parts) > 1:
        parts = [a + b for a, b in zip(parts[0::2], parts[1::2])]
    total = parts[0] + pltpu.roll(parts[0], 4, 0)
    columns = dot(wide_ref[...], total, ((1,), (1,)), highest)
    row = iota((128, 128), 0)
    lane = iota((128, 128), 1)
    near = row // 32 == lane // 32
    row_imag = (row // 16) % 2 == 1
    lane_imag = (lane // 16) % 2 == 1
    flipped = jnp.concatenate(
        [columns[(n ^ 1) * 16 : (n ^ 1) * 16 + 16] for n in range(8)], axis=0
    )
    signed = jnp.where(row_imag[:, 0:8], -columns, columns)
    out = []
    for kz_hi in range(4):
        same = jnp.broadcast_to(signed[:, kz_hi : kz_hi + 1], (128, 128))
        other = jnp.broadcast_to(flipped[:, kz_hi : kz_hi + 1], (128, 128))
        factor = jnp.where(near, jnp.where(lane_imag, other, same), 0.0)
        product = factor * weight_ref[pl.ds(kz_hi * 128, 128), :]
        out.append(jnp.sum(product, axis=0, keepdims=True))
    tile = jnp.concatenate(out + out, axis=0) * (1.0 / (NZ * NX * NY))
    for step in range(32):
        out_ref[pl.ds(step * 8, 8), :] = tile


def scatter_groups_kernel(phase_ref, hi_ref, lo_ref, in_ref, out_ref):
    real = [None] * 16
    imag = [None] * 16
    for kz_hi in range(4):
        tiles = [in_ref[pl.ds(q * 64 + kz_hi, 16, stride=4), :] for q in range(4)]
        for kz_lo, tile in enumerate(exchange(tiles)):
            turned = times_j(tile)
            real[kz_lo * 4 + kz_hi] = tile * phase_ref[0] + turned * phase_ref[1]
            imag[kz_lo * 4 + kz_hi] = turned * phase_ref[0] - tile * phase_ref[1]
    real = three(hi_ref[...], lo_ref[...], jnp.concatenate(real + imag, axis=0))
    imag = times_j(real)
    cos, sin, flip = quarter_signs((128, 128))
    out_ref[0] = real
    out_ref[1] = cos * real + sin * imag
    out_ref[2] = flip * real
    out_ref[3] = cos * real - sin * imag


def twice_gelu(values):
    return values + values * lax.erf(values * np.float32(math.sqrt(0.5)))


def lookup(table, index):
    numbers = lax.GatherDimensionNumbers(
        offset_dims=(),
        collapsed_slice_dims=(1,),
        start_index_map=(1,),
        operand_batching_dims=(0,),
        start_indices_batching_dims=(0,),
    )
    return lax.gather(
        table,
        index[..., None],
        numbers,
        slice_sizes=(1, 1),
        mode=lax.GatherScatterMode.PROMISE_IN_BOUNDS,
    )


ZB = 8
STEPS = LZ // ZB


def point_kernel(
    modes_ref, hi_ref, lo_ref, ytab_ref, label_ref, table_ref, wide1_ref, wide2_ref, bias2_ref,
    out_ref, planes_ref, act_ref, pre_ref,
):
    step = pl.program_id(0)

    @pl.when(step == 0)
    def _():
        high_lane = (iota((128, 128), 1) // 8) % 2 == 1
        for c_hi in range(2):
            tiles = []
            for pair in range(2):
                even = modes_ref[2 * pair]
                odd = modes_ref[2 * pair + 1]
                if c_hi == 0:
                    tile = jnp.where(high_lane, pltpu.roll(odd, 8, 1), even)
                else:
                    tile = jnp.where(high_lane, odd, pltpu.roll(even, 120, 1))
                tiles.append(jnp.concatenate([tile, times_j(tile)], axis=0))
            full = three(hi_ref[...], lo_ref[...], jnp.concatenate(tiles, axis=1))
            full = full.astype(bf16).astype(f32)
            planes_ref[c_hi * 2] = full[:, 0:128]
            planes_ref[c_hi * 2 + 1] = full[:, 128:256]

    def finish(sub):
        slot = sub % 2
        hidden = twice_gelu(pre_ref[slot]).astype(bf16)
        bias2 = jnp.concatenate([bias2_ref[...]] * 4, axis=1)
        encoded = (dot(wide2_ref[...], hidden) + bias2).astype(bf16)
        for half in range(2):
            tile = encoded[:, half * 256 : half * 256 + 256]
            out_ref[:, sub * 2 + half] = tile.reshape(16, 8, 256)

    def transform(pair):
        own = jnp.where(iota((16, 256), 0) % 8 == iota((16, 256), 1) % 8, 1.0, 0.0).astype(bf16)
        left = []
        for row in range(16):
            base = pl.multiple_of(pair * 16, 16) + row
            rows = [planes_ref[t, pl.ds(base, 8, stride=0), :] for t in range(4)]
            block = jnp.concatenate(
                [jnp.concatenate(rows[0:2], axis=1), jnp.concatenate(rows[2:4], axis=1)],
                axis=0,
            )
            left.append(block.astype(bf16) * own)
        return dot(jnp.concatenate(left, axis=0), ytab_ref[...])

    def activate(spatial, pair, slot):
        low = table_ref[0:8, :]
        high = table_ref[8:16, :]
        for row in range(16):
            base = pl.multiple_of(pair * 16, 16) + row
            for half in range(2):
                label = label_ref[half, pl.ds(base, 8, stride=0), :]
                point = jnp.concatenate(
                    [
                        lookup(low, label),
                        lookup(high, label),
                    ],
                    axis=0,
                )
                total = spatial[row * 16 : row * 16 + 16, half * 128 : half * 128 + 128] + point
                lane = (row // 8) * 256 + half * 128
                place = (row % 8) * 16
                act_ref[slot, place : place + 16, lane : lane + 128] = twice_gelu(total).astype(bf16)

    def expand(slot):
        pre_ref[slot] = dot(wide1_ref[:, 0:144], act_ref[slot])

    @pl.when(step == 0)
    def _():
        for slot in range(2):
            act_ref[slot, 128:144] = jnp.ones((16, 512), bf16)
            activate(transform(slot), slot, slot)
        expand(0)

    @pl.when(step < STEPS - 1)
    def _():
        for sub in range(ZB // 2):
            pair = step * (ZB // 2) + sub + 2
            spatial = transform(pair)
            expand(1 - sub % 2)
            finish(sub)
            activate(spatial, pair, sub % 2)

    @pl.when(step == STEPS - 1)
    def _():
        for sub in range(ZB // 2):
            pair = step * (ZB // 2) + sub + 2
            if sub < ZB // 2 - 2:
                spatial = transform(pair)
            if sub < ZB // 2 - 1:
                expand(1 - sub % 2)
            finish(sub)
            if sub < ZB // 2 - 2:
                activate(spatial, pair, sub % 2)


def room(mib):
    return pltpu.CompilerParams(vmem_limit_bytes=mib * 1024 * 1024)


def vmem():
    return pl.BlockSpec(memory_space=pltpu.VMEM)


def far(*values):
    return [pltpu.with_memory_space_constraint(jnp.asarray(v), pltpu.HBM) for v in values]


def shards(
    occupancy,
    embedding,
    spectral_weight,
    point_weight,
    point_bias,
    expand_weight,
    expand_bias,
    reduce_weight,
    reduce_bias,
):
    ytab = y_tables()
    z_hi, z_lo = split(z_tables())
    x_hi, x_lo = split(x_tables())
    shape = jax.ShapeDtypeStruct
    labels = occupancy.reshape(ROWS, NY)
    partial = pl.pallas_call(
        forward_kernel,
        out_shape=shape((4, 128, 128), f32),
        in_specs=[pl.BlockSpec(memory_space=pltpu.HBM)] * 4,
        out_specs=vmem(),
        scratch_shapes=[
            pltpu.VMEM((ROWS, NY), jnp.int32),
            pltpu.VMEM((32, 256), bf16),
            pltpu.VMEM((256, 512), bf16),
            pltpu.VMEM((256, 512), bf16),
            pltpu.VMEM((ROWS, NY), bf16),
            pltpu.VMEM((4, 512, 128), f32),
            pltpu.SemaphoreType.DMA((4,)),
        ],
        compiler_params=room(16),
        cost_estimate=pl.CostEstimate(flops=400000000, bytes_accessed=1000000, transcendentals=0),
        name="forward",
    )(*far(labels, ytab, z_hi.T.copy(), z_lo.T.copy()))
    made = pl.pallas_call(
        prepare_kernel,
        out_shape=[
            shape((128, 128), f32),
            shape((512, 128), f32),
            shape((256, 256), bf16),
            shape((256, 256), bf16),
            shape((128, 512), bf16),
            shape((128, 512), bf16),
            shape((512, 256), bf16),
            shape((512, 256), bf16),
            shape((256, 256), bf16),
            shape((2, 512, 128), jnp.int32),
            shape((2, 16, 128), f32),
            shape((16, 128), f32),
            shape((512, 256), bf16),
            shape((128, 512), bf16),
            shape((128, 128), f32),
        ],
        in_specs=[pl.BlockSpec(memory_space=pltpu.HBM)] * 17,
        out_specs=[vmem()] * 15,
        scratch_shapes=[
            pltpu.VMEM((ROWS, NY), jnp.int32),
            pltpu.VMEM((64, 128), f32),
            pltpu.VMEM((NCLASS, CH), f32),
            pltpu.VMEM((512, 16), f32),
            pltpu.VMEM((CH, CH), f32),
            pltpu.VMEM((1, CH), f32),
            pltpu.VMEM((CH, HIDDEN), bf16),
            pltpu.VMEM((1, HIDDEN), f32),
            pltpu.VMEM((CH, HIDDEN), bf16),
            pltpu.VMEM((1, CH), f32),
            pltpu.SemaphoreType.DMA((17,)),
        ],
        compiler_params=room(16),
        cost_estimate=pl.CostEstimate(flops=200000000, bytes_accessed=3000000, transcendentals=0),
        name="prepare",
    )(
        *far(
            labels,
            x_hi.transpose(2, 0, 1).reshape(256, 256),
            x_lo.transpose(2, 0, 1).reshape(256, 256),
            x_hi.transpose(1, 0, 2).reshape(128, 512),
            x_lo.transpose(1, 0, 2).reshape(128, 512),
            z_hi,
            z_lo,
            y_lanes(ytab),
            pen_phases(),
            embedding,
            spectral_weight.reshape(512, 16),
            point_weight,
            point_bias.reshape(1, CH),
            expand_weight,
            expand_bias.reshape(1, HIDDEN),
            reduce_weight.T,
            reduce_bias.reshape(1, CH),
        )
    )
    wide, weight, xi_hi, xi_lo, xo_hi, xo_lo = made[:6]
    z_hi, z_lo, ylane, labels, phases, table, wide1, wide2, bias2 = made[6:]
    partial = lax.all_to_all(partial, "grp", 0, 0, tiled=True)
    chunks = pl.pallas_call(
        gather_groups_kernel,
        out_shape=shape((256, 128), f32),
        in_specs=[vmem()] * 4,
        out_specs=vmem(),
        compiler_params=room(8),
        name="gather_groups",
    )(phases, xi_hi, xi_lo, partial)
    chunks = lax.all_to_all(chunks.reshape(64, 4, 128), "pen", 0, 0, tiled=True)
    mixed = pl.pallas_call(
        mix_kernel,
        out_shape=shape((256, 128), f32),
        in_specs=[vmem()] * 3,
        out_specs=vmem(),
        compiler_params=room(8),
        name="mix",
    )(chunks.reshape(256, 128), weight, wide)
    mixed = lax.all_to_all(mixed.reshape(64, 4, 128), "pen", 0, 0, tiled=True)
    modes = pl.pallas_call(
        scatter_groups_kernel,
        out_shape=shape((4, 128, 128), f32),
        in_specs=[vmem()] * 4,
        out_specs=vmem(),
        compiler_params=room(8),
        name="scatter_groups",
    )(phases, xo_hi, xo_lo, mixed.reshape(256, 128))
    modes = lax.all_to_all(modes, "grp", 0, 0, tiled=True)
    return pl.pallas_call(
        point_kernel,
        out_shape=shape((CH, LZ, LX, NY), bf16),
        grid=(STEPS,),
        in_specs=[vmem()] * 9,
        out_specs=pl.BlockSpec((CH, ZB, LX, NY), lambda i: (0, i, 0, 0)),
        scratch_shapes=[
            pltpu.VMEM((4, 512, 128), f32),
            pltpu.VMEM((ZB // 2, 144, 512), bf16),
            pltpu.VMEM((ZB // 2, 512, 512), f32),
        ],
        compiler_params=room(24),
        name="point",
    )(modes, z_hi, z_lo, ylane, labels, table, wide1, wide2, bias2)


def solution(mesh):
    return jax.shard_map(
        shards,
        mesh=mesh,
        in_specs=(
            P("grp", "pen", None),
            P(),
            P(("grp", "pen"), None, None, None, None),
            P(),
            P(),
            P(),
            P(),
            P(),
            P(),
        ),
        out_specs=P(None, "grp", "pen", None),
        check_vma=False,
    )
```

```python
import functools
import math

import jax
import jax.numpy as jnp
import ml_dtypes
import numpy as np
from jax import lax
from jax.experimental import pallas as pl
from jax.experimental.pallas import tpu as pltpu
from jax.sharding import PartitionSpec as P

NZ = 256
NX = 512
NY = 256
CH = 16
MODES = 16
NCLASS = 12
HIDDEN = 64
LZ = 64
LX = 8
ROWS = LZ * LX

highest = lax.Precision.HIGHEST
f32 = jnp.float32
bf16 = jnp.bfloat16
FREQ = np.where(np.arange(MODES) < 8, np.arange(MODES), np.arange(MODES) - MODES)


def split(values):
    hi = values.astype(ml_dtypes.bfloat16)
    lo = (values - hi.astype(np.float64)).astype(ml_dtypes.bfloat16)
    return hi, lo


def y_tables():
    product = np.remainder(FREQ[:, None] * np.arange(NY)[None, :], NY)
    angles = product.astype(np.float32) * np.float32(2.0 * math.pi / NY)
    cos = np.cos(angles).astype(ml_dtypes.bfloat16)
    sin = np.sin(angles).astype(ml_dtypes.bfloat16)
    return np.stack([cos, -sin], axis=1).reshape(2 * MODES, NY)


def z_tables():
    angles = 2.0 * np.pi * np.remainder(FREQ[None, :] * np.arange(LZ)[:, None], NZ) / NZ
    table = np.zeros((LZ, LX, 2, LX, MODES))
    for x in range(LX):
        table[:, x, 0, x] = np.cos(angles)
        table[:, x, 1, x] = np.sin(angles)
    return table.reshape(ROWS, 2 * LX * MODES)


def x_tables():
    angles = 2.0 * np.pi * np.remainder(FREQ[None, :] * np.arange(LX)[:, None], NX) / NX
    table = np.zeros((2, LX, MODES, MODES, MODES))
    for kz in range(MODES):
        table[0, :, kz, :, kz] = np.cos(angles)
        table[1, :, kz, :, kz] = np.sin(angles)
    table = table.reshape(2, LX * MODES, MODES, 4, 4)
    return table.transpose(0, 1, 4, 3, 2).reshape(2, LX * MODES, MODES * MODES)


def y_lanes(ytab):
    table = ytab.reshape(2, 2, 4, 2, NY)
    table = np.moveaxis(table, (0, 1, 2, 3), (0, 3, 1, 2))
    return np.repeat(table.reshape(2 * MODES, NY), 8, axis=0)


def pen_phases():
    turn = np.remainder(np.arange(64)[:, None] * FREQ[None, :], 64)
    angles = 2.0 * np.pi * turn / 64
    table = np.zeros((64, 128), np.float32)
    table[:, 0:16] = np.cos(angles)
    table[:, 16:32] = np.sin(angles)
    return table


def iota(shape, axis):
    return lax.broadcasted_iota(jnp.int32, shape, axis)


def times_j(tile):
    imag_lane = (iota(tile.shape, 1) // 16) % 2 == 1
    return jnp.where(imag_lane, pltpu.roll(tile, 16, 1), -pltpu.roll(tile, 112, 1))


def exchange(tiles):
    block = iota(tiles[0].shape, 1) // 32
    out = []
    for i in range(4):
        best = tiles[i]
        for j in range(4):
            if j != i:
                best = jnp.where(block == j, pltpu.roll(tiles[j], 32 * (j - i) % 128, 1), best)
        out.append(best)
    return out


def quarter_signs(shape):
    quarter = iota(shape, 0) % 4
    cos = jnp.where(quarter == 0, 1.0, jnp.where(quarter == 2, -1.0, 0.0))
    sin = jnp.where(quarter == 1, 1.0, jnp.where(quarter == 3, -1.0, 0.0))
    flip = jnp.where(quarter % 2 == 0, 1.0, -1.0)
    return cos, sin, flip


def to_parts(values):
    hi = values.astype(bf16)
    lo = (values - hi.astype(f32)).astype(bf16)
    return hi, lo


def dot(left, right, dims=((1,), (0,)), precision=None):
    return lax.dot_general(
        left, right, (dims, ((), ())), precision=precision, preferred_element_type=f32
    )


def three(hi, lo, right):
    right_hi, right_lo = to_parts(right)
    return dot(hi, right_hi) + dot(hi, right_lo) + dot(lo, right_hi)


def forward_kernel(
    occ, ytab, zt_hi, zt_lo, own_ref, one_ref, two_ref, three_ref,
    occ_v, ytab_v, zt_hi_v, zt_lo_v, small_ref, rows_ref, tile_ref, sems,
):
    pairs = [(occ, occ_v), (ytab, ytab_v), (zt_hi, zt_hi_v), (zt_lo, zt_lo_v)]
    copies = [pltpu.make_async_copy(a, b, sems.at[i]) for i, (a, b) in enumerate(pairs)]
    for copy in copies:
        copy.start()
    for label in range(NCLASS, 16):
        for quarter in range(4):
            rows_ref[quarter, pl.ds(label, 32, stride=16), :] = jnp.zeros((32, 128), f32)
    copies[0].wait()
    copies[1].wait()
    small_ref[...] = occ_v[...].astype(f32).astype(bf16)
    for label in range(NCLASS):
        same = small_ref[...] == jnp.array(label, bf16)
        hot = jnp.where(same, jnp.array(1.0, bf16), jnp.array(0.0, bf16))
        part = dot(ytab_v[...], hot, ((1,), (1,)))
        for quarter in range(4):
            rows_ref[quarter, pl.ds(label, 32, stride=16), :] = part[
                :, quarter * 128 : (quarter + 1) * 128
            ]
    copies[2].wait()
    copies[3].wait()
    nt = ((1,), (1,))
    for pair in range(2):
        block = [rows_ref[quarter, pl.ds(pair * 256, 256), :] for quarter in range(4)]
        block_hi, block_lo = to_parts(jnp.concatenate(block, axis=1))
        full = (
            dot(zt_hi_v[...], block_hi, nt)
            + dot(zt_hi_v[...], block_lo, nt)
            + dot(zt_lo_v[...], block_hi, nt)
        )
        for half in range(2):
            tile = full[:, half * 128 : (half + 1) * 128]
            tile_ref[pair * 2 + half] = tile[:128] - times_j(tile[128:])
    here = lax.axis_index("grp")
    for k, ref in enumerate((own_ref, one_ref, two_ref, three_ref)):
        ref[...] = tile_ref[(here + k) % 4]


def prepare_kernel(
    occ, xi_hi, xi_lo, xo_hi, xo_lo, z_hi, z_lo, ylane, phase, emb, weight, pw, pb, w1, b1, w2, b2,
    wide_ref, rep_ref, xi_hi_out, xi_lo_out, xo_hi_out, xo_lo_out, z_hi_out, z_lo_out,
    ylane_out, label_ref, phase_out, table_ref, wide1_ref, wide2_ref, bias2_ref,
    occ_v, phase_v, emb_v, weight_v, pw_v, pb_v, w1_v, b1_v, w2_v, b2_v, sems,
):
    pairs = [
        (occ, occ_v), (emb, emb_v), (weight, weight_v), (pw, pw_v), (pb, pb_v), (w1, w1_v),
        (b1, b1_v), (w2, w2_v), (b2, b2_v), (phase, phase_v), (xi_hi, xi_hi_out),
        (xi_lo, xi_lo_out), (xo_hi, xo_hi_out), (xo_lo, xo_lo_out), (z_hi, z_hi_out),
        (z_lo, z_lo_out), (ylane, ylane_out),
    ]
    copies = [pltpu.make_async_copy(a, b, sems.at[i]) for i, (a, b) in enumerate(pairs)]
    for copy in copies:
        copy.start()
    for copy in copies:
        copy.wait()
    for half in range(2):
        label_ref[half] = occ_v[:, half * 128 : (half + 1) * 128]
    left = jnp.where(iota((128, NCLASS), 0) % 16 == iota((128, NCLASS), 1), 1.0, 0.0).astype(f32)
    right = jnp.where(iota((16, 128), 1) % 16 == iota((16, 128), 0), 1.0, 0.0).astype(f32)
    lifted = dot(left, emb_v[...], precision=highest)
    wide = dot(right, lifted, ((0,), (1,)), highest)
    wide_ref[...] = jnp.where(
        iota((128, 128), 0) // 16 == iota((128, 128), 1) // 16, wide, 0.0
    )
    rep_ref[...] = jnp.concatenate([weight_v[...]] * 8, axis=1)
    row = phase_v[pl.ds(lax.axis_index("pen"), 16, stride=0), :]
    for half in range(2):
        pick = iota((16, 128), 1) == iota((16, 128), 0) + 16 * half
        column = jnp.sum(jnp.where(pick, row, 0.0), axis=1, keepdims=True)
        phase_out[half] = jnp.broadcast_to(column, (16, 128))

    table = dot(pw_v[...], emb_v[...], ((0,), (1,)), highest)
    spread = jnp.where(
        iota((NCLASS, 128), 0) == iota((NCLASS, 128), 1), 1.0, 0.0
    ).astype(f32)
    eye = iota((16, 16), 0) == iota((16, 16), 1)
    bias = jnp.sum(jnp.where(eye, pb_v[...], 0.0), axis=1, keepdims=True)
    table_ref[...] = dot(table, spread, precision=highest) + bias
    r1 = jnp.where(iota((64, 64), 0) == iota((64, 64), 1), 1.0, 0.0)
    r2 = jnp.where(iota((16, 128), 1) % 16 == iota((16, 128), 0), 0.5, 0.0).astype(bf16)
    full1 = dot(dot(r1.astype(bf16), w1_v[...], ((1,), (1,))).astype(bf16), r2)
    col1 = jnp.broadcast_to(jnp.sum(r1 * b1_v[...], axis=1, keepdims=True), (64, 128))
    first = col1.astype(bf16).astype(f32)
    second = (col1 - first).astype(bf16).astype(f32)
    third = col1 - first - second
    lane = iota((64, 128), 1)
    extra = jnp.where(
        lane == 0, first, jnp.where(lane == 1, second, jnp.where(lane == 2, third, 0.0))
    ).astype(bf16)
    for x in range(LX):
        wide1_ref[x * 64 : x * 64 + 64, 0:128] = jnp.where(lane // 16 == x, full1, 0.0).astype(bf16)
        wide1_ref[x * 64 : x * 64 + 64, 128:256] = extra
    r3 = jnp.where(iota((128, 16), 0) // 8 == iota((128, 16), 1), 1.0, 0.0)
    r4 = jnp.where(iota((64, 128), 1) % 64 == iota((64, 128), 0), 0.5, 0.0).astype(bf16)
    full2 = dot(dot(r3.astype(bf16), w2_v[...]).astype(bf16), r4)
    x_row = iota((128, 128), 0) % 8
    x_lane = iota((128, 128), 1) // 64
    for tile in range(4):
        wide2_ref[:, tile * 128 : tile * 128 + 128] = jnp.where(
            x_row == x_lane + 2 * tile, full2, 0.0
        ).astype(bf16)
    col2 = jnp.sum(r3 * b2_v[...], axis=1, keepdims=True)
    bias2_ref[...] = jnp.broadcast_to(col2, (128, 128))


def gather_groups_kernel(phase_ref, hi_ref, lo_ref, own_ref, one_ref, two_ref, three_ref, out_ref, in_ref):
    here = lax.axis_index("grp")
    for k, ref in enumerate((own_ref, one_ref, two_ref, three_ref)):
        in_ref[(here + 4 - k) % 4] = ref[...]
    cos, sin, flip = quarter_signs((128, 128))
    real = in_ref[0] + flip * in_ref[2] + cos * (in_ref[1] + in_ref[3])
    imag = sin * (in_ref[3] - in_ref[1])
    real = real + times_j(imag)
    both = three(hi_ref[...], lo_ref[...], jnp.concatenate([real, -times_j(real)], axis=0))
    turned = times_j(both)
    for kz_hi in range(4):
        tiles = []
        for kz_lo in range(4):
            rows = slice((kz_lo * 4 + kz_hi) * 16, (kz_lo * 4 + kz_hi) * 16 + 16)
            tiles.append(both[rows] * phase_ref[0] - turned[rows] * phase_ref[1])
        for q, tile in enumerate(exchange(tiles)):
            out_ref[pl.ds(q * 64 + kz_hi, 16, stride=4), :] = tile


def mix_kernel(in_ref, weight_ref, wide_ref, out_ref):
    parts = [in_ref[pl.ds(step * 8, 8), :] for step in range(32)]
    while len(parts) > 1:
        parts = [a + b for a, b in zip(parts[0::2], parts[1::2])]
    total = parts[0] + pltpu.roll(parts[0], 4, 0)
    columns = dot(wide_ref[...], total, ((1,), (1,)), highest)
    row = iota((128, 128), 0)
    lane = iota((128, 128), 1)
    near = row // 32 == lane // 32
    row_imag = (row // 16) % 2 == 1
    lane_imag = (lane // 16) % 2 == 1
    flipped = jnp.concatenate(
        [columns[(n ^ 1) * 16 : (n ^ 1) * 16 + 16] for n in range(8)], axis=0
    )
    signed = jnp.where(row_imag[:, 0:8], -columns, columns)
    out = []
    for kz_hi in range(4):
        same = jnp.broadcast_to(signed[:, kz_hi : kz_hi + 1], (128, 128))
        other = jnp.broadcast_to(flipped[:, kz_hi : kz_hi + 1], (128, 128))
        factor = jnp.where(near, jnp.where(lane_imag, other, same), 0.0)
        product = factor * weight_ref[pl.ds(kz_hi * 128, 128), :]
        out.append(jnp.sum(product, axis=0, keepdims=True))
    tile = jnp.concatenate(out + out, axis=0) * (1.0 / (NZ * NX * NY))
    for step in range(32):
        out_ref[pl.ds(step * 8, 8), :] = tile


def scatter_groups_kernel(phase_ref, hi_ref, lo_ref, in_ref, own_ref, one_ref, two_ref, three_ref, out_ref):
    real = [None] * 16
    imag = [None] * 16
    for kz_hi in range(4):
        tiles = [in_ref[pl.ds(q * 64 + kz_hi, 16, stride=4), :] for q in range(4)]
        for kz_lo, tile in enumerate(exchange(tiles)):
            turned = times_j(tile)
            real[kz_lo * 4 + kz_hi] = tile * phase_ref[0] + turned * phase_ref[1]
            imag[kz_lo * 4 + kz_hi] = turned * phase_ref[0] - tile * phase_ref[1]
    real = three(hi_ref[...], lo_ref[...], jnp.concatenate(real + imag, axis=0))
    imag = times_j(real)
    cos, sin, flip = quarter_signs((128, 128))
    out_ref[0] = real
    out_ref[1] = cos * real + sin * imag
    out_ref[2] = flip * real
    out_ref[3] = cos * real - sin * imag
    here = lax.axis_index("grp")
    for k, ref in enumerate((own_ref, one_ref, two_ref, three_ref)):
        ref[...] = out_ref[(here + k) % 4]


def twice_gelu(values):
    return values + values * lax.erf(values * np.float32(math.sqrt(0.5)))


def lookup(table, index):
    numbers = lax.GatherDimensionNumbers(
        offset_dims=(),
        collapsed_slice_dims=(1,),
        start_index_map=(1,),
        operand_batching_dims=(0,),
        start_indices_batching_dims=(0,),
    )
    return lax.gather(
        table,
        index[..., None],
        numbers,
        slice_sizes=(1, 1),
        mode=lax.GatherScatterMode.PROMISE_IN_BOUNDS,
    )


ZB = 16
STEPS = LZ // ZB


def point_kernel(
    own_ref, one_ref, two_ref, three_ref, hi_ref, lo_ref, ytab_ref, label_ref, table_ref, wide1_ref, wide2_ref, bias2_ref,
    out_ref, planes_ref, act_ref, pre_ref, modes_ref,
):
    step = pl.program_id(0)

    @pl.when(step == 0)
    def _():
        here = lax.axis_index("grp")
        for k, ref in enumerate((own_ref, one_ref, two_ref, three_ref)):
            modes_ref[(here + 4 - k) % 4] = ref[...]
        high_lane = (iota((128, 128), 1) // 8) % 2 == 1
        for c_hi in range(2):
            tiles = []
            for pair in range(2):
                even = modes_ref[2 * pair]
                odd = modes_ref[2 * pair + 1]
                if c_hi == 0:
                    tile = jnp.where(high_lane, pltpu.roll(odd, 8, 1), even)
                else:
                    tile = jnp.where(high_lane, odd, pltpu.roll(even, 120, 1))
                tiles.append(jnp.concatenate([tile, times_j(tile)], axis=0))
            full = three(hi_ref[...], lo_ref[...], jnp.concatenate(tiles, axis=1))
            full = full.astype(bf16).astype(f32)
            planes_ref[c_hi * 2] = full[:, 0:128]
            planes_ref[c_hi * 2 + 1] = full[:, 128:256]

    def finish(sub):
        slot = sub % 2
        hidden = twice_gelu(pre_ref[slot]).astype(bf16)
        bias2 = jnp.concatenate([bias2_ref[...]] * 4, axis=1)
        encoded = (dot(wide2_ref[...], hidden) + bias2).astype(bf16)
        for half in range(2):
            tile = encoded[:, half * 256 : half * 256 + 256]
            out_ref[:, sub * 2 + half] = tile.reshape(16, 8, 256)

    def transform(pair):
        own = jnp.where(iota((16, 256), 0) % 8 == iota((16, 256), 1) % 8, 1.0, 0.0).astype(bf16)
        left = []
        for row in range(16):
            base = pl.multiple_of(pair * 16, 16) + row
            rows = [planes_ref[t, pl.ds(base, 8, stride=0), :] for t in range(4)]
            block = jnp.concatenate(
                [jnp.concatenate(rows[0:2], axis=1), jnp.concatenate(rows[2:4], axis=1)],
                axis=0,
            )
            left.append(block.astype(bf16) * own)
        return dot(jnp.concatenate(left, axis=0), ytab_ref[...])

    def activate(spatial, pair, slot):
        low = table_ref[0:8, :]
        high = table_ref[8:16, :]
        for row in range(16):
            base = pl.multiple_of(pair * 16, 16) + row
            for half in range(2):
                label = label_ref[half, pl.ds(base, 8, stride=0), :]
                point = jnp.concatenate(
                    [
                        lookup(low, label),
                        lookup(high, label),
                    ],
                    axis=0,
                )
                total = spatial[row * 16 : row * 16 + 16, half * 128 : half * 128 + 128] + point
                lane = (row // 8) * 256 + half * 128
                place = (row % 8) * 16
                act_ref[slot, place : place + 16, lane : lane + 128] = twice_gelu(total).astype(bf16)

    def expand(slot):
        pre_ref[slot] = dot(wide1_ref[:, 0:144], act_ref[slot])

    @pl.when(step == 0)
    def _():
        for slot in range(2):
            act_ref[slot, 128:144] = jnp.ones((16, 512), bf16)
            activate(transform(slot), slot, slot)
        expand(0)

    @pl.when(step < STEPS - 1)
    def _():
        for sub in range(ZB // 2):
            pair = step * (ZB // 2) + sub + 2
            spatial = transform(pair)
            expand(1 - sub % 2)
            finish(sub)
            activate(spatial, pair, sub % 2)

    @pl.when(step == STEPS - 1)
    def _():
        for sub in range(ZB // 2):
            pair = step * (ZB // 2) + sub + 2
            if sub < ZB // 2 - 2:
                spatial = transform(pair)
            if sub < ZB // 2 - 1:
                expand(1 - sub % 2)
            finish(sub)
            if sub < ZB // 2 - 2:
                activate(spatial, pair, sub % 2)


def room(mib):
    return pltpu.CompilerParams(vmem_limit_bytes=mib * 1024 * 1024)


def vmem():
    return pl.BlockSpec(memory_space=pltpu.VMEM)


def rotate(tiles):
    moved = [tiles[0]]
    for k in range(1, 4):
        moved.append(lax.ppermute(tiles[k], "grp", [(i, (i + k) % 4) for i in range(4)]))
    return moved


def far(*values):
    return [pltpu.with_memory_space_constraint(jnp.asarray(v), pltpu.HBM) for v in values]


def shards(
    occupancy,
    embedding,
    spectral_weight,
    point_weight,
    point_bias,
    expand_weight,
    expand_bias,
    reduce_weight,
    reduce_bias,
):
    ytab = y_tables()
    z_hi, z_lo = split(z_tables())
    x_hi, x_lo = split(x_tables())
    shape = jax.ShapeDtypeStruct
    labels = occupancy.reshape(ROWS, NY)
    partial = pl.pallas_call(
        forward_kernel,
        out_shape=[shape((128, 128), f32)] * 4,
        in_specs=[pl.BlockSpec(memory_space=pltpu.HBM)] * 4,
        out_specs=[vmem()] * 4,
        scratch_shapes=[
            pltpu.VMEM((ROWS, NY), jnp.int32),
            pltpu.VMEM((32, 256), bf16),
            pltpu.VMEM((256, 512), bf16),
            pltpu.VMEM((256, 512), bf16),
            pltpu.VMEM((ROWS, NY), bf16),
            pltpu.VMEM((4, 512, 128), f32),
            pltpu.VMEM((4, 128, 128), f32),
            pltpu.SemaphoreType.DMA((4,)),
        ],
        compiler_params=room(16),
        cost_estimate=pl.CostEstimate(flops=400000000, bytes_accessed=1000000, transcendentals=0),
        name="forward",
    )(*far(labels, ytab, z_hi.T.copy(), z_lo.T.copy()))
    made = pl.pallas_call(
        prepare_kernel,
        out_shape=[
            shape((128, 128), f32),
            shape((512, 128), f32),
            shape((256, 256), bf16),
            shape((256, 256), bf16),
            shape((128, 512), bf16),
            shape((128, 512), bf16),
            shape((512, 256), bf16),
            shape((512, 256), bf16),
            shape((256, 256), bf16),
            shape((2, 512, 128), jnp.int32),
            shape((2, 16, 128), f32),
            shape((16, 128), f32),
            shape((512, 256), bf16),
            shape((128, 512), bf16),
            shape((128, 128), f32),
        ],
        in_specs=[pl.BlockSpec(memory_space=pltpu.HBM)] * 17,
        out_specs=[vmem()] * 15,
        scratch_shapes=[
            pltpu.VMEM((ROWS, NY), jnp.int32),
            pltpu.VMEM((64, 128), f32),
            pltpu.VMEM((NCLASS, CH), f32),
            pltpu.VMEM((512, 16), f32),
            pltpu.VMEM((CH, CH), f32),
            pltpu.VMEM((1, CH), f32),
            pltpu.VMEM((CH, HIDDEN), bf16),
            pltpu.VMEM((1, HIDDEN), f32),
            pltpu.VMEM((CH, HIDDEN), bf16),
            pltpu.VMEM((1, CH), f32),
            pltpu.SemaphoreType.DMA((17,)),
        ],
        compiler_params=room(16),
        cost_estimate=pl.CostEstimate(flops=200000000, bytes_accessed=3000000, transcendentals=0),
        name="prepare",
    )(
        *far(
            labels,
            x_hi.transpose(2, 0, 1).reshape(256, 256),
            x_lo.transpose(2, 0, 1).reshape(256, 256),
            x_hi.transpose(1, 0, 2).reshape(128, 512),
            x_lo.transpose(1, 0, 2).reshape(128, 512),
            z_hi,
            z_lo,
            y_lanes(ytab),
            pen_phases(),
            embedding,
            spectral_weight.reshape(512, 16),
            point_weight,
            point_bias.reshape(1, CH),
            expand_weight,
            expand_bias.reshape(1, HIDDEN),
            reduce_weight.T,
            reduce_bias.reshape(1, CH),
        )
    )
    wide, weight, xi_hi, xi_lo, xo_hi, xo_lo = made[:6]
    z_hi, z_lo, ylane, labels, phases, table, wide1, wide2, bias2 = made[6:]
    partial = rotate(partial)
    chunks = pl.pallas_call(
        gather_groups_kernel,
        out_shape=shape((256, 128), f32),
        in_specs=[vmem()] * 7,
        out_specs=vmem(),
        scratch_shapes=[pltpu.VMEM((4, 128, 128), f32)],
        compiler_params=room(8),
        name="gather_groups",
    )(phases, xi_hi, xi_lo, *partial)
    chunks = lax.all_to_all(chunks.reshape(64, 4, 128), "pen", 0, 0, tiled=True)
    mixed = pl.pallas_call(
        mix_kernel,
        out_shape=shape((256, 128), f32),
        in_specs=[vmem()] * 3,
        out_specs=vmem(),
        compiler_params=room(8),
        name="mix",
    )(chunks.reshape(256, 128), weight, wide)
    mixed = lax.all_to_all(mixed.reshape(64, 4, 128), "pen", 0, 0, tiled=True)
    modes = pl.pallas_call(
        scatter_groups_kernel,
        out_shape=[shape((128, 128), f32)] * 4,
        in_specs=[vmem()] * 4,
        out_specs=[vmem()] * 4,
        scratch_shapes=[pltpu.VMEM((4, 128, 128), f32)],
        compiler_params=room(8),
        name="scatter_groups",
    )(phases, xo_hi, xo_lo, mixed.reshape(256, 128))
    modes = rotate(modes)
    return pl.pallas_call(
        point_kernel,
        out_shape=shape((CH, LZ, LX, NY), bf16),
        grid=(STEPS,),
        in_specs=[vmem()] * 12,
        out_specs=pl.BlockSpec((CH, ZB, LX, NY), lambda i: (0, i, 0, 0)),
        scratch_shapes=[
            pltpu.VMEM((4, 512, 128), f32),
            pltpu.VMEM((2, 144, 512), bf16),
            pltpu.VMEM((2, 512, 512), f32),
            pltpu.VMEM((4, 128, 128), f32),
        ],
        compiler_params=room(24),
        name="point",
    )(*modes, z_hi, z_lo, ylane, labels, table, wide1, wide2, bias2)


def solution(mesh):
    return jax.shard_map(
        shards,
        mesh=mesh,
        in_specs=(
            P("grp", "pen", None),
            P(),
            P(("grp", "pen"), None, None, None, None),
            P(),
            P(),
            P(),
            P(),
            P(),
            P(),
        ),
        out_specs=P(None, "grp", "pen", None),
        check_vma=False,
    )
```

```python
import functools
import math

import jax
import jax.numpy as jnp
import ml_dtypes
import numpy as np
from jax import lax
from jax.experimental import pallas as pl
from jax.experimental.pallas import tpu as pltpu
from jax.sharding import PartitionSpec as P

NZ = 256
NX = 512
NY = 256
CH = 16
MODES = 16
NCLASS = 12
HIDDEN = 64
LZ = 64
LX = 8
ROWS = LZ * LX

highest = lax.Precision.HIGHEST
f32 = jnp.float32
bf16 = jnp.bfloat16
FREQ = np.where(np.arange(MODES) < 8, np.arange(MODES), np.arange(MODES) - MODES)


def split(values):
    hi = values.astype(ml_dtypes.bfloat16)
    lo = (values - hi.astype(np.float64)).astype(ml_dtypes.bfloat16)
    return hi, lo


def y_tables():
    product = np.remainder(FREQ[:, None] * np.arange(NY)[None, :], NY)
    angles = product.astype(np.float32) * np.float32(2.0 * math.pi / NY)
    cos = np.cos(angles).astype(ml_dtypes.bfloat16)
    sin = np.sin(angles).astype(ml_dtypes.bfloat16)
    return np.stack([cos, -sin], axis=1).reshape(2 * MODES, NY)


def z_tables():
    angles = 2.0 * np.pi * np.remainder(FREQ[None, :] * np.arange(LZ)[:, None], NZ) / NZ
    table = np.zeros((LZ, LX, 2, LX, MODES))
    for x in range(LX):
        table[:, x, 0, x] = np.cos(angles)
        table[:, x, 1, x] = np.sin(angles)
    return table.reshape(ROWS, 2 * LX * MODES)


def x_tables():
    angles = 2.0 * np.pi * np.remainder(FREQ[None, :] * np.arange(LX)[:, None], NX) / NX
    table = np.zeros((2, LX, MODES, MODES, MODES))
    for kz in range(MODES):
        table[0, :, kz, :, kz] = np.cos(angles)
        table[1, :, kz, :, kz] = np.sin(angles)
    table = table.reshape(2, LX * MODES, MODES, 4, 4)
    return table.transpose(0, 1, 4, 3, 2).reshape(2, LX * MODES, MODES * MODES)


def y_lanes(ytab):
    table = ytab.reshape(2, 2, 4, 2, NY)
    table = np.moveaxis(table, (0, 1, 2, 3), (0, 3, 1, 2))
    return np.repeat(table.reshape(2 * MODES, NY), 8, axis=0)


def pen_phases():
    turn = np.remainder(np.arange(64)[:, None] * FREQ[None, :], 64)
    angles = 2.0 * np.pi * turn / 64
    table = np.zeros((64, 128), np.float32)
    table[:, 0:16] = np.cos(angles)
    table[:, 16:32] = np.sin(angles)
    return table


def iota(shape, axis):
    return lax.broadcasted_iota(jnp.int32, shape, axis)


def times_j(tile):
    imag_lane = (iota(tile.shape, 1) // 16) % 2 == 1
    return jnp.where(imag_lane, pltpu.roll(tile, 16, 1), -pltpu.roll(tile, 112, 1))


def exchange(tiles):
    block = iota(tiles[0].shape, 1) // 32
    out = []
    for i in range(4):
        best = tiles[i]
        for j in range(4):
            if j != i:
                best = jnp.where(block == j, pltpu.roll(tiles[j], 32 * (j - i) % 128, 1), best)
        out.append(best)
    return out


def quarter_signs(shape):
    quarter = iota(shape, 0) % 4
    cos = jnp.where(quarter == 0, 1.0, jnp.where(quarter == 2, -1.0, 0.0))
    sin = jnp.where(quarter == 1, 1.0, jnp.where(quarter == 3, -1.0, 0.0))
    flip = jnp.where(quarter % 2 == 0, 1.0, -1.0)
    return cos, sin, flip


def to_parts(values):
    hi = values.astype(bf16)
    lo = (values - hi.astype(f32)).astype(bf16)
    return hi, lo


def dot(left, right, dims=((1,), (0,)), precision=None):
    return lax.dot_general(
        left, right, (dims, ((), ())), precision=precision, preferred_element_type=f32
    )


def three(hi, lo, right):
    right_hi, right_lo = to_parts(right)
    return dot(hi, right_hi) + dot(hi, right_lo) + dot(lo, right_hi)


def forward_kernel(
    occ, ytab, zt_hi, zt_lo, xi_hi, xi_lo, xo_hi, xo_lo, z_hi, z_lo, ylane, phase, emb, weight, pw,
    pb, w1, b1, w2, b2, own_ref, one_ref, two_ref, three_ref, label_ref, *rest
):
    held, (ytab_v, zt_hi_v, zt_lo_v, small_ref, rows_ref, tile_ref, sems) = rest[:16], rest[16:]
    pairs = [(occ.at[:, pl.ds(half * 128, 128)], label_ref.at[half]) for half in range(2)]
    pairs += [(ytab, ytab_v), (zt_hi, zt_hi_v), (zt_lo, zt_lo_v)]
    later = [xi_hi, xi_lo, emb, weight, pw, pb, w1, b1, w2, b2, phase]
    later += [xo_hi, xo_lo, z_hi, z_lo, ylane]
    pairs += list(zip(later, held))
    copies = [pltpu.make_async_copy(a, b, sems.at[i]) for i, (a, b) in enumerate(pairs)]
    for copy in copies:
        copy.start()
    for label in range(NCLASS, 16):
        for quarter in range(4):
            rows_ref[quarter, pl.ds(label, 32, stride=16), :] = jnp.zeros((32, 128), f32)
    for copy in copies[:3]:
        copy.wait()
    for half in range(2):
        small_ref[:, half * 128 : (half + 1) * 128] = label_ref[half].astype(f32).astype(bf16)
    for label in range(NCLASS):
        same = small_ref[...] == jnp.array(label, bf16)
        hot = jnp.where(same, jnp.array(1.0, bf16), jnp.array(0.0, bf16))
        part = dot(ytab_v[...], hot, ((1,), (1,)))
        for quarter in range(4):
            rows_ref[quarter, pl.ds(label, 32, stride=16), :] = part[
                :, quarter * 128 : (quarter + 1) * 128
            ]
    for copy in copies[3:]:
        copy.wait()
    nt = ((1,), (1,))
    for pair in range(2):
        block = [rows_ref[quarter, pl.ds(pair * 256, 256), :] for quarter in range(4)]
        block_hi, block_lo = to_parts(jnp.concatenate(block, axis=1))
        full = (
            dot(zt_hi_v[...], block_hi, nt)
            + dot(zt_hi_v[...], block_lo, nt)
            + dot(zt_lo_v[...], block_hi, nt)
        )
        for half in range(2):
            tile = full[:, half * 128 : (half + 1) * 128]
            tile_ref[pair * 2 + half] = tile[:128] - times_j(tile[128:])
    here = lax.axis_index("grp")
    for k, ref in enumerate((own_ref, one_ref, two_ref, three_ref)):
        ref[...] = tile_ref[(here + k) % 4]


def prepare_kernel(
    emb_v, weight_v, pw_v, pb_v, w1_v, b1_v, w2_v, b2_v, phase_v,
    wide_ref, rep_ref, phase_out, table_ref, wide1_ref, wide2_ref, bias2_ref,
):
    left = jnp.where(iota((128, NCLASS), 0) % 16 == iota((128, NCLASS), 1), 1.0, 0.0).astype(f32)
    right = jnp.where(iota((16, 128), 1) % 16 == iota((16, 128), 0), 1.0, 0.0).astype(f32)
    lifted = dot(left, emb_v[...], precision=highest)
    wide = dot(right, lifted, ((0,), (1,)), highest)
    wide_ref[...] = jnp.where(
        iota((128, 128), 0) // 16 == iota((128, 128), 1) // 16, wide, 0.0
    )
    rep_ref[...] = jnp.concatenate([weight_v[...]] * 8, axis=1)
    row = phase_v[pl.ds(lax.axis_index("pen"), 16, stride=0), :]
    for half in range(2):
        pick = iota((16, 128), 1) == iota((16, 128), 0) + 16 * half
        column = jnp.sum(jnp.where(pick, row, 0.0), axis=1, keepdims=True)
        phase_out[half] = jnp.broadcast_to(column, (16, 128))

    table = dot(pw_v[...], emb_v[...], ((0,), (1,)), highest)
    spread = jnp.where(
        iota((NCLASS, 128), 0) == iota((NCLASS, 128), 1), 1.0, 0.0
    ).astype(f32)
    eye = iota((16, 16), 0) == iota((16, 16), 1)
    bias = jnp.sum(jnp.where(eye, pb_v[...], 0.0), axis=1, keepdims=True)
    table_ref[...] = dot(table, spread, precision=highest) + bias
    r1 = jnp.where(iota((64, 64), 0) == iota((64, 64), 1), 1.0, 0.0)
    r2 = jnp.where(iota((16, 128), 1) % 16 == iota((16, 128), 0), 0.5, 0.0).astype(bf16)
    full1 = dot(dot(r1.astype(bf16), w1_v[...], ((1,), (1,))).astype(bf16), r2)
    col1 = jnp.broadcast_to(jnp.sum(r1 * b1_v[...], axis=1, keepdims=True), (64, 128))
    first = col1.astype(bf16).astype(f32)
    second = (col1 - first).astype(bf16).astype(f32)
    third = col1 - first - second
    lane = iota((64, 128), 1)
    extra = jnp.where(
        lane == 0, first, jnp.where(lane == 1, second, jnp.where(lane == 2, third, 0.0))
    ).astype(bf16)
    for x in range(LX):
        wide1_ref[x * 64 : x * 64 + 64, 0:128] = jnp.where(lane // 16 == x, full1, 0.0).astype(bf16)
        wide1_ref[x * 64 : x * 64 + 64, 128:256] = extra
    r3 = jnp.where(iota((128, 16), 0) // 8 == iota((128, 16), 1), 1.0, 0.0)
    r4 = jnp.where(iota((64, 128), 1) % 64 == iota((64, 128), 0), 0.5, 0.0).astype(bf16)
    full2 = dot(dot(r3.astype(bf16), w2_v[...]).astype(bf16), r4)
    x_row = iota((128, 128), 0) % 8
    x_lane = iota((128, 128), 1) // 64
    for tile in range(4):
        wide2_ref[:, tile * 128 : tile * 128 + 128] = jnp.where(
            x_row == x_lane + 2 * tile, full2, 0.0
        ).astype(bf16)
    col2 = jnp.sum(r3 * b2_v[...], axis=1, keepdims=True)
    bias2_ref[...] = jnp.broadcast_to(col2, (128, 128))


def gather_groups_kernel(phase_ref, hi_ref, lo_ref, own_ref, one_ref, two_ref, three_ref, out_ref, in_ref):
    here = lax.axis_index("grp")
    for k, ref in enumerate((own_ref, one_ref, two_ref, three_ref)):
        in_ref[(here + 4 - k) % 4] = ref[...]
    cos, sin, flip = quarter_signs((128, 128))
    real = in_ref[0] + flip * in_ref[2] + cos * (in_ref[1] + in_ref[3])
    imag = sin * (in_ref[3] - in_ref[1])
    real = real + times_j(imag)
    both = three(hi_ref[...], lo_ref[...], jnp.concatenate([real, -times_j(real)], axis=0))
    turned = times_j(both)
    for kz_hi in range(4):
        tiles = []
        for kz_lo in range(4):
            rows = slice((kz_lo * 4 + kz_hi) * 16, (kz_lo * 4 + kz_hi) * 16 + 16)
            tiles.append(both[rows] * phase_ref[0] - turned[rows] * phase_ref[1])
        for q, tile in enumerate(exchange(tiles)):
            out_ref[pl.ds(q * 64 + kz_hi, 16, stride=4), :] = tile


def mix_kernel(in_ref, weight_ref, wide_ref, out_ref):
    parts = [in_ref[pl.ds(step * 8, 8), :] for step in range(32)]
    while len(parts) > 1:
        parts = [a + b for a, b in zip(parts[0::2], parts[1::2])]
    total = parts[0] + pltpu.roll(parts[0], 4, 0)
    columns = dot(wide_ref[...], total, ((1,), (1,)), highest)
    row = iota((128, 128), 0)
    lane = iota((128, 128), 1)
    near = row // 32 == lane // 32
    row_imag = (row // 16) % 2 == 1
    lane_imag = (lane // 16) % 2 == 1
    flipped = jnp.concatenate(
        [columns[(n ^ 1) * 16 : (n ^ 1) * 16 + 16] for n in range(8)], axis=0
    )
    signed = jnp.where(row_imag[:, 0:8], -columns, columns)
    out = []
    for kz_hi in range(4):
        same = jnp.broadcast_to(signed[:, kz_hi : kz_hi + 1], (128, 128))
        other = jnp.broadcast_to(flipped[:, kz_hi : kz_hi + 1], (128, 128))
        factor = jnp.where(near, jnp.where(lane_imag, other, same), 0.0)
        product = factor * weight_ref[pl.ds(kz_hi * 128, 128), :]
        out.append(jnp.sum(product, axis=0, keepdims=True))
    tile = jnp.concatenate(out + out, axis=0) * (1.0 / (NZ * NX * NY))
    for step in range(32):
        out_ref[pl.ds(step * 8, 8), :] = tile


def scatter_groups_kernel(phase_ref, hi_ref, lo_ref, in_ref, own_ref, one_ref, two_ref, three_ref, out_ref):
    real = [None] * 16
    imag = [None] * 16
    for kz_hi in range(4):
        tiles = [in_ref[pl.ds(q * 64 + kz_hi, 16, stride=4), :] for q in range(4)]
        for kz_lo, tile in enumerate(exchange(tiles)):
            turned = times_j(tile)
            real[kz_lo * 4 + kz_hi] = tile * phase_ref[0] + turned * phase_ref[1]
            imag[kz_lo * 4 + kz_hi] = turned * phase_ref[0] - tile * phase_ref[1]
    real = three(hi_ref[...], lo_ref[...], jnp.concatenate(real + imag, axis=0))
    imag = times_j(real)
    cos, sin, flip = quarter_signs((128, 128))
    out_ref[0] = real
    out_ref[1] = cos * real + sin * imag
    out_ref[2] = flip * real
    out_ref[3] = cos * real - sin * imag
    here = lax.axis_index("grp")
    for k, ref in enumerate((own_ref, one_ref, two_ref, three_ref)):
        ref[...] = out_ref[(here + k) % 4]


def twice_gelu(values):
    return values + values * lax.erf(values * np.float32(math.sqrt(0.5)))


def lookup(table, index):
    numbers = lax.GatherDimensionNumbers(
        offset_dims=(),
        collapsed_slice_dims=(1,),
        start_index_map=(1,),
        operand_batching_dims=(0,),
        start_indices_batching_dims=(0,),
    )
    return lax.gather(
        table,
        index[..., None],
        numbers,
        slice_sizes=(1, 1),
        mode=lax.GatherScatterMode.PROMISE_IN_BOUNDS,
    )


ZB = 16
STEPS = LZ // ZB


def point_kernel(
    own_ref, one_ref, two_ref, three_ref, hi_ref, lo_ref, ytab_ref, label_ref, table_ref, wide1_ref, wide2_ref, bias2_ref,
    out_ref, planes_ref, act_ref, pre_ref, modes_ref,
):
    step = pl.program_id(0)

    @pl.when(step == 0)
    def _():
        here = lax.axis_index("grp")
        for k, ref in enumerate((own_ref, one_ref, two_ref, three_ref)):
            modes_ref[(here + 4 - k) % 4] = ref[...]
        high_lane = (iota((128, 128), 1) // 8) % 2 == 1
        for c_hi in range(2):
            tiles = []
            for pair in range(2):
                even = modes_ref[2 * pair]
                odd = modes_ref[2 * pair + 1]
                if c_hi == 0:
                    tile = jnp.where(high_lane, pltpu.roll(odd, 8, 1), even)
                else:
                    tile = jnp.where(high_lane, odd, pltpu.roll(even, 120, 1))
                tiles.append(jnp.concatenate([tile, times_j(tile)], axis=0))
            full = three(hi_ref[...], lo_ref[...], jnp.concatenate(tiles, axis=1))
            full = full.astype(bf16).astype(f32)
            planes_ref[c_hi * 2] = full[:, 0:128]
            planes_ref[c_hi * 2 + 1] = full[:, 128:256]

    def finish(sub):
        slot = sub % 2
        hidden = twice_gelu(pre_ref[slot]).astype(bf16)
        bias2 = jnp.concatenate([bias2_ref[...]] * 4, axis=1)
        encoded = (dot(wide2_ref[...], hidden) + bias2).astype(bf16)
        for half in range(2):
            tile = encoded[:, half * 256 : half * 256 + 256]
            out_ref[:, sub * 2 + half] = tile.reshape(16, 8, 256)

    def transform(pair):
        own = jnp.where(iota((16, 256), 0) % 8 == iota((16, 256), 1) % 8, 1.0, 0.0).astype(bf16)
        left = []
        for row in range(16):
            base = pl.multiple_of(pair * 16, 16) + row
            rows = [planes_ref[t, pl.ds(base, 8, stride=0), :] for t in range(4)]
            block = jnp.concatenate(
                [jnp.concatenate(rows[0:2], axis=1), jnp.concatenate(rows[2:4], axis=1)],
                axis=0,
            )
            left.append(block.astype(bf16) * own)
        return dot(jnp.concatenate(left, axis=0), ytab_ref[...])

    def activate(spatial, pair, slot):
        low = table_ref[0:8, :]
        high = table_ref[8:16, :]
        for row in range(16):
            base = pl.multiple_of(pair * 16, 16) + row
            for half in range(2):
                label = label_ref[half, pl.ds(base, 8, stride=0), :]
                point = jnp.concatenate(
                    [
                        lookup(low, label),
                        lookup(high, label),
                    ],
                    axis=0,
                )
                total = spatial[row * 16 : row * 16 + 16, half * 128 : half * 128 + 128] + point
                lane = (row // 8) * 256 + half * 128
                place = (row % 8) * 16
                act_ref[slot, place : place + 16, lane : lane + 128] = twice_gelu(total).astype(bf16)

    def expand(slot):
        pre_ref[slot] = dot(wide1_ref[:, 0:144], act_ref[slot])

    @pl.when(step == 0)
    def _():
        for slot in range(2):
            act_ref[slot, 128:144] = jnp.ones((16, 512), bf16)
            activate(transform(slot), slot, slot)
        expand(0)

    @pl.when(step < STEPS - 1)
    def _():
        for sub in range(ZB // 2):
            pair = step * (ZB // 2) + sub + 2
            spatial = transform(pair)
            expand(1 - sub % 2)
            finish(sub)
            activate(spatial, pair, sub % 2)

    @pl.when(step == STEPS - 1)
    def _():
        for sub in range(ZB // 2):
            pair = step * (ZB // 2) + sub + 2
            if sub < ZB // 2 - 2:
                spatial = transform(pair)
            if sub < ZB // 2 - 1:
                expand(1 - sub % 2)
            finish(sub)
            if sub < ZB // 2 - 2:
                activate(spatial, pair, sub % 2)


def room(mib):
    return pltpu.CompilerParams(vmem_limit_bytes=mib * 1024 * 1024)


def vmem():
    return pl.BlockSpec(memory_space=pltpu.VMEM)


def rotate(tiles):
    moved = [tiles[0]]
    for k in range(1, 4):
        moved.append(lax.ppermute(tiles[k], "grp", [(i, (i + k) % 4) for i in range(4)]))
    return moved


def far(*values):
    return [pltpu.with_memory_space_constraint(jnp.asarray(v), pltpu.HBM) for v in values]


def shards(
    occupancy,
    embedding,
    spectral_weight,
    point_weight,
    point_bias,
    expand_weight,
    expand_bias,
    reduce_weight,
    reduce_bias,
):
    ytab = y_tables()
    z_hi, z_lo = split(z_tables())
    x_hi, x_lo = split(x_tables())
    shape = jax.ShapeDtypeStruct
    sources = far(
        occupancy.reshape(ROWS, NY),
        ytab,
        z_hi.T.copy(),
        z_lo.T.copy(),
        x_hi.transpose(2, 0, 1).reshape(256, 256),
        x_lo.transpose(2, 0, 1).reshape(256, 256),
        x_hi.transpose(1, 0, 2).reshape(128, 512),
        x_lo.transpose(1, 0, 2).reshape(128, 512),
        z_hi,
        z_lo,
        y_lanes(ytab),
        pen_phases(),
        embedding,
        spectral_weight.reshape(512, 16),
        point_weight,
        point_bias.reshape(1, CH),
        expand_weight,
        expand_bias.reshape(1, HIDDEN),
        reduce_weight.T,
        reduce_bias.reshape(1, CH),
    )
    made = pl.pallas_call(
        forward_kernel,
        out_shape=[shape((128, 128), f32)] * 4
        + [
            shape((2, ROWS, 128), jnp.int32),
            shape((256, 256), bf16),
            shape((256, 256), bf16),
            shape((NCLASS, CH), f32),
            shape((512, 16), f32),
            shape((CH, CH), f32),
            shape((1, CH), f32),
            shape((CH, HIDDEN), bf16),
            shape((1, HIDDEN), f32),
            shape((CH, HIDDEN), bf16),
            shape((1, CH), f32),
            shape((64, 128), f32),
            shape((128, 512), bf16),
            shape((128, 512), bf16),
            shape((512, 256), bf16),
            shape((512, 256), bf16),
            shape((256, 256), bf16),
        ],
        in_specs=[pl.BlockSpec(memory_space=pltpu.HBM)] * 20,
        out_specs=[vmem()] * 21,
        scratch_shapes=[
            pltpu.VMEM((32, 256), bf16),
            pltpu.VMEM((256, 512), bf16),
            pltpu.VMEM((256, 512), bf16),
            pltpu.VMEM((ROWS, NY), bf16),
            pltpu.VMEM((4, 512, 128), f32),
            pltpu.VMEM((4, 128, 128), f32),
            pltpu.SemaphoreType.DMA((21,)),
        ],
        compiler_params=room(16),
        cost_estimate=pl.CostEstimate(flops=400000000, bytes_accessed=3000000, transcendentals=0),
        name="forward",
    )(*sources)
    partial, (labels, xi_hi, xi_lo), small = made[:4], made[4:7], made[7:16]
    xo_hi, xo_lo, z_hi, z_lo, ylane = made[16:]
    wide, weight, phases, table, wide1, wide2, bias2 = pl.pallas_call(
        prepare_kernel,
        out_shape=[
            shape((128, 128), f32),
            shape((512, 128), f32),
            shape((2, 16, 128), f32),
            shape((16, 128), f32),
            shape((512, 256), bf16),
            shape((128, 512), bf16),
            shape((128, 128), f32),
        ],
        in_specs=[vmem()] * 9,
        out_specs=[vmem()] * 7,
        compiler_params=room(8),
        cost_estimate=pl.CostEstimate(flops=200000000, bytes_accessed=1000000, transcendentals=0),
        name="prepare",
    )(*small)
    partial = rotate(partial)
    chunks = pl.pallas_call(
        gather_groups_kernel,
        out_shape=shape((256, 128), f32),
        in_specs=[vmem()] * 7,
        out_specs=vmem(),
        scratch_shapes=[pltpu.VMEM((4, 128, 128), f32)],
        compiler_params=room(8),
        name="gather_groups",
    )(phases, xi_hi, xi_lo, *partial)
    chunks = lax.all_to_all(chunks.reshape(64, 4, 128), "pen", 0, 0, tiled=True)
    mixed = pl.pallas_call(
        mix_kernel,
        out_shape=shape((256, 128), f32),
        in_specs=[vmem()] * 3,
        out_specs=vmem(),
        compiler_params=room(8),
        name="mix",
    )(chunks.reshape(256, 128), weight, wide)
    mixed = lax.all_to_all(mixed.reshape(64, 4, 128), "pen", 0, 0, tiled=True)
    modes = pl.pallas_call(
        scatter_groups_kernel,
        out_shape=[shape((128, 128), f32)] * 4,
        in_specs=[vmem()] * 4,
        out_specs=[vmem()] * 4,
        scratch_shapes=[pltpu.VMEM((4, 128, 128), f32)],
        compiler_params=room(8),
        name="scatter_groups",
    )(phases, xo_hi, xo_lo, mixed.reshape(256, 128))
    modes = rotate(modes)
    return pl.pallas_call(
        point_kernel,
        out_shape=shape((CH, LZ, LX, NY), bf16),
        grid=(STEPS,),
        in_specs=[vmem()] * 12,
        out_specs=pl.BlockSpec((CH, ZB, LX, NY), lambda i: (0, i, 0, 0)),
        scratch_shapes=[
            pltpu.VMEM((4, 512, 128), f32),
            pltpu.VMEM((2, 144, 512), bf16),
            pltpu.VMEM((2, 512, 512), f32),
            pltpu.VMEM((4, 128, 128), f32),
        ],
        compiler_params=room(24),
        name="point",
    )(*modes, z_hi, z_lo, ylane, labels, table, wide1, wide2, bias2)


def solution(mesh):
    return jax.shard_map(
        shards,
        mesh=mesh,
        in_specs=(
            P("grp", "pen", None),
            P(),
            P(("grp", "pen"), None, None, None, None),
            P(),
            P(),
            P(),
            P(),
            P(),
            P(),
        ),
        out_specs=P(None, "grp", "pen", None),
        check_vma=False,
    )
```

```python
import functools
import math

import jax
import jax.numpy as jnp
import ml_dtypes
import numpy as np
from jax import lax
from jax.experimental import pallas as pl
from jax.experimental.pallas import tpu as pltpu
from jax.sharding import PartitionSpec as P

NZ = 256
NX = 512
NY = 256
CH = 16
MODES = 16
NCLASS = 12
HIDDEN = 64
LZ = 64
LX = 8
ROWS = LZ * LX
ORDER = (0, 2, 1, 3)

highest = lax.Precision.HIGHEST
f32 = jnp.float32
bf16 = jnp.bfloat16
FREQ = np.where(np.arange(MODES) < 8, np.arange(MODES), np.arange(MODES) - MODES)


def split(values):
    hi = values.astype(ml_dtypes.bfloat16)
    lo = (values - hi.astype(np.float64)).astype(ml_dtypes.bfloat16)
    return hi, lo


def y_tables():
    product = np.remainder(FREQ[:, None] * np.arange(NY)[None, :], NY)
    angles = product.astype(np.float32) * np.float32(2.0 * math.pi / NY)
    cos = np.cos(angles).astype(ml_dtypes.bfloat16)
    sin = np.sin(angles).astype(ml_dtypes.bfloat16)
    return np.stack([cos, -sin], axis=1).reshape(2 * MODES, NY)


def z_tables():
    angles = 2.0 * np.pi * np.remainder(FREQ[None, :] * np.arange(LZ)[:, None], NZ) / NZ
    table = np.zeros((LZ, LX, 2, LX, MODES))
    for x in range(LX):
        table[:, x, 0, x] = np.cos(angles)
        table[:, x, 1, x] = np.sin(angles)
    return table.reshape(ROWS, 2 * LX * MODES)


def x_tables():
    angles = 2.0 * np.pi * np.remainder(FREQ[None, :] * np.arange(LX)[:, None], NX) / NX
    table = np.zeros((2, LX, MODES, MODES, MODES))
    for kz in range(MODES):
        table[0, :, kz, :, kz] = np.cos(angles)
        table[1, :, kz, :, kz] = np.sin(angles)
    table = table.reshape(2, LX * MODES, MODES, 4, 4)
    return table.transpose(0, 1, 4, 3, 2).reshape(2, LX * MODES, MODES * MODES)


def y_lanes(ytab):
    table = ytab.reshape(2, 2, 4, 2, NY)
    table = np.moveaxis(table, (0, 1, 2, 3), (0, 3, 1, 2))
    return np.repeat(table.reshape(2 * MODES, NY), 8, axis=0)


def pen_phases():
    turn = np.remainder(np.arange(64)[:, None] * FREQ[None, :], 64)
    angles = 2.0 * np.pi * turn / 64
    table = np.zeros((80, 128), np.float32)
    table[:64, 0:16] = np.cos(angles)
    table[:64, 16:32] = np.sin(angles)
    return table


def iota(shape, axis):
    return lax.broadcasted_iota(jnp.int32, shape, axis)


def times_j(tile):
    imag_lane = (iota(tile.shape, 1) // 16) % 2 == 1
    return jnp.where(imag_lane, pltpu.roll(tile, 16, 1), -pltpu.roll(tile, 112, 1))


def exchange(tiles):
    block = iota(tiles[0].shape, 1) // 32
    out = []
    for i in range(4):
        best = tiles[i]
        for j in range(4):
            if j != i:
                best = jnp.where(block == j, pltpu.roll(tiles[j], 32 * (j - i) % 128, 1), best)
        out.append(best)
    return out


def quarter_signs(shape):
    quarter = iota(shape, 0) % 4
    cos = jnp.where(quarter == 0, 1.0, jnp.where(quarter == 2, -1.0, 0.0))
    sin = jnp.where(quarter == 1, 1.0, jnp.where(quarter == 3, -1.0, 0.0))
    flip = jnp.where(quarter % 2 == 0, 1.0, -1.0)
    return cos, sin, flip


def to_parts(values):
    hi = values.astype(bf16)
    lo = (values - hi.astype(f32)).astype(bf16)
    return hi, lo


def dot(left, right, dims=((1,), (0,)), precision=None):
    return lax.dot_general(
        left, right, (dims, ((), ())), precision=precision, preferred_element_type=f32
    )


def three(hi, lo, right):
    right_hi, right_lo = to_parts(right)
    return dot(hi, right_hi) + dot(hi, right_lo) + dot(lo, right_hi)


def forward_kernel(
    occ, ytab, zt_hi, zt_lo, xi_hi, xi_lo, xo_hi, xo_lo, z_hi, z_lo, ylane, phase, emb, weight, pw,
    pb, w1, b1, w2, b2, own_ref, first_ref, second_ref, third_ref, label_ref, *rest
):
    held, (ytab_v, zt_hi_v, zt_lo_v, small_ref, rows_ref, tile_ref, sems) = rest[:16], rest[16:]
    pairs = [(occ.at[:, pl.ds(half * 128, 128)], label_ref.at[half, pl.ds(0, ROWS)]) for half in range(2)]
    pairs += [(ytab, ytab_v), (zt_hi, zt_hi_v), (zt_lo, zt_lo_v)]
    later = [xi_hi, xi_lo, emb, weight, pw, pb, w1, b1, w2, b2, phase]
    later += [xo_hi, xo_lo, z_hi, z_lo, ylane]
    pairs += list(zip(later, held))
    copies = [pltpu.make_async_copy(a, b, sems.at[i]) for i, (a, b) in enumerate(pairs)]
    for copy in copies[:5]:
        copy.start()
    for label in range(NCLASS, 16):
        for quarter in range(4):
            rows_ref[quarter, pl.ds(label, 32, stride=16), :] = jnp.zeros((32, 128), f32)
    for copy in copies[:3]:
        copy.wait()
    for copy in copies[5:]:
        copy.start()
    for half in range(2):
        small_ref[:, half * 128 : (half + 1) * 128] = label_ref[half, 0:ROWS].astype(f32).astype(bf16)
    for label in range(NCLASS):
        same = small_ref[...] == jnp.array(label, bf16)
        hot = jnp.where(same, jnp.array(1.0, bf16), jnp.array(0.0, bf16))
        part = dot(ytab_v[...], hot, ((1,), (1,)))
        for quarter in range(4):
            rows_ref[quarter, pl.ds(label, 32, stride=16), :] = part[
                :, quarter * 128 : (quarter + 1) * 128
            ]
    for copy in copies[3:5]:
        copy.wait()
    nt = ((1,), (1,))
    for pair in range(2):
        block = [rows_ref[quarter, pl.ds(pair * 256, 256), :] for quarter in range(4)]
        block_hi, block_lo = to_parts(jnp.concatenate(block, axis=1))
        full = (
            dot(zt_hi_v[...], block_hi, nt)
            + dot(zt_hi_v[...], block_lo, nt)
            + dot(zt_lo_v[...], block_hi, nt)
        )
        for half in range(2):
            tile = full[:, half * 128 : (half + 1) * 128]
            tile_ref[pair * 2 + half] = tile[:128] - times_j(tile[128:])
    here = lax.axis_index("grp")
    for k, ref in zip(ORDER, (own_ref, first_ref, second_ref, third_ref)):
        ref[...] = tile_ref[(here + k) % 4]
    for copy in copies[5:]:
        copy.wait()


def prepare_kernel(
    emb_v, weight_v, pw_v, pb_v, w1_v, b1_v, w2_v, b2_v, phase_v,
    wide_ref, rep_ref, phase_out, table_ref, wide1_ref, wide2_ref, bias2_ref,
):
    left = jnp.where(iota((128, NCLASS), 0) % 16 == iota((128, NCLASS), 1), 1.0, 0.0).astype(f32)
    right = jnp.where(iota((16, 128), 1) % 16 == iota((16, 128), 0), 1.0, 0.0).astype(f32)
    lifted = dot(left, emb_v[...], precision=highest)
    wide = dot(right, lifted, ((0,), (1,)), highest)
    wide_ref[...] = jnp.where(
        iota((128, 128), 0) // 16 == iota((128, 128), 1) // 16, wide, 0.0
    )
    rep_ref[...] = jnp.concatenate([weight_v[...]] * 8, axis=1)
    row = phase_v[pl.ds(lax.axis_index("pen"), 16, stride=0), :]
    for half in range(2):
        pick = iota((16, 128), 1) == iota((16, 128), 0) + 16 * half
        column = jnp.sum(jnp.where(pick, row, 0.0), axis=1, keepdims=True)
        phase_out[half] = jnp.broadcast_to(column, (16, 128))

    table = dot(pw_v[...], emb_v[...], ((0,), (1,)), highest)
    spread = jnp.where(
        iota((NCLASS, 128), 0) == iota((NCLASS, 128), 1), 1.0, 0.0
    ).astype(f32)
    eye = iota((16, 16), 0) == iota((16, 16), 1)
    bias = jnp.sum(jnp.where(eye, pb_v[...], 0.0), axis=1, keepdims=True)
    table_ref[...] = dot(table, spread, precision=highest) + bias
    r1 = jnp.where(iota((64, 64), 0) == iota((64, 64), 1), 1.0, 0.0)
    r2 = jnp.where(iota((16, 128), 1) % 16 == iota((16, 128), 0), 0.5, 0.0).astype(bf16)
    full1 = dot(dot(r1.astype(bf16), w1_v[...], ((1,), (1,))).astype(bf16), r2)
    col1 = jnp.broadcast_to(jnp.sum(r1 * b1_v[...], axis=1, keepdims=True), (64, 128))
    first = col1.astype(bf16).astype(f32)
    second = (col1 - first).astype(bf16).astype(f32)
    third = col1 - first - second
    lane = iota((64, 128), 1)
    extra = jnp.where(
        lane == 0, first, jnp.where(lane == 1, second, jnp.where(lane == 2, third, 0.0))
    ).astype(bf16)
    for x in range(LX):
        wide1_ref[x * 64 : x * 64 + 64, 0:128] = jnp.where(lane // 16 == x, full1, 0.0).astype(bf16)
        wide1_ref[x * 64 : x * 64 + 64, 128:256] = extra
    r3 = jnp.where(iota((128, 16), 0) // 8 == iota((128, 16), 1), 1.0, 0.0)
    r4 = jnp.where(iota((64, 128), 1) % 64 == iota((64, 128), 0), 0.5, 0.0).astype(bf16)
    full2 = dot(dot(r3.astype(bf16), w2_v[...]).astype(bf16), r4)
    x_row = iota((128, 128), 0) % 8
    x_lane = iota((128, 128), 1) // 64
    for tile in range(4):
        wide2_ref[:, tile * 128 : tile * 128 + 128] = jnp.where(
            x_row == x_lane + 2 * tile, full2, 0.0
        ).astype(bf16)
    col2 = jnp.sum(r3 * b2_v[...], axis=1, keepdims=True)
    bias2_ref[...] = jnp.broadcast_to(col2, (128, 128))


def gather_groups_kernel(phase_ref, hi_ref, lo_ref, own_ref, first_ref, second_ref, third_ref, out_ref, in_ref):
    here = lax.axis_index("grp")
    for k, ref in zip(ORDER, (own_ref, first_ref, second_ref, third_ref)):
        in_ref[(here + 4 - k) % 4] = ref[...]
    cos, sin, flip = quarter_signs((128, 128))
    real = in_ref[0] + flip * in_ref[2] + cos * (in_ref[1] + in_ref[3])
    imag = sin * (in_ref[3] - in_ref[1])
    real = real + times_j(imag)
    both = three(hi_ref[...], lo_ref[...], jnp.concatenate([real, -times_j(real)], axis=0))
    turned = times_j(both)
    for kz_hi in range(4):
        tiles = []
        for kz_lo in range(4):
            rows = slice((kz_lo * 4 + kz_hi) * 16, (kz_lo * 4 + kz_hi) * 16 + 16)
            tiles.append(both[rows] * phase_ref[0] - turned[rows] * phase_ref[1])
        for q, tile in enumerate(exchange(tiles)):
            out_ref[pl.ds(q * 64 + kz_hi, 16, stride=4), :] = tile


def mix_kernel(in_ref, weight_ref, wide_ref, out_ref):
    parts = [in_ref[pl.ds(step * 8, 8), :] for step in range(32)]
    while len(parts) > 1:
        parts = [a + b for a, b in zip(parts[0::2], parts[1::2])]
    total = parts[0] + pltpu.roll(parts[0], 4, 0)
    columns = dot(wide_ref[...], total, ((1,), (1,)), highest)
    row = iota((128, 128), 0)
    lane = iota((128, 128), 1)
    near = row // 32 == lane // 32
    row_imag = (row // 16) % 2 == 1
    lane_imag = (lane // 16) % 2 == 1
    flipped = jnp.concatenate(
        [columns[(n ^ 1) * 16 : (n ^ 1) * 16 + 16] for n in range(8)], axis=0
    )
    signed = jnp.where(row_imag[:, 0:8], -columns, columns)
    out = []
    for kz_hi in range(4):
        same = jnp.broadcast_to(signed[:, kz_hi : kz_hi + 1], (128, 128))
        other = jnp.broadcast_to(flipped[:, kz_hi : kz_hi + 1], (128, 128))
        factor = jnp.where(near, jnp.where(lane_imag, other, same), 0.0)
        product = factor * weight_ref[pl.ds(kz_hi * 128, 128), :]
        out.append(jnp.sum(product, axis=0, keepdims=True))
    tile = jnp.concatenate(out + out, axis=0) * (1.0 / (NZ * NX * NY))
    for step in range(32):
        out_ref[pl.ds(step * 8, 8), :] = tile


def scatter_groups_kernel(phase_ref, hi_ref, lo_ref, in_ref, own_ref, first_ref, second_ref, third_ref, out_ref):
    real = [None] * 16
    imag = [None] * 16
    for kz_hi in range(4):
        tiles = [in_ref[pl.ds(q * 64 + kz_hi, 16, stride=4), :] for q in range(4)]
        for kz_lo, tile in enumerate(exchange(tiles)):
            turned = times_j(tile)
            real[kz_lo * 4 + kz_hi] = tile * phase_ref[0] + turned * phase_ref[1]
            imag[kz_lo * 4 + kz_hi] = turned * phase_ref[0] - tile * phase_ref[1]
    real = three(hi_ref[...], lo_ref[...], jnp.concatenate(real + imag, axis=0))
    imag = times_j(real)
    cos, sin, flip = quarter_signs((128, 128))
    out_ref[0] = real
    out_ref[1] = cos * real + sin * imag
    out_ref[2] = flip * real
    out_ref[3] = cos * real - sin * imag
    here = lax.axis_index("grp")
    for k, ref in zip(ORDER, (own_ref, first_ref, second_ref, third_ref)):
        ref[...] = out_ref[(here + k) % 4]


def twice_gelu(values):
    return values + values * lax.erf(values * np.float32(math.sqrt(0.5)))


def lookup(table, index):
    numbers = lax.GatherDimensionNumbers(
        offset_dims=(),
        collapsed_slice_dims=(1,),
        start_index_map=(1,),
        operand_batching_dims=(0,),
        start_indices_batching_dims=(0,),
    )
    return lax.gather(
        table,
        index[..., None],
        numbers,
        slice_sizes=(1, 1),
        mode=lax.GatherScatterMode.PROMISE_IN_BOUNDS,
    )


ZB = 16
STEPS = LZ // ZB


def point_kernel(
    own_ref, first_ref, second_ref, third_ref, hi_ref, lo_ref, ytab_ref, label_ref, table_ref, wide1_ref, wide2_ref, bias2_ref,
    out_ref, planes_ref, act_ref, pre_ref, modes_ref,
):
    step = pl.program_id(0)

    def finish(sub):
        slot = sub % 2
        hidden = twice_gelu(pre_ref[slot]).astype(bf16)
        bias2 = jnp.concatenate([bias2_ref[...]] * 4, axis=1)
        encoded = (dot(wide2_ref[...], hidden) + bias2).astype(bf16)
        for half in range(2):
            tile = encoded[:, half * 256 : half * 256 + 256]
            out_ref[:, sub * 2 + half] = tile.reshape(16, 8, 256)

    def transform(pair):
        own = jnp.where(iota((16, 256), 0) % 8 == iota((16, 256), 1) % 8, 1.0, 0.0).astype(bf16)
        left = []
        for row in range(16):
            base = pl.multiple_of(pair * 16, 16) + row
            rows = [planes_ref[t, pl.ds(base, 8, stride=0), :] for t in range(4)]
            block = jnp.concatenate(
                [jnp.concatenate(rows[0:2], axis=1), jnp.concatenate(rows[2:4], axis=1)],
                axis=0,
            )
            left.append(block.astype(bf16) * own)
        return dot(jnp.concatenate(left, axis=0), ytab_ref[...])

    def activate(spatial, pair, slot):
        low = table_ref[0:8, :]
        high = table_ref[8:16, :]
        for row in range(16):
            base = pl.multiple_of(pair * 16, 16) + row
            for half in range(2):
                label = label_ref[half, pl.ds(base, 8, stride=0), :]
                point = jnp.concatenate(
                    [
                        lookup(low, label),
                        lookup(high, label),
                    ],
                    axis=0,
                )
                total = spatial[row * 16 : row * 16 + 16, half * 128 : half * 128 + 128] + point
                lane = (row // 8) * 256 + half * 128
                place = (row % 8) * 16
                act_ref[slot, place : place + 16, lane : lane + 128] = twice_gelu(total).astype(bf16)

    def expand(slot):
        pre_ref[slot] = dot(wide1_ref[:, 0:144], act_ref[slot])

    @pl.when(step == 0)
    def _():
        here = lax.axis_index("grp")
        for k, ref in zip(ORDER, (own_ref, first_ref, second_ref, third_ref)):
            modes_ref[(here + 4 - k) % 4] = ref[...]
        high_lane = (iota((128, 128), 1) // 8) % 2 == 1
        for c_hi in range(2):
            tiles = []
            for pair in range(2):
                even = modes_ref[2 * pair]
                odd = modes_ref[2 * pair + 1]
                if c_hi == 0:
                    tile = jnp.where(high_lane, pltpu.roll(odd, 8, 1), even)
                else:
                    tile = jnp.where(high_lane, odd, pltpu.roll(even, 120, 1))
                tiles.append(jnp.concatenate([tile, times_j(tile)], axis=0))
            full = three(hi_ref[...], lo_ref[...], jnp.concatenate(tiles, axis=1))
            full = full.astype(bf16).astype(f32)
            planes_ref[c_hi * 2, 0:ROWS] = full[:, 0:128]
            planes_ref[c_hi * 2 + 1, 0:ROWS] = full[:, 128:256]
        for slot in range(2):
            act_ref[slot, 128:144] = jnp.ones((16, 512), bf16)
            activate(transform(slot), slot, slot)
        expand(0)

    @pl.when(step < STEPS - 1)
    def _():
        for sub in range(ZB // 2):
            pair = step * (ZB // 2) + sub + 2
            spatial = transform(pair)
            expand(1 - sub % 2)
            finish(sub)
            activate(spatial, pair, sub % 2)

    @pl.when(step == STEPS - 1)
    def _():
        for sub in range(ZB // 2):
            pair = step * (ZB // 2) + sub + 2
            if sub < ZB // 2 - 2:
                spatial = transform(pair)
            if sub < ZB // 2 - 1:
                expand(1 - sub % 2)
            finish(sub)
            if sub < ZB // 2 - 2:
                activate(spatial, pair, sub % 2)


def room(mib):
    return pltpu.CompilerParams(vmem_limit_bytes=mib * 1024 * 1024)


def vmem():
    return pl.BlockSpec(memory_space=pltpu.VMEM)


def rotate(tiles):
    moved = [tiles[0]]
    for k, tile in zip(ORDER[1:], tiles[1:]):
        moved.append(lax.ppermute(tile, "grp", [(i, (i + k) % 4) for i in range(4)]))
    return moved


def far(*values):
    return [pltpu.with_memory_space_constraint(jnp.asarray(v), pltpu.HBM) for v in values]


def shards(
    occupancy,
    embedding,
    spectral_weight,
    point_weight,
    point_bias,
    expand_weight,
    expand_bias,
    reduce_weight,
    reduce_bias,
):
    ytab = y_tables()
    z_hi, z_lo = split(z_tables())
    x_hi, x_lo = split(x_tables())
    shape = jax.ShapeDtypeStruct
    sources = far(
        occupancy.reshape(ROWS, NY),
        ytab,
        z_hi.T.copy(),
        z_lo.T.copy(),
        x_hi.transpose(2, 0, 1).reshape(256, 256),
        x_lo.transpose(2, 0, 1).reshape(256, 256),
        x_hi.transpose(1, 0, 2).reshape(128, 512),
        x_lo.transpose(1, 0, 2).reshape(128, 512),
        z_hi,
        z_lo,
        y_lanes(ytab),
        pen_phases(),
        embedding,
        spectral_weight.reshape(512, 16),
        point_weight,
        point_bias.reshape(1, CH),
        expand_weight,
        expand_bias.reshape(1, HIDDEN),
        reduce_weight.T,
        reduce_bias.reshape(1, CH),
    )
    made = pl.pallas_call(
        forward_kernel,
        out_shape=[shape((128, 128), f32)] * 4
        + [
            shape((2, ROWS + 8, 128), jnp.int32),
            shape((256, 256), bf16),
            shape((256, 256), bf16),
            shape((NCLASS, CH), f32),
            shape((512, 16), f32),
            shape((CH, CH), f32),
            shape((1, CH), f32),
            shape((CH, HIDDEN), bf16),
            shape((1, HIDDEN), f32),
            shape((CH, HIDDEN), bf16),
            shape((1, CH), f32),
            shape((80, 128), f32),
            shape((128, 512), bf16),
            shape((128, 512), bf16),
            shape((512, 256), bf16),
            shape((512, 256), bf16),
            shape((256, 256), bf16),
        ],
        in_specs=[pl.BlockSpec(memory_space=pltpu.HBM)] * 20,
        out_specs=[vmem()] * 21,
        scratch_shapes=[
            pltpu.VMEM((32, 256), bf16),
            pltpu.VMEM((256, 512), bf16),
            pltpu.VMEM((256, 512), bf16),
            pltpu.VMEM((ROWS, NY), bf16),
            pltpu.VMEM((4, 512, 128), f32),
            pltpu.VMEM((4, 128, 128), f32),
            pltpu.SemaphoreType.DMA((21,)),
        ],
        compiler_params=room(16),
        cost_estimate=pl.CostEstimate(flops=400000000, bytes_accessed=3000000, transcendentals=0),
        name="forward",
    )(*sources)
    partial, (labels, xi_hi, xi_lo), small = made[:4], made[4:7], made[7:16]
    xo_hi, xo_lo, z_hi, z_lo, ylane = made[16:]
    wide, weight, phases, table, wide1, wide2, bias2 = pl.pallas_call(
        prepare_kernel,
        out_shape=[
            shape((128, 128), f32),
            shape((512, 128), f32),
            shape((2, 16, 128), f32),
            shape((16, 128), f32),
            shape((512, 256), bf16),
            shape((128, 512), bf16),
            shape((128, 128), f32),
        ],
        in_specs=[vmem()] * 9,
        out_specs=[vmem()] * 7,
        compiler_params=room(8),
        cost_estimate=pl.CostEstimate(flops=200000000, bytes_accessed=1000000, transcendentals=0),
        name="prepare",
    )(*small)
    partial = rotate(partial)
    chunks = pl.pallas_call(
        gather_groups_kernel,
        out_shape=shape((256, 128), f32),
        in_specs=[vmem()] * 7,
        out_specs=vmem(),
        scratch_shapes=[pltpu.VMEM((4, 128, 128), f32)],
        compiler_params=room(8),
        name="gather_groups",
    )(phases, xi_hi, xi_lo, *partial)
    chunks = lax.all_to_all(chunks.reshape(64, 4, 128), "pen", 0, 0, tiled=True)
    mixed = pl.pallas_call(
        mix_kernel,
        out_shape=shape((256, 128), f32),
        in_specs=[vmem()] * 3,
        out_specs=vmem(),
        compiler_params=room(8),
        name="mix",
    )(chunks.reshape(256, 128), weight, wide)
    mixed = lax.all_to_all(mixed.reshape(64, 4, 128), "pen", 0, 0, tiled=True)
    modes = pl.pallas_call(
        scatter_groups_kernel,
        out_shape=[shape((128, 128), f32)] * 4,
        in_specs=[vmem()] * 4,
        out_specs=[vmem()] * 4,
        scratch_shapes=[pltpu.VMEM((4, 128, 128), f32)],
        compiler_params=room(8),
        name="scatter_groups",
    )(phases, xo_hi, xo_lo, mixed.reshape(256, 128))
    modes = rotate(modes)
    return pl.pallas_call(
        point_kernel,
        out_shape=shape((CH, LZ, LX, NY), bf16),
        grid=(STEPS,),
        in_specs=[vmem()] * 12,
        out_specs=pl.BlockSpec((CH, ZB, LX, NY), lambda i: (0, i, 0, 0)),
        scratch_shapes=[
            pltpu.VMEM((4, ROWS + 8, 128), f32),
            pltpu.VMEM((2, 144, 512), bf16),
            pltpu.VMEM((2, 512, 512), f32),
            pltpu.VMEM((4, 128, 128), f32),
        ],
        compiler_params=room(24),
        name="point",
    )(*modes, z_hi, z_lo, ylane, labels, table, wide1, wide2, bias2)


def solution(mesh):
    return jax.shard_map(
        shards,
        mesh=mesh,
        in_specs=(
            P("grp", "pen", None),
            P(),
            P(("grp", "pen"), None, None, None, None),
            P(),
            P(),
            P(),
            P(),
            P(),
            P(),
        ),
        out_specs=P(None, "grp", "pen", None),
        check_vma=False,
    )
```

```python
import functools
import math

import jax
import jax.numpy as jnp
import ml_dtypes
import numpy as np
from jax import lax
from jax.experimental import pallas as pl
from jax.experimental.pallas import tpu as pltpu
from jax.sharding import PartitionSpec as P

NZ = 256
NX = 512
NY = 256
CH = 16
MODES = 16
NCLASS = 12
HIDDEN = 64
LZ = 64
LX = 8
ROWS = LZ * LX
ORDER = (0, 2, 1, 3)

highest = lax.Precision.HIGHEST
f32 = jnp.float32
bf16 = jnp.bfloat16
FREQ = np.where(np.arange(MODES) < 8, np.arange(MODES), np.arange(MODES) - MODES)


def split(values):
    hi = values.astype(ml_dtypes.bfloat16)
    lo = (values - hi.astype(np.float64)).astype(ml_dtypes.bfloat16)
    return hi, lo


def y_tables():
    product = np.remainder(FREQ[:, None] * np.arange(NY)[None, :], NY)
    angles = product.astype(np.float32) * np.float32(2.0 * math.pi / NY)
    cos = np.cos(angles).astype(ml_dtypes.bfloat16)
    sin = np.sin(angles).astype(ml_dtypes.bfloat16)
    return np.stack([cos, -sin], axis=1).reshape(2 * MODES, NY)


def z_tables():
    angles = 2.0 * np.pi * np.remainder(FREQ[None, :] * np.arange(LZ)[:, None], NZ) / NZ
    table = np.zeros((LZ, LX, 2, LX, MODES))
    for x in range(LX):
        table[:, x, 0, x] = np.cos(angles)
        table[:, x, 1, x] = np.sin(angles)
    return table.reshape(ROWS, 2 * LX * MODES)


def x_tables():
    angles = 2.0 * np.pi * np.remainder(FREQ[None, :] * np.arange(LX)[:, None], NX) / NX
    table = np.zeros((2, LX, MODES, MODES, MODES))
    for kz in range(MODES):
        table[0, :, kz, :, kz] = np.cos(angles)
        table[1, :, kz, :, kz] = np.sin(angles)
    table = table.reshape(2, LX * MODES, MODES, 4, 4)
    return table.transpose(0, 1, 4, 3, 2).reshape(2, LX * MODES, MODES * MODES)


def y_lanes(ytab):
    table = ytab.reshape(2, 2, 4, 2, NY)
    table = np.moveaxis(table, (0, 1, 2, 3), (0, 3, 1, 2))
    return np.repeat(table.reshape(2 * MODES, NY), 8, axis=0)


def pen_phases():
    turn = np.remainder(np.arange(64)[:, None] * FREQ[None, :], 64)
    angles = 2.0 * np.pi * turn / 64
    table = np.zeros((80, 128), np.float32)
    table[:64, 0:16] = np.cos(angles)
    table[:64, 16:32] = np.sin(angles)
    return table


def iota(shape, axis):
    return lax.broadcasted_iota(jnp.int32, shape, axis)


def times_j(tile):
    imag_lane = (iota(tile.shape, 1) // 16) % 2 == 1
    return jnp.where(imag_lane, pltpu.roll(tile, 16, 1), -pltpu.roll(tile, 112, 1))


def exchange(tiles):
    block = iota(tiles[0].shape, 1) // 32
    out = []
    for i in range(4):
        best = tiles[i]
        for j in range(4):
            if j != i:
                best = jnp.where(block == j, pltpu.roll(tiles[j], 32 * (j - i) % 128, 1), best)
        out.append(best)
    return out


def quarter_signs(shape):
    quarter = iota(shape, 0) % 4
    cos = jnp.where(quarter == 0, 1.0, jnp.where(quarter == 2, -1.0, 0.0))
    sin = jnp.where(quarter == 1, 1.0, jnp.where(quarter == 3, -1.0, 0.0))
    flip = jnp.where(quarter % 2 == 0, 1.0, -1.0)
    return cos, sin, flip


def to_parts(values):
    hi = values.astype(bf16)
    lo = (values - hi.astype(f32)).astype(bf16)
    return hi, lo


def dot(left, right, dims=((1,), (0,)), precision=None):
    return lax.dot_general(
        left, right, (dims, ((), ())), precision=precision, preferred_element_type=f32
    )


def three(hi, lo, right):
    right_hi, right_lo = to_parts(right)
    return dot(hi, right_hi) + dot(hi, right_lo) + dot(lo, right_hi)


def forward_kernel(
    occ, ytab, zt_hi, zt_lo, xi_hi, xi_lo, xo_hi, xo_lo, z_hi, z_lo, ylane, phase, emb, weight, pw,
    pb, w1, b1, w2, b2, own_ref, first_ref, second_ref, third_ref, label_ref, *rest
):
    held, (ytab_v, zt_hi_v, zt_lo_v, small_ref, rows_ref, tile_ref, sems) = rest[:16], rest[16:]
    pairs = [(occ.at[:, pl.ds(half * 128, 128)], label_ref.at[half, pl.ds(0, ROWS)]) for half in range(2)]
    pairs += [(ytab, ytab_v), (zt_hi, zt_hi_v), (zt_lo, zt_lo_v)]
    later = [xi_hi, xi_lo, emb, weight, pw, pb, w1, b1, w2, b2, phase]
    later += [xo_hi, xo_lo, z_hi, z_lo, ylane]
    pairs += list(zip(later, held))
    copies = [pltpu.make_async_copy(a, b, sems.at[i]) for i, (a, b) in enumerate(pairs)]
    for copy in copies[:5]:
        copy.start()
    for label in range(NCLASS, 16):
        for quarter in range(4):
            rows_ref[quarter, pl.ds(label, 32, stride=16), :] = jnp.zeros((32, 128), f32)
    for copy in copies[:3]:
        copy.wait()
    for copy in copies[5:]:
        copy.start()
    for half in range(2):
        small_ref[:, half * 128 : (half + 1) * 128] = label_ref[half, 0:ROWS].astype(f32).astype(bf16)
    for label in range(NCLASS):
        same = small_ref[...] == jnp.array(label, bf16)
        hot = jnp.where(same, jnp.array(1.0, bf16), jnp.array(0.0, bf16))
        part = dot(ytab_v[...], hot, ((1,), (1,)))
        for quarter in range(4):
            rows_ref[quarter, pl.ds(label, 32, stride=16), :] = part[
                :, quarter * 128 : (quarter + 1) * 128
            ]
    for copy in copies[3:5]:
        copy.wait()
    nt = ((1,), (1,))
    for pair in range(2):
        block = [rows_ref[quarter, pl.ds(pair * 256, 256), :] for quarter in range(4)]
        block_hi, block_lo = to_parts(jnp.concatenate(block, axis=1))
        full = (
            dot(zt_hi_v[...], block_hi, nt)
            + dot(zt_hi_v[...], block_lo, nt)
            + dot(zt_lo_v[...], block_hi, nt)
        )
        for half in range(2):
            tile = full[:, half * 128 : (half + 1) * 128]
            tile_ref[pair * 2 + half] = tile[:128] - times_j(tile[128:])
    here = lax.axis_index("grp")
    for k, ref in zip(ORDER, (own_ref, first_ref, second_ref, third_ref)):
        ref[...] = tile_ref[(here + k) % 4]
    for copy in copies[5:]:
        copy.wait()


def prepare_kernel(
    emb_v, weight_v, pw_v, pb_v, w1_v, b1_v, w2_v, b2_v, phase_v,
    wide_ref, rep_ref, phase_out, table_ref, wide1_ref, wide2_ref, bias2_ref,
):
    left = jnp.where(iota((128, NCLASS), 0) % 16 == iota((128, NCLASS), 1), 1.0, 0.0).astype(f32)
    right = jnp.where(iota((16, 128), 1) % 16 == iota((16, 128), 0), 1.0, 0.0).astype(f32)
    lifted = dot(left, emb_v[...], precision=highest)
    wide = dot(right, lifted, ((0,), (1,)), highest)
    wide_ref[...] = jnp.where(
        iota((128, 128), 0) // 16 == iota((128, 128), 1) // 16, wide, 0.0
    )
    rep_ref[...] = jnp.concatenate([weight_v[...]] * 8, axis=1)
    row = phase_v[pl.ds(lax.axis_index("pen"), 16, stride=0), :]
    for half in range(2):
        pick = iota((16, 128), 1) == iota((16, 128), 0) + 16 * half
        column = jnp.sum(jnp.where(pick, row, 0.0), axis=1, keepdims=True)
        phase_out[half] = jnp.broadcast_to(column, (16, 128))

    table = dot(pw_v[...], emb_v[...], ((0,), (1,)), highest)
    spread = jnp.where(
        iota((NCLASS, 128), 0) == iota((NCLASS, 128), 1), 1.0, 0.0
    ).astype(f32)
    eye = iota((16, 16), 0) == iota((16, 16), 1)
    bias = jnp.sum(jnp.where(eye, pb_v[...], 0.0), axis=1, keepdims=True)
    table_ref[...] = dot(table, spread, precision=highest) + bias
    r1 = jnp.where(iota((64, 64), 0) == iota((64, 64), 1), 1.0, 0.0)
    r2 = jnp.where(iota((16, 128), 1) % 16 == iota((16, 128), 0), 0.5, 0.0).astype(bf16)
    full1 = dot(dot(r1.astype(bf16), w1_v[...], ((1,), (1,))).astype(bf16), r2)
    col1 = jnp.broadcast_to(jnp.sum(r1 * b1_v[...], axis=1, keepdims=True), (64, 128))
    first = col1.astype(bf16).astype(f32)
    second = (col1 - first).astype(bf16).astype(f32)
    third = col1 - first - second
    lane = iota((64, 128), 1)
    extra = jnp.where(
        lane == 0, first, jnp.where(lane == 1, second, jnp.where(lane == 2, third, 0.0))
    ).astype(bf16)
    for x in range(LX):
        wide1_ref[x * 64 : x * 64 + 64, 0:128] = jnp.where(lane // 16 == x, full1, 0.0).astype(bf16)
        wide1_ref[x * 64 : x * 64 + 64, 128:256] = extra
    r3 = jnp.where(iota((128, 16), 0) // 8 == iota((128, 16), 1), 1.0, 0.0)
    r4 = jnp.where(iota((64, 128), 1) % 64 == iota((64, 128), 0), 0.5, 0.0).astype(bf16)
    full2 = dot(dot(r3.astype(bf16), w2_v[...]).astype(bf16), r4)
    x_row = iota((128, 128), 0) % 8
    x_lane = iota((128, 128), 1) // 64
    for tile in range(4):
        wide2_ref[:, tile * 128 : tile * 128 + 128] = jnp.where(
            x_row == x_lane + 2 * tile, full2, 0.0
        ).astype(bf16)
    col2 = jnp.sum(r3 * b2_v[...], axis=1, keepdims=True)
    bias2_ref[...] = jnp.broadcast_to(col2, (128, 128))


def gather_groups_kernel(phase_ref, hi_ref, lo_ref, own_ref, first_ref, second_ref, third_ref, out_ref, in_ref):
    here = lax.axis_index("grp")
    for k, ref in zip(ORDER, (own_ref, first_ref, second_ref, third_ref)):
        in_ref[(here + 4 - k) % 4] = ref[...]
    cos, sin, flip = quarter_signs((128, 128))
    real = in_ref[0] + flip * in_ref[2] + cos * (in_ref[1] + in_ref[3])
    imag = sin * (in_ref[3] - in_ref[1])
    real = real + times_j(imag)
    both = three(hi_ref[...], lo_ref[...], jnp.concatenate([real, -times_j(real)], axis=0))
    turned = times_j(both)
    for kz_hi in range(4):
        tiles = []
        for kz_lo in range(4):
            rows = slice((kz_lo * 4 + kz_hi) * 16, (kz_lo * 4 + kz_hi) * 16 + 16)
            tiles.append(both[rows] * phase_ref[0] - turned[rows] * phase_ref[1])
        for q, tile in enumerate(exchange(tiles)):
            out_ref[pl.ds(q * 64 + kz_hi, 16, stride=4), :] = tile


def mix_kernel(in_ref, weight_ref, wide_ref, out_ref):
    parts = [in_ref[pl.ds(step * 8, 8), :] for step in range(32)]
    while len(parts) > 1:
        parts = [a + b for a, b in zip(parts[0::2], parts[1::2])]
    total = parts[0] + pltpu.roll(parts[0], 4, 0)
    columns = dot(wide_ref[...], total, ((1,), (1,)), highest)
    row = iota((128, 128), 0)
    lane = iota((128, 128), 1)
    near = row // 32 == lane // 32
    row_imag = (row // 16) % 2 == 1
    lane_imag = (lane // 16) % 2 == 1
    flipped = jnp.concatenate(
        [columns[(n ^ 1) * 16 : (n ^ 1) * 16 + 16] for n in range(8)], axis=0
    )
    signed = jnp.where(row_imag[:, 0:8], -columns, columns)
    out = []
    for kz_hi in range(4):
        same = jnp.broadcast_to(signed[:, kz_hi : kz_hi + 1], (128, 128))
        other = jnp.broadcast_to(flipped[:, kz_hi : kz_hi + 1], (128, 128))
        factor = jnp.where(near, jnp.where(lane_imag, other, same), 0.0)
        product = factor * weight_ref[pl.ds(kz_hi * 128, 128), :]
        out.append(jnp.sum(product, axis=0, keepdims=True))
    tile = jnp.concatenate(out + out, axis=0) * (1.0 / (NZ * NX * NY))
    for step in range(32):
        out_ref[pl.ds(step * 8, 8), :] = tile


def scatter_groups_kernel(phase_ref, hi_ref, lo_ref, in_ref, own_ref, first_ref, second_ref, third_ref, out_ref):
    real = [None] * 16
    imag = [None] * 16
    for kz_hi in range(4):
        tiles = [in_ref[pl.ds(q * 64 + kz_hi, 16, stride=4), :] for q in range(4)]
        for kz_lo, tile in enumerate(exchange(tiles)):
            turned = times_j(tile)
            real[kz_lo * 4 + kz_hi] = tile * phase_ref[0] + turned * phase_ref[1]
            imag[kz_lo * 4 + kz_hi] = turned * phase_ref[0] - tile * phase_ref[1]
    real = three(hi_ref[...], lo_ref[...], jnp.concatenate(real + imag, axis=0))
    imag = times_j(real)
    cos, sin, flip = quarter_signs((128, 128))
    out_ref[0] = real
    out_ref[1] = cos * real + sin * imag
    out_ref[2] = flip * real
    out_ref[3] = cos * real - sin * imag
    here = lax.axis_index("grp")
    for k, ref in zip(ORDER, (own_ref, first_ref, second_ref, third_ref)):
        ref[...] = out_ref[(here + k) % 4]


def twice_gelu(values):
    return values + values * lax.erf(values * np.float32(math.sqrt(0.5)))


def lookup(table, index):
    numbers = lax.GatherDimensionNumbers(
        offset_dims=(),
        collapsed_slice_dims=(1,),
        start_index_map=(1,),
        operand_batching_dims=(0,),
        start_indices_batching_dims=(0,),
    )
    return lax.gather(
        table,
        index[..., None],
        numbers,
        slice_sizes=(1, 1),
        mode=lax.GatherScatterMode.PROMISE_IN_BOUNDS,
    )


ZB = 16
STEPS = LZ // ZB


def point_kernel(
    own_ref, first_ref, second_ref, third_ref, hi_ref, lo_ref, ytab_ref, label_ref, table_ref, wide1_ref, wide2_ref, bias2_ref,
    out_ref, planes_ref, act_ref, pre_ref, modes_ref,
):
    step = pl.program_id(0)

    def finish(sub):
        slot = sub % 2
        hidden = twice_gelu(pre_ref[slot]).astype(bf16)
        bias2 = jnp.concatenate([bias2_ref[...]] * 4, axis=1)
        encoded = (dot(wide2_ref[...], hidden) + bias2).astype(bf16)
        for half in range(2):
            tile = encoded[:, half * 256 : half * 256 + 256]
            out_ref[:, sub * 2 + half] = tile.reshape(16, 8, 256)

    def transform(pair, count):
        own = jnp.where(iota((16, 256), 0) % 8 == iota((16, 256), 1) % 8, 1.0, 0.0).astype(bf16)
        left = []
        for row in range(count):
            base = pl.multiple_of(pair * 16, 16) + row
            rows = [planes_ref[t, pl.ds(base, 8, stride=0), :] for t in range(4)]
            block = jnp.concatenate(
                [jnp.concatenate(rows[0:2], axis=1), jnp.concatenate(rows[2:4], axis=1)],
                axis=0,
            )
            left.append(block.astype(bf16) * own)
        return dot(jnp.concatenate(left, axis=0), ytab_ref[...])

    def activate(spatial, pair, slot):
        low = table_ref[0:8, :]
        high = table_ref[8:16, :]
        for row in range(16):
            base = pl.multiple_of(pair * 16, 16) + row
            for half in range(2):
                label = label_ref[half, pl.ds(base, 8, stride=0), :]
                point = jnp.concatenate(
                    [
                        lookup(low, label),
                        lookup(high, label),
                    ],
                    axis=0,
                )
                total = spatial[row * 16 : row * 16 + 16, half * 128 : half * 128 + 128] + point
                lane = (row // 8) * 256 + half * 128
                place = (row % 8) * 16
                act_ref[slot, place : place + 16, lane : lane + 128] = twice_gelu(total).astype(bf16)

    def expand(slot):
        pre_ref[slot] = dot(wide1_ref[:, 0:144], act_ref[slot])

    @pl.when(step == 0)
    def _():
        here = lax.axis_index("grp")
        for k, ref in zip(ORDER, (own_ref, first_ref, second_ref, third_ref)):
            modes_ref[(here + 4 - k) % 4] = ref[...]
        high_lane = (iota((128, 128), 1) // 8) % 2 == 1
        for c_hi in range(2):
            tiles = []
            for pair in range(2):
                even = modes_ref[2 * pair]
                odd = modes_ref[2 * pair + 1]
                if c_hi == 0:
                    tile = jnp.where(high_lane, pltpu.roll(odd, 8, 1), even)
                else:
                    tile = jnp.where(high_lane, odd, pltpu.roll(even, 120, 1))
                tiles.append(jnp.concatenate([tile, times_j(tile)], axis=0))
            full = three(hi_ref[...], lo_ref[...], jnp.concatenate(tiles, axis=1))
            full = full.astype(bf16).astype(f32)
            planes_ref[c_hi * 2, 0:ROWS] = full[:, 0:128]
            planes_ref[c_hi * 2 + 1, 0:ROWS] = full[:, 128:256]
        both = transform(0, 32)
        for slot in range(2):
            act_ref[slot, 128:144] = jnp.ones((16, 512), bf16)
            activate(both[slot * 256 : slot * 256 + 256], slot, slot)
        expand(0)

    @pl.when(step < STEPS - 1)
    def _():
        for sub in range(ZB // 2):
            pair = step * (ZB // 2) + sub + 2
            spatial = transform(pair, 16)
            expand(1 - sub % 2)
            finish(sub)
            activate(spatial, pair, sub % 2)

    @pl.when(step == STEPS - 1)
    def _():
        for sub in range(ZB // 2):
            pair = step * (ZB // 2) + sub + 2
            if sub < ZB // 2 - 2:
                spatial = transform(pair, 16)
            if sub < ZB // 2 - 1:
                expand(1 - sub % 2)
            finish(sub)
            if sub < ZB // 2 - 2:
                activate(spatial, pair, sub % 2)


def room(mib):
    return pltpu.CompilerParams(vmem_limit_bytes=mib * 1024 * 1024)


def vmem():
    return pl.BlockSpec(memory_space=pltpu.VMEM)


def rotate(tiles):
    moved = [tiles[0]]
    for k, tile in zip(ORDER[1:], tiles[1:]):
        moved.append(lax.ppermute(tile, "grp", [(i, (i + k) % 4) for i in range(4)]))
    return moved


def far(*values):
    return [pltpu.with_memory_space_constraint(jnp.asarray(v), pltpu.HBM) for v in values]


def shards(
    occupancy,
    embedding,
    spectral_weight,
    point_weight,
    point_bias,
    expand_weight,
    expand_bias,
    reduce_weight,
    reduce_bias,
):
    ytab = y_tables()
    z_hi, z_lo = split(z_tables())
    x_hi, x_lo = split(x_tables())
    shape = jax.ShapeDtypeStruct
    sources = far(
        occupancy.reshape(ROWS, NY),
        ytab,
        z_hi.T.copy(),
        z_lo.T.copy(),
        x_hi.transpose(2, 0, 1).reshape(256, 256),
        x_lo.transpose(2, 0, 1).reshape(256, 256),
        x_hi.transpose(1, 0, 2).reshape(128, 512),
        x_lo.transpose(1, 0, 2).reshape(128, 512),
        z_hi,
        z_lo,
        y_lanes(ytab),
        pen_phases(),
        embedding,
        spectral_weight.reshape(512, 16),
        point_weight,
        point_bias.reshape(1, CH),
        expand_weight,
        expand_bias.reshape(1, HIDDEN),
        reduce_weight.T,
        reduce_bias.reshape(1, CH),
    )
    made = pl.pallas_call(
        forward_kernel,
        out_shape=[shape((128, 128), f32)] * 4
        + [
            shape((2, ROWS + 8, 128), jnp.int32),
            shape((256, 256), bf16),
            shape((256, 256), bf16),
            shape((NCLASS, CH), f32),
            shape((512, 16), f32),
            shape((CH, CH), f32),
            shape((1, CH), f32),
            shape((CH, HIDDEN), bf16),
            shape((1, HIDDEN), f32),
            shape((CH, HIDDEN), bf16),
            shape((1, CH), f32),
            shape((80, 128), f32),
            shape((128, 512), bf16),
            shape((128, 512), bf16),
            shape((512, 256), bf16),
            shape((512, 256), bf16),
            shape((256, 256), bf16),
        ],
        in_specs=[pl.BlockSpec(memory_space=pltpu.HBM)] * 20,
        out_specs=[vmem()] * 21,
        scratch_shapes=[
            pltpu.VMEM((32, 256), bf16),
            pltpu.VMEM((256, 512), bf16),
            pltpu.VMEM((256, 512), bf16),
            pltpu.VMEM((ROWS, NY), bf16),
            pltpu.VMEM((4, 512, 128), f32),
            pltpu.VMEM((4, 128, 128), f32),
            pltpu.SemaphoreType.DMA((21,)),
        ],
        compiler_params=room(16),
        cost_estimate=pl.CostEstimate(flops=400000000, bytes_accessed=3000000, transcendentals=0),
        name="forward",
    )(*sources)
    partial, (labels, xi_hi, xi_lo), small = made[:4], made[4:7], made[7:16]
    xo_hi, xo_lo, z_hi, z_lo, ylane = made[16:]
    wide, weight, phases, table, wide1, wide2, bias2 = pl.pallas_call(
        prepare_kernel,
        out_shape=[
            shape((128, 128), f32),
            shape((512, 128), f32),
            shape((2, 16, 128), f32),
            shape((16, 128), f32),
            shape((512, 256), bf16),
            shape((128, 512), bf16),
            shape((128, 128), f32),
        ],
        in_specs=[vmem()] * 9,
        out_specs=[vmem()] * 7,
        compiler_params=room(8),
        cost_estimate=pl.CostEstimate(flops=200000000, bytes_accessed=1000000, transcendentals=0),
        name="prepare",
    )(*small)
    partial = rotate(partial)
    chunks = pl.pallas_call(
        gather_groups_kernel,
        out_shape=shape((256, 128), f32),
        in_specs=[vmem()] * 7,
        out_specs=vmem(),
        scratch_shapes=[pltpu.VMEM((4, 128, 128), f32)],
        compiler_params=room(8),
        name="gather_groups",
    )(phases, xi_hi, xi_lo, *partial)
    chunks = lax.all_to_all(chunks.reshape(64, 4, 128), "pen", 0, 0, tiled=True)
    mixed = pl.pallas_call(
        mix_kernel,
        out_shape=shape((256, 128), f32),
        in_specs=[vmem()] * 3,
        out_specs=vmem(),
        compiler_params=room(8),
        name="mix",
    )(chunks.reshape(256, 128), weight, wide)
    mixed = lax.all_to_all(mixed.reshape(64, 4, 128), "pen", 0, 0, tiled=True)
    modes = pl.pallas_call(
        scatter_groups_kernel,
        out_shape=[shape((128, 128), f32)] * 4,
        in_specs=[vmem()] * 4,
        out_specs=[vmem()] * 4,
        scratch_shapes=[pltpu.VMEM((4, 128, 128), f32)],
        compiler_params=room(8),
        name="scatter_groups",
    )(phases, xo_hi, xo_lo, mixed.reshape(256, 128))
    modes = rotate(modes)
    return pl.pallas_call(
        point_kernel,
        out_shape=shape((CH, LZ, LX, NY), bf16),
        grid=(STEPS,),
        in_specs=[vmem()] * 12,
        out_specs=pl.BlockSpec((CH, ZB, LX, NY), lambda i: (0, i, 0, 0)),
        scratch_shapes=[
            pltpu.VMEM((4, ROWS + 8, 128), f32),
            pltpu.VMEM((2, 144, 512), bf16),
            pltpu.VMEM((2, 512, 512), f32),
            pltpu.VMEM((4, 128, 128), f32),
        ],
        compiler_params=room(24),
        name="point",
    )(*modes, z_hi, z_lo, ylane, labels, table, wide1, wide2, bias2)


def solution(mesh):
    return jax.shard_map(
        shards,
        mesh=mesh,
        in_specs=(
            P("grp", "pen", None),
            P(),
            P(("grp", "pen"), None, None, None, None),
            P(),
            P(),
            P(),
            P(),
            P(),
            P(),
        ),
        out_specs=P(None, "grp", "pen", None),
        check_vma=False,
    )
```
